32 devices in a mesh: shard: 4 (over z), ctx: 4 (over x, core), tp: 2 (over y).
Axes of the slice: x: 2, y: 2, z: 4, core: 2. Of those that a mesh axis runs over, the one named last changes fastest.
Arguments:
- hidden_in: bfloat16 [8, 2048, 768], P('shard', ('ctx', 'tp')), may hold values from -6 to 6
- doc_lengths: int32 [8, 4], P('shard'), may hold values from 1 to 1024, 2048 in all within a row
- ln1_gain: bfloat16 [2, 768], P(None, 'shard'), may hold values from 0.25 to 1.75
- ln1_bias: bfloat16 [2, 768], P(None, 'shard'), may hold values from -1.1953125 to 1.1953125
- qkv_weight: bfloat16 [2, 768, 2304], P(None, 'shard'), may hold values from -0.21875 to 0.21875
- qv_bias: bfloat16 [2, 1536], P(None, 'shard'), may hold values from -0.29882812 to 0.29882812
- out_weight: bfloat16 [2, 768, 768], P(None, 'shard'), may hold values from -2.5 to 2.5
- out_bias: bfloat16 [2, 768], P(None, 'shard'), may hold values from -1.1953125 to 1.1953125
- ln2_gain: bfloat16 [2, 768], P(None, 'shard'), may hold values from 0.25 to 1.75
- ln2_bias: bfloat16 [2, 768], P(None, 'shard'), may hold values from -1.1953125 to 1.1953125
- up_weight: bfloat16 [2, 768, 3072], P(None, None, ('shard', 'tp')), may hold values from -0.21875 to 0.21875
- up_bias: bfloat16 [2, 3072], P(None, ('shard', 'tp')), may hold values from -3 to 3
- down_weight: bfloat16 [2, 3072, 768], P(None, ('shard', 'tp')), may hold values from -0.109375 to 0.109375
- down_bias: bfloat16 [2, 768], P(None, 'shard'), may hold values from -1.1953125 to 1.1953125
- output_grad: bfloat16 [8, 2048, 768], P('shard', ('ctx', 'tp')), may hold values from -6 to 6
Outputs:
- hidden_out: bfloat16 [8, 2048, 768], P('shard', ('ctx', 'tp'))
- hidden_grad: float32 [8, 2048, 768], P('shard', ('ctx', 'tp'))
- ln1_gain_grad: float32 [2, 768], P(None, 'shard')
- ln1_bias_grad: float32 [2, 768], P(None, 'shard')
- qkv_weight_grad: float32 [2, 768, 2304], P(None, 'shard')
- qv_bias_grad: float32 [2, 1536], P(None, 'shard')
- out_weight_grad: float32 [2, 768, 768], P(None, 'shard')
- out_bias_grad: float32 [2, 768], P(None, 'shard')
- ln2_gain_grad: float32 [2, 768], P(None, 'shard')
- ln2_bias_grad: float32 [2, 768], P(None, 'shard')
- up_weight_grad: float32 [2, 768, 3072], P(None, None, ('shard', 'tp'))
- up_bias_grad: float32 [2, 3072], P(None, ('shard', 'tp'))
- down_weight_grad: float32 [2, 3072, 768], P(None, ('shard', 'tp'))
- down_bias_grad: float32 [2, 768], P(None, 'shard')
The draws below stay inside these ranges and needn't reach their ends.
Inputs may be any that keep to these rules, and one draw needn't show every extreme that they name: `doc_lengths`: row s holds the lengths of sequence s's 3 documents in order, then the number of padding tokens at its end; each row sums to 2048.
All inputs are finite; a program needn't handle non-finite values.
Results may differ from the reference program's by a relative error of at most 0.017.
Values may be sent and summed in bfloat16 or wider, within the bound.
No kernel may reach another device: no remote copies, remote signals or barrier semaphores. Data moves between devices by JAX's collectives and lax.ppermute only.
A program may use at most 192 MiB of HBM per device.

```python
import math
import jax
import jax.numpy as jnp
import numpy as np
from jax import lax

D = 768
HEADS = 12
HEAD = 64
FF = 3072
LAYERS = 2
LENGTH = 2048
DOCS = 3
MOST_DOC = 1024
SEQS = 8


def raised(array, rng, source, target, shards_of, factor):
    def block_of(position):
        return (jnp.arange(array.shape[position]) // (array.shape[position] // shards_of)).reshape((-1,) + (1,) * (array.ndim - 1 - position))

    first = jax.random.permutation(rng, shards_of)[block_of(target)]
    far = (block_of(target) + shards_of // 2) % shards_of
    return jnp.where((block_of(source) == first) | (block_of(source) == far), factor * array, array)


def block_levels(key, extent, split, least, largest):
    def one(position, shards_of):
        draws = jax.random.uniform(jax.random.fold_in(jax.random.fold_in(key, 6), position), (shards_of,), jnp.float32, least / len(split), largest / len(split))
        return jnp.repeat(jnp.exp(draws), extent[position] // shards_of).reshape((-1,) + (1,) * (len(extent) - position - 1))

    level = one(*split[0])
    for cut in split[1:]:
        level = level * one(*cut)
    return level


def split_up(count, total, most, lean):
    weights = [(1 << 20) // math.isqrt(rank ** lean) + 1 for rank in range(2, count + 1)]
    spare, given = total - most - (count - 1), [1] * (count - 1)
    while spare > 0:
        candidates = [i for i in range(count - 1) if given[i] < most]
        mass, budget = sum([weights[i] for i in candidates]), spare
        for i in candidates:
            more = min(most - given[i], max(1, budget * weights[i] // mass), spare)
            given[i] = given[i] + more
            spare = spare - more
    return np.array([most] + given)


def uneven(own_key, amount, total, reach, skew):
    if amount == 2:
        one = jax.random.randint(own_key, (), max(1, total - reach), min(reach, total - 1) + 1)
        return jnp.stack([one, total - one])
    sizes = jnp.asarray(split_up(amount, total, reach, skew), jnp.int32)
    twos = (amount - 1) // 2
    giver, taker = sizes[1:1 + 2 * twos:2], sizes[2:2 + 2 * twos:2]
    room = jnp.minimum(giver - 1, reach - taker)
    passed = jax.random.randint(jax.random.fold_in(own_key, 1), (twos,), 0, 1 << 20) % (room + 1)
    sizes = sizes.at[1:1 + 2 * twos:2].set(giver - passed).at[2:2 + 2 * twos:2].set(taker + passed)
    return sizes[jax.random.permutation(jax.random.fold_in(own_key, 2), amount)]


def bell_draw(stream_key, shape, deviation, limit, cuts=(), held_as=jnp.bfloat16):
    values = jax.random.normal(stream_key, shape, jnp.float32) * deviation
    if len(cuts) > 0:
        values = block_levels(stream_key, shape, cuts, -0.22, 0.18) * values
    return jnp.clip(values, min=-limit, max=limit).astype(held_as)


def noise_with(own_key, extent, width, reach, split, heavy, kind=jnp.bfloat16):
    drawn = width * jax.random.normal(own_key, extent, jnp.float32)
    if split:
        drawn = drawn * block_levels(own_key, extent, split, -0.22, 0.18)
    return jnp.clip(raised(drawn, jax.random.fold_in(own_key, 3), *heavy), -reach, reach).astype(kind)


def setup_inputs(seed: int = 0) -> dict:
    splits = jax.random.split(jax.random.key(seed), 16)
    hidden_in = bell_draw(splits[0], (SEQS, LENGTH, D), 1.0, 6.0, ((0, 4), (1, 8)))
    doc_lengths = jax.vmap(lambda own: uneven(own, DOCS + 1, LENGTH, MOST_DOC, 2))(jax.random.split(splits[1], SEQS)).reshape((SEQS, DOCS + 1)).astype(jnp.int32)
    ln1_gain = jnp.clip(1.0 + 0.15 * jax.random.normal(splits[2], (LAYERS, D), jnp.float32), 0.25, 1.75).astype(jnp.bfloat16)
    ln1_bias = bell_draw(splits[3], (LAYERS, D), 0.2, 1.1953125, ((1, 4),))
    qkv_weight = bell_draw(splits[4], (LAYERS, D, 3 * D), D ** -0.5, 0.21875, ((1, 4),))
    qv_bias = bell_draw(splits[5], (LAYERS, 2 * D), 0.05, 0.29882812, ((1, 4),))
    out_weight = bell_draw(splits[6], (LAYERS, D, D), (max(1, D // 128)) ** -0.5, 2.5, ((1, 4),))
    out_bias = bell_draw(splits[7], (LAYERS, D), 0.2, 1.1953125, ((1, 4),))
    ln2_gain = jnp.clip(1.0 + 0.15 * jax.random.normal(splits[8], (LAYERS, D), jnp.float32), 0.25, 1.75).astype(jnp.bfloat16)
    ln2_bias = bell_draw(splits[9], (LAYERS, D), 0.2, 1.1953125, ((1, 4),))
    up_weight = bell_draw(splits[10], (LAYERS, D, FF), D ** -0.5, 0.21875, ((2, 8),))
    up_bias = bell_draw(splits[11], (LAYERS, FF), 0.5, 3.0, ((1, 8),))
    down_weight = bell_draw(splits[12], (LAYERS, FF, D), FF ** -0.5, 0.109375, ((1, 8),))
    down_bias = bell_draw(splits[13], (LAYERS, D), 0.2, 1.1953125, ((1, 4),))
    output_grad = noise_with(splits[14], (SEQS, LENGTH, D), 1.0, 6.0, ((0, 4), (1, 8)), (0, 2, 4, 2.0))
    return dict(hidden_in=hidden_in, doc_lengths=doc_lengths, ln1_gain=ln1_gain, ln1_bias=ln1_bias, qkv_weight=qkv_weight, qv_bias=qv_bias, out_weight=out_weight, out_bias=out_bias, ln2_gain=ln2_gain, ln2_bias=ln2_bias, up_weight=up_weight, up_bias=up_bias, down_weight=down_weight, down_bias=down_bias, output_grad=output_grad)


@jax.custom_vjp
def low(v):
    return lax.optimization_barrier(v.astype(jnp.bfloat16)).astype(jnp.float32)

@jax.custom_vjp
def low_back(v):
    return v

def low_keep(v):
    return (low(v), None)

def low_pass(kept, grad):
    return (grad,)

def back_keep(v):
    return (v, None)

def back_low(kept, grad):
    return (low(grad),)
low.defvjp(low_keep, low_pass)
low_back.defvjp(back_keep, back_low)
ln_epsilon = 1e-06
masked_score = -1e+30

def layer_norm(values_in, gain, bias):
    row_mean = lax.optimization_barrier(jnp.mean(values_in, axis=-1, keepdims=True))
    centred = values_in - row_mean
    variance = lax.optimization_barrier(jnp.mean(centred * centred, axis=-1, keepdims=True))
    return centred * lax.rsqrt(variance + ln_epsilon) * gain + bias

def matmul(left, right):
    return jnp.dot(left, right, precision=lax.Precision.HIGHEST)

def segment_ids(doc_lengths):
    doc_ends = jnp.cumsum(doc_lengths[:, :DOCS], axis=1).astype(jnp.int32)
    places = jnp.arange(LENGTH, dtype=jnp.int32)
    return lax.optimization_barrier(jnp.sum((places[None, :, None] >= doc_ends[:, None, :]).astype(jnp.int32), axis=2))

def head_attention(queries, key_rows, values, segments):
    scores = jnp.einsum('gqd,gkd->gqk', queries, key_rows, precision=lax.Precision.HIGHEST) * HEAD ** (-0.5)
    scores = low_back(scores)
    allowed = segments[:, :, None] == segments[:, None, :]
    attn_probs = jax.nn.softmax(jnp.where(allowed, scores, masked_score), axis=-1)
    return jnp.einsum('gqk,gkd->gqd', low(attn_probs), values, precision=lax.Precision.HIGHEST)

def attention(queries, key_rows, values, segments):
    groups = queries.shape[0]

    def to_heads(tensor):
        return jnp.transpose(tensor.reshape(groups, LENGTH, HEADS, HEAD), (2, 0, 1, 3))

    def one_head(inputs):
        return head_attention(inputs[0], inputs[1], inputs[2], segments)
    per_head = lax.map(jax.checkpoint(one_head), (to_heads(queries), to_heads(key_rows), to_heads(values)))
    return jnp.transpose(per_head, (1, 2, 0, 3)).reshape(groups, LENGTH, D)

def encoder_layer(hidden, weights, segments):
    gain_one, bias_one, w_qkv, b_qv, w_out, b_out, gain_two, bias_two, w_up, b_up, w_down, b_down = weights
    normed = low(layer_norm(hidden, gain_one, bias_one))
    projected = matmul(normed, w_qkv)
    queries = low_back(low(projected[..., :D] + b_qv[:D]))
    key_rows = low_back(low(projected[..., D:2 * D]))
    values = low_back(low(projected[..., 2 * D:] + b_qv[D:]))
    context = low_back(low(attention(queries, key_rows, values, segments)))
    branch = low_back(matmul(context, w_out) + b_out)
    middle = hidden + branch
    inner_input = low(layer_norm(middle, gain_two, bias_two))
    pre_act = low_back(matmul(inner_input, w_up) + b_up)
    activated = low(jax.nn.gelu(pre_act, approximate=True))
    return middle + low_back(matmul(activated, w_down) + b_down)

def forward(hidden, params, segments, keep_mask):
    for layer_index in range(LAYERS):
        weights = tuple((stacked[layer_index] for stacked in params))
        hidden = encoder_layer(hidden, weights, segments)
    return hidden * keep_mask[..., None]

def reference(hidden_in, doc_lengths, ln1_gain, ln1_bias, qkv_weight, qv_bias, out_weight, out_bias, ln2_gain, ln2_bias, up_weight, up_bias, down_weight, down_bias, output_grad):
    params = tuple((stacked.astype(jnp.float32) for stacked in (ln1_gain, ln1_bias, qkv_weight, qv_bias, out_weight, out_bias, ln2_gain, ln2_bias, up_weight, up_bias, down_weight, down_bias)))
    segments = segment_ids(doc_lengths)
    keep_mask = (segments < DOCS).astype(jnp.float32)
    group_size = math.gcd(SEQS, max(1, 4096 // LENGTH))
    group_count = SEQS // group_size

    def regroup(tensor):
        return tensor.reshape((group_count, group_size) + tensor.shape[1:])

    def advance(totals, inputs):
        hidden, cotangent, group_segs, group_keep = inputs

        def forward_run(hidden_value, param_values):
            return forward(hidden_value, param_values, group_segs, group_keep)
        result, pullback = jax.vjp(forward_run, hidden.astype(jnp.float32), params)
        input_grad, param_grads = pullback(cotangent.astype(jnp.float32))
        totals = tuple((left + right for left, right in zip(totals, param_grads)))
        return (totals, (result.astype(jnp.bfloat16), input_grad))
    empty_grads = tuple((jnp.zeros(stacked.shape, jnp.float32) for stacked in params))
    totals, (outputs, input_grads) = lax.scan(advance, empty_grads, (regroup(hidden_in), regroup(output_grad), regroup(segments), regroup(keep_mask)))
    hidden_out = outputs.reshape(SEQS, LENGTH, D)
    hidden_grad = input_grads.reshape(SEQS, LENGTH, D)
    return (hidden_out, hidden_grad, totals[0], totals[1], totals[2], totals[3], totals[4], totals[5], totals[6], totals[7], totals[8], totals[9], totals[10], totals[11])
```

```python
import jax
import jax.numpy as jnp
from jax import lax
from jax.experimental import pallas as pl
from jax.experimental.pallas import tpu as pltpu
from jax.sharding import Mesh
from jax.sharding import PartitionSpec as P

HEADS = 12
HEAD = 64
LAYERS = 2
BLK = 256
NEG = -1e30
EPS = 1e-06
F32 = jnp.float32
BF16 = jnp.bfloat16


def dot(left, right, dims=((1,), (0,))):
    return lax.dot_general(left, right, (dims, ((), ())), preferred_element_type=F32)


def swap(value, axis):
    return lax.ppermute(value, axis, ((0, 1), (1, 0)))


def block_place(block, dev, half):
    return (((block // 2) ^ dev) * 2) + ((block % 2) ^ half)


def doc_range(first, ends, length):
    last = first + BLK - 1
    start, stop = jnp.int32(0), jnp.int32(length)
    for end in ends:
        start = jnp.maximum(start, jnp.where(first >= end, end, 0))
        stop = jnp.minimum(stop, jnp.where(last < end, end, length))
    return start // BLK, (stop + BLK - 1) // BLK


def seg_of(places, ends):
    seg = (places >= ends[0]).astype(jnp.int32)
    for end in ends[1:]:
        seg = seg + (places >= end).astype(jnp.int32)
    return seg


def three_heads(pair, single):
    blank = jnp.zeros_like(single)
    return (
        jnp.concatenate((pair[:HEAD], blank), axis=0),
        jnp.concatenate((blank, pair[HEAD:]), axis=0),
        jnp.concatenate((single, blank), axis=0),
    )


def attention_forward_kernel(info, qkv_ref, out_ref, lse_ref, v01_t, v2_t):
    step = pl.program_id(0)
    length = qkv_ref.shape[0]
    ends = (info[0], info[1], info[2])
    dev, half = info[3], info[4]

    @pl.when(step == 0)
    def _():
        v01_t[...] = qkv_ref[:, 256:384].T
        v2_t[...] = qkv_ref[:, 128:256].T

    mine = pl.ds(pl.multiple_of(step * BLK, BLK), BLK)
    first = block_place(step, dev, half) * BLK
    seg_q = seg_of(first + lax.broadcasted_iota(jnp.int32, (1, BLK), 1), ends)
    queries = three_heads(qkv_ref[mine, 384:512].T, qkv_ref[mine, 512:576].T)
    low, high = doc_range(first, ends, length)

    def body(block, carry):
        rows = pl.ds(pl.multiple_of(block_place(block, dev, half) * BLK, BLK), BLK)
        places = block * BLK + lax.broadcasted_iota(jnp.int32, (BLK, 1), 0)
        allowed = seg_of(places, ends) == seg_q
        k01 = qkv_ref[rows, 0:128]
        k2 = qkv_ref[rows, 128:256]
        values = (v01_t[0:HEAD, rows], v01_t[HEAD:128, rows], v2_t[HEAD:128, rows])
        result = []
        for head in range(3):
            top, total, acc = carry[head]
            scores = dot(k2 if head == 2 else k01, queries[head])
            scores = jnp.where(allowed, scores, NEG)
            new_top = jnp.maximum(top, jnp.max(scores, axis=0, keepdims=True))
            exps = jnp.exp(scores - new_top)
            shrink = jnp.exp(top - new_top)
            total = total * shrink + jnp.sum(exps, axis=0, keepdims=True)
            acc = acc * shrink + dot(values[head], exps.astype(BF16))
            result.append((new_top, total, acc))
        return tuple(result)

    start = tuple(
        (
            jnp.full((1, BLK), NEG, F32),
            jnp.zeros((1, BLK), F32),
            jnp.zeros((HEAD, BLK), F32),
        )
        for _ in range(3)
    )
    final = lax.fori_loop(low, high, body, start)
    for head in range(3):
        top, total, acc = final[head]
        out_ref[0, head * HEAD : (head + 1) * HEAD, :] = (acc / total).astype(BF16)
        lse_ref[head : head + 1, :] = top + jnp.log(total)
    lse_ref[3:8, :] = jnp.zeros((5, BLK), F32)


def attention_forward(info, qkv):
    length = qkv.shape[0]
    return pl.pallas_call(
        attention_forward_kernel,
        name="attention_forward",
        grid_spec=pltpu.PrefetchScalarGridSpec(
            num_scalar_prefetch=1,
            grid=(length // BLK,),
            in_specs=[pl.BlockSpec(qkv.shape, lambda i, info: (0, 0))],
            out_specs=[
                pl.BlockSpec((1, 192, BLK), lambda i, info: (i // 2, 0, i % 2)),
                pl.BlockSpec((8, BLK), lambda i, info: (0, i)),
            ],
            scratch_shapes=[
                pltpu.VMEM((128, length), BF16),
                pltpu.VMEM((128, length), BF16),
            ],
        ),
        out_shape=(
            jax.ShapeDtypeStruct((length // 512, 192, 512), BF16),
            jax.ShapeDtypeStruct((8, length), F32),
        ),
        compiler_params=pltpu.CompilerParams(vmem_limit_bytes=48 << 20),
        cost_estimate=pl.CostEstimate(
            flops=4 * 3 * HEAD * length * 1024, transcendentals=3 * length * 1024, bytes_accessed=6 << 20
        ),
    )(info, qkv)


def attention_backward_kernel(info, qkv_ref, out_ref, grad_ref, lse_ref, du_ref, q01_t, q2_t, delta, dq_t):
    step = pl.program_id(0)
    length = qkv_ref.shape[0]
    ends = (info[0], info[1], info[2])
    dev, half = info[3], info[4]

    @pl.when(step == 0)
    def _():
        q01_t[...] = qkv_ref[:, 384:512].T
        q2_t[...] = qkv_ref[:, 512:576].T
        dq_t[...] = jnp.zeros_like(dq_t)
        for part in range(length // 512):
            both = out_ref[part].astype(F32) * grad_ref[part].astype(F32)
            for head in range(3):
                delta[head : head + 1, part * 512 : (part + 1) * 512] = jnp.sum(
                    both[head * HEAD : (head + 1) * HEAD], axis=0, keepdims=True
                )

    mine = pl.ds(pl.multiple_of(step * BLK, BLK), BLK)
    first = block_place(step, dev, half) * BLK
    seg_k = seg_of(first + lax.broadcasted_iota(jnp.int32, (BLK, 1), 0), ends)
    k01 = qkv_ref[mine, 0:128]
    k2v2 = qkv_ref[mine, 128:256]
    v01 = qkv_ref[mine, 256:384]
    k01_t = k01.T
    k2_t = k2v2.T[:HEAD]
    keys_t = (k01_t[:HEAD], k01_t[HEAD:], k2_t)
    low, high = doc_range(first, ends, length)

    def body(block, carry):
        dk01, dk2v2, dv01 = carry
        place = block_place(block, dev, half)
        cols = pl.ds(pl.multiple_of(place * BLK, BLK), BLK)
        part_cols = pl.ds(pl.multiple_of((place % 2) * BLK, BLK), BLK)
        places = block * BLK + lax.broadcasted_iota(jnp.int32, (1, BLK), 1)
        allowed = seg_k == seg_of(places, ends)
        queries = three_heads(q01_t[:, cols], q2_t[:, cols])
        grads = grad_ref[place // 2, :, part_cols]
        blank = jnp.zeros((HEAD, BLK), BF16)
        dos = (
            jnp.concatenate((grads[:HEAD], blank), axis=0),
            jnp.concatenate((blank, grads[HEAD:128]), axis=0),
            jnp.concatenate((blank, grads[128:192]), axis=0),
        )
        for head in range(3):
            scores = dot(k2v2 if head == 2 else k01, queries[head])
            probs = jnp.where(allowed, jnp.exp(scores - lse_ref[head : head + 1, cols]), 0.0)
            grad_probs = dot(k2v2 if head == 2 else v01, dos[head])
            grad_scores = (probs * (grad_probs - delta[head : head + 1, cols])).astype(BF16)
            probs = probs.astype(BF16)
            more_k = dot(grad_scores, queries[head], ((1,), (1,)))
            more_v = dot(probs, dos[head], ((1,), (1,)))
            if head == 2:
                dk2v2 = dk2v2 + more_k + more_v
            else:
                dk01 = dk01 + more_k
                dv01 = dv01 + more_v
            rows = slice(head * HEAD, (head + 1) * HEAD)
            dq_t[rows, cols] = dq_t[rows, cols] + dot(keys_t[head], grad_scores)
        return dk01, dk2v2, dv01

    zero = jnp.zeros((BLK, 128), F32)
    dk01, dk2v2, dv01 = lax.fori_loop(low, high, body, (zero, zero, zero))
    du_ref[mine, 0:128] = dk01.astype(BF16)
    du_ref[mine, 128:256] = dk2v2.astype(BF16)
    du_ref[mine, 256:384] = dv01.astype(BF16)

    @pl.when(step == pl.num_programs(0) - 1)
    def _():
        scale = HEAD**-0.5
        du_ref[:, 384:512] = (dq_t[0:128, :] * scale).T.astype(BF16)
        du_ref[:, 512:576] = (dq_t[128:192, :] * scale).T.astype(BF16)


def attention_backward(info, qkv, out, grad, lse):
    length = qkv.shape[0]

    def whole(shape):
        return pl.BlockSpec(shape, lambda i, info: (0,) * len(shape))

    return pl.pallas_call(
        attention_backward_kernel,
        name="attention_backward",
        grid_spec=pltpu.PrefetchScalarGridSpec(
            num_scalar_prefetch=1,
            grid=(length // BLK,),
            in_specs=[whole(qkv.shape), whole(out.shape), whole(grad.shape), whole(lse.shape)],
            out_specs=whole(qkv.shape),
            scratch_shapes=[
                pltpu.VMEM((128, length), BF16),
                pltpu.VMEM((64, length), BF16),
                pltpu.VMEM((8, length), F32),
                pltpu.VMEM((192, length), F32),
            ],
        ),
        out_shape=jax.ShapeDtypeStruct(qkv.shape, BF16),
        compiler_params=pltpu.CompilerParams(vmem_limit_bytes=48 << 20),
        cost_estimate=pl.CostEstimate(
            flops=10 * 3 * HEAD * length * 1024, transcendentals=3 * length * 1024, bytes_accessed=10 << 20
        ),
    )(info, qkv, out, grad, lse)


def norm_forward(values, gain, bias):
    centred = values - jnp.mean(values, axis=-1, keepdims=True)
    inv_std = lax.rsqrt(jnp.mean(centred * centred, axis=-1, keepdims=True) + EPS)
    normed = centred * inv_std
    return normed * gain + bias, normed, inv_std


def norm_backward(grad_out, normed, inv_std, gain):
    grad_normed = grad_out * gain
    grad_in = inv_std * (
        grad_normed
        - jnp.mean(grad_normed, axis=-1, keepdims=True)
        - normed * jnp.mean(grad_normed * normed, axis=-1, keepdims=True)
    )
    return grad_in, jnp.sum(grad_out * normed, axis=0), jnp.sum(grad_out, axis=0)


GELU_A = (2.0 / 3.141592653589793) ** 0.5
GELU_B = 0.044715


def gelu(t):
    return 0.5 * t * (1.0 + jnp.tanh(GELU_A * (t + GELU_B * t * t * t)))


def gelu_slope(t):
    tanh = jnp.tanh(GELU_A * (t + GELU_B * t * t * t))
    return 0.5 * (1.0 + tanh) + 0.5 * t * (1.0 - tanh * tanh) * GELU_A * (1.0 + 3.0 * GELU_B * t * t)


def local(
    hidden_in,
    doc_lengths,
    ln1_gain,
    ln1_bias,
    qkv_weight,
    qv_bias,
    out_weight,
    out_bias,
    ln2_gain,
    ln2_bias,
    up_weight,
    up_bias,
    down_weight,
    down_bias,
    output_grad,
):
    shards = lax.axis_size("shard")
    ix, ic, iy = lax.axis_index("cx"), lax.axis_index("core"), lax.axis_index("tp")
    dev = ix * 2 + ic
    seqs, toks, width = hidden_in.shape
    rows = ln1_gain.shape[1]
    hid = up_bias.shape[1] // 2
    loc = width // 4
    hidden_all = up_bias.shape[1] * shards * 2

    def to_sequence(tokens):
        own = lax.dynamic_index_in_dim(tokens, iy, 0, keepdims=False)
        other = lax.dynamic_index_in_dim(tokens, 1 - iy, 0, keepdims=False)
        return jnp.concatenate((own, swap(other, "tp")), axis=0).astype(F32)

    def from_sequence(tokens):
        own, other = tokens[:toks], swap(tokens[toks:], "tp")
        return jnp.where(iy == 0, jnp.stack((own, other)), jnp.stack((other, own)))

    lengths = lax.dynamic_index_in_dim(doc_lengths, iy, 0, keepdims=False)
    end0 = lengths[0]
    end1 = end0 + lengths[1]
    end2 = end1 + lengths[2]
    info = jnp.stack((end0, end1, end2, dev, iy, dev, dev, dev)).astype(jnp.int32)
    row_ids = jnp.arange(2 * toks, dtype=jnp.int32)
    places = dev * (2 * toks) + ((row_ids // toks) ^ iy) * toks + row_ids % toks
    keep = (places < end2).astype(F32)[:, None]

    small = jnp.concatenate(
        [p.reshape(-1) for p in (ln1_gain, ln1_bias, out_bias, ln2_gain, ln2_bias, down_bias, qv_bias, up_bias)]
    ).reshape(1, -1)
    small_all = lax.all_gather(small, ("shard", "tp"), axis=0, tiled=True).astype(F32)
    small_all = small_all.reshape(shards, 2, -1)
    at = 0
    smalls = []
    for _ in range(6):
        piece = small_all[:, 0, at : at + LAYERS * rows].reshape(shards, LAYERS, rows)
        smalls.append(jnp.transpose(piece, (1, 0, 2)).reshape(LAYERS, width))
        at += LAYERS * rows
    piece = small_all[:, 0, at : at + LAYERS * 2 * rows].reshape(shards, LAYERS, 2 * rows)
    qv_full = jnp.transpose(piece, (1, 0, 2)).reshape(LAYERS, 2 * width)
    at += LAYERS * 2 * rows
    up_bias_all = small_all[:, :, at:].reshape(shards, 2, LAYERS, 2, hid)

    def columns(array, start):
        return lax.dynamic_slice_in_dim(array, start, loc, 1)

    def gather_attention(layer):
        weight = qkv_weight[layer]
        q, k, v = (columns(weight, which * width + loc * dev) for which in range(3))
        out = columns(out_weight[layer], loc * dev)
        piece = jnp.concatenate((k[:, :128], k[:, 128:], v[:, 128:], v[:, :128], q, out), axis=1)
        gathered = lax.all_gather(piece, "shard", axis=0, tiled=True)
        qkv_w = gathered[:, : 3 * loc]
        own = gathered[:, 3 * loc :]
        core = swap(own, "core")
        far = swap(own, "cx")
        diag = swap(far, "core")
        full = jnp.zeros((width, width), BF16)
        for rel, part in enumerate((own, core, far, diag)):
            full = lax.dynamic_update_slice_in_dim(full, part, loc * (dev ^ rel), 1)
        return qkv_w, full

    def gather_hidden(piece):
        own = lax.all_gather(piece, "shard", axis=0, tiled=True)
        other = swap(own, "tp")
        return (own, other, swap(own, "core"), swap(other, "core"))

    def bias_parts(layer):
        parts = []
        for rc in range(2):
            for ry in range(2):
                part = lax.dynamic_index_in_dim(up_bias_all[:, :, layer], iy ^ ry, 1, keepdims=False)
                part = lax.dynamic_index_in_dim(part, ic ^ rc, 1, keepdims=False)
                parts.append(part.reshape(-1))
        return parts

    weights = []
    for layer in range(LAYERS):
        w_qkv, w_out = gather_attention(layer)
        up_piece = lax.dynamic_slice_in_dim(up_weight[layer], ic * hid, hid, 1).T
        down_piece = lax.dynamic_slice_in_dim(down_weight[layer], ic * hid, hid, 0)
        weights.append((w_qkv, w_out, gather_hidden(up_piece), gather_hidden(down_piece)))

    qkv_scale = jnp.concatenate((jnp.ones((2 * loc,), F32), jnp.full((loc,), HEAD**-0.5, F32)))

    current = to_sequence(hidden_in)
    grad = to_sequence(output_grad) * keep
    saved = []
    for layer in range(LAYERS):
        gain_one, bias_one, bias_out, gain_two, bias_two, bias_down = (s[layer] for s in smalls)
        w_qkv, w_out, w_up, w_down = weights[layer]
        normed, normed_one, inv_one = norm_forward(current, gain_one, bias_one)
        own = normed.astype(BF16)
        far = swap(own, "cx")
        attn_in = jnp.concatenate((own, swap(own, "core"), far, swap(far, "core")), axis=0)
        q_bias = lax.dynamic_slice_in_dim(qv_full[layer], loc * dev, loc, 0)
        v_bias = lax.dynamic_slice_in_dim(qv_full[layer], width + loc * dev, loc, 0)
        zeros = jnp.zeros((128,), F32)
        bias = jnp.concatenate((zeros, zeros[:64], v_bias[128:], v_bias[:128], q_bias))
        qkv = ((dot(attn_in, w_qkv) + bias) * qkv_scale).astype(BF16)
        attended, lse = attention_forward(info, qkv)
        from_core = swap(attended[1], "core")
        from_far = lax.ppermute(attended[2], "cx", ((0, 1), (1, 0)))
        from_diag = lax.ppermute(attended[3], ("cx", "core"), ((0, 3), (1, 2), (2, 1), (3, 0)))
        context = jnp.zeros((width, 2 * toks), BF16)
        for rel, part in enumerate((attended[0], from_core, from_far, from_diag)):
            context = lax.dynamic_update_slice_in_dim(context, part, loc * (dev ^ rel), 0)
        middle = current + dot(context, w_out, ((0,), (0,))) + bias_out
        mlp_in, normed_two, inv_two = norm_forward(middle, gain_two, bias_two)
        mlp_in = mlp_in.astype(BF16)
        pre, act = [], []
        result = middle + bias_down
        for part, part_bias in enumerate(bias_parts(layer)):
            pre_act = dot(mlp_in, w_up[part], ((1,), (1,))) + part_bias
            pre.append(pre_act.astype(BF16))
            act.append(gelu(pre_act).astype(BF16))
        for part in range(4):
            result = result + dot(act[part], w_down[part])
        saved.append((normed_one, inv_one, attn_in, qkv, attended, lse, context, normed_two, inv_two, mlp_in, pre, act))
        current = result
    hidden_out = from_sequence((current * keep).astype(BF16))

    def reduce_hidden(parts):
        send = swap(jnp.concatenate((parts[2], parts[3]), axis=0).astype(BF16), "core").astype(F32)
        own = parts[0] + send[: parts[0].shape[0]]
        other = parts[1] + send[parts[0].shape[0] :]
        own = own + swap(other.astype(BF16), "tp").astype(F32)
        return lax.psum_scatter(own.astype(BF16), "shard", scatter_dimension=0, tiled=True)

    small_grads = [None] * LAYERS
    qkv_grads = [None] * LAYERS
    out_grads = [None] * LAYERS
    up_grads = [None] * LAYERS
    down_grads = [None] * LAYERS
    quarter = rows // 4
    for layer in reversed(range(LAYERS)):
        normed_one, inv_one, attn_in, qkv, attended, lse, context, normed_two, inv_two, mlp_in, pre, act = saved[layer]
        gain_one, _, _, gain_two, _, _ = (s[layer] for s in smalls)
        w_qkv, w_out, w_up, w_down = weights[layer]
        mlp_grad = grad.astype(BF16)
        b_down_grad = jnp.sum(mlp_grad.astype(F32), axis=0)
        pre_grads = []
        mlp_in_grad = None
        for part in range(4):
            act_grad = dot(mlp_grad, w_down[part], ((1,), (1,)))
            pre_grad = (act_grad * gelu_slope(pre[part].astype(F32))).astype(BF16)
            pre_grads.append(pre_grad)
            term = dot(pre_grad, w_up[part])
            mlp_in_grad = term if mlp_in_grad is None else mlp_in_grad + term
        norm_grad, gain_two_grad, bias_two_grad = norm_backward(mlp_in_grad, normed_two, inv_two, gain_two)
        middle_grad = grad + norm_grad
        branch_grad = middle_grad.astype(BF16)
        b_out_grad = jnp.sum(branch_grad.astype(F32), axis=0)
        context_grad = dot(w_out, branch_grad, ((1,), (1,))).astype(BF16)
        pieces = [lax.dynamic_slice_in_dim(context_grad, loc * (dev ^ rel), loc, 0) for rel in range(4)]
        attn_grad = jnp.stack(
            (
                pieces[0],
                swap(pieces[1], "core"),
                swap(pieces[2], "cx"),
                lax.ppermute(pieces[3], ("cx", "core"), ((0, 3), (1, 2), (2, 1), (3, 0))),
            )
        )
        down_parts = [dot(act[part], mlp_grad, ((0,), (0,))) for part in range(4)]
        up_parts = [dot(pre_grads[part], mlp_in, ((0,), (0,))) for part in range(4)]
        b_up_parts = [jnp.sum(pre_grads[part].astype(F32), axis=0).reshape(shards, hid) for part in range(4)]
        w_out_grad = dot(context, branch_grad).reshape(shards, 2, 2, quarter, width)
        bundle = []
        for rc in range(2):
            for ry in range(2):
                piece = lax.dynamic_index_in_dim(w_out_grad, ic ^ rc, 1, keepdims=False)
                piece = lax.dynamic_index_in_dim(piece, iy ^ ry, 1, keepdims=False)
                up_part = up_parts[rc * 2 + ry].reshape(shards, hid, width)
                bundle.append(jnp.concatenate((up_part, piece), axis=1).reshape(-1, width))
        down_grads[layer] = reduce_hidden(down_parts)
        up_grads[layer] = reduce_hidden(bundle)
        du = attention_backward(info, qkv, attended, attn_grad, lse)
        w_qkv_grad = dot(attn_in, du, ((0,), (0,))).astype(BF16)
        qkv_grads[layer] = lax.psum_scatter(w_qkv_grad, "shard", scatter_dimension=0, tiled=True)
        attn_in_grad = dot(du, w_qkv, ((1,), (1,)))
        n = 2 * toks
        send = swap(jnp.concatenate((attn_in_grad[n : 2 * n], attn_in_grad[3 * n :]), axis=0).astype(BF16), "core")
        far = (attn_in_grad[2 * n : 3 * n] + send[n:].astype(F32)).astype(BF16)
        normed_grad = attn_in_grad[:n] + send[:n].astype(F32) + swap(far, "cx").astype(F32)
        du_sum = jnp.sum(du.astype(F32), axis=0)
        norm_grad, gain_one_grad, bias_one_grad = norm_backward(normed_grad, normed_one, inv_one, gain_one)
        grad = middle_grad + norm_grad
        v_sum = jnp.concatenate((du_sum[256:384], du_sum[192:256]))
        qv_grad = jnp.zeros((2 * width,), F32)
        qv_grad = lax.dynamic_update_slice_in_dim(qv_grad, du_sum[384:], loc * dev, 0)
        qv_grad = lax.dynamic_update_slice_in_dim(qv_grad, v_sum, width + loc * dev, 0)
        b_up_grad = jnp.zeros((shards, 2, 2, hid), F32)
        for rc in range(2):
            for ry in range(2):
                piece = b_up_parts[rc * 2 + ry][:, None, None]
                b_up_grad = lax.dynamic_update_slice(b_up_grad, piece, (0, iy ^ ry, ic ^ rc, 0))
        small_grads[layer] = jnp.concatenate(
            (
                gain_one_grad,
                bias_one_grad,
                b_out_grad,
                gain_two_grad,
                bias_two_grad,
                b_down_grad,
                qv_grad,
                b_up_grad.reshape(-1),
            )
        )

    hidden_grad = from_sequence(grad.astype(BF16)).astype(F32)

    total = jnp.stack(small_grads).reshape(-1, 128)
    for axis in ("core", "cx", "tp"):
        total = total + swap(total, axis)
    if shards <= 4:
        shifted = [
            lax.ppermute(total, "shard", [(i, (i + by) % shards) for i in range(shards)]) for by in range(1, shards)
        ]
        for term in shifted:
            total = total + term
    else:
        total = lax.psum(total, "shard")
    total = total.reshape(LAYERS, -1)
    shard = lax.axis_index("shard")
    outs_small = [
        lax.dynamic_slice_in_dim(total[:, which * width : (which + 1) * width], shard * rows, rows, 1)
        for which in range(6)
    ]
    qv_out = lax.dynamic_slice_in_dim(total[:, 6 * width : 8 * width], shard * 2 * rows, 2 * rows, 1)
    up_bias_out = lax.dynamic_slice_in_dim(
        total[:, 8 * width : 8 * width + hidden_all], (shard * 2 + iy) * 2 * hid, 2 * hid, 1
    )

    def both_cores(value):
        other = swap(value, "core")
        return jnp.where(ic == 0, jnp.stack((value, other)), jnp.stack((other, value)))

    w_qkv_out, w_out_out, w_up_out, w_down_out = [], [], [], []
    for layer in range(LAYERS):
        own = qkv_grads[layer]
        own = (own.astype(F32) + swap(own, "tp").astype(F32)).astype(BF16)
        core = swap(own, "core")
        far = swap(own, "cx")
        diag = swap(far, "core")
        full = jnp.zeros((rows, 3, 4, loc), F32)
        for rel, part in enumerate((own, core, far, diag)):
            part = part.astype(F32)
            k = part[:, :192]
            v = jnp.concatenate((part[:, 256:384], part[:, 192:256]), axis=1)
            q = part[:, 384:]
            full = lax.dynamic_update_slice(full, jnp.stack((q, k, v), axis=1)[:, :, None], (0, 0, dev ^ rel, 0))
        w_qkv_out.append(full.reshape(rows, 3 * width))
        own = down_grads[layer]
        own = (own.astype(F32) + swap(own, "cx").astype(F32)).astype(BF16)
        w_down_out.append(both_cores(own).reshape(2 * hid, width).astype(F32))
        own = up_grads[layer]
        own = (own.astype(F32) + swap(own, "cx").astype(F32)).astype(BF16)
        both = both_cores(own)
        w_up_out.append(both[:, :hid].reshape(2 * hid, width).astype(F32).T)
        mine = both[:, hid:]
        other = swap(mine, "tp")
        out_rows = jnp.where(iy == 0, jnp.stack((mine, other), axis=1), jnp.stack((other, mine), axis=1))
        w_out_out.append(out_rows.reshape(rows, width).astype(F32))

    return (
        hidden_out,
        hidden_grad,
        outs_small[0],
        outs_small[1],
        jnp.stack(w_qkv_out),
        qv_out,
        jnp.stack(w_out_out),
        outs_small[2],
        outs_small[3],
        outs_small[4],
        jnp.stack(w_up_out),
        up_bias_out,
        jnp.stack(w_down_out),
        outs_small[5],
    )


def solution(mesh):
    names = tuple(mesh.axis_names)
    shape = dict(mesh.shape)
    split = Mesh(
        mesh.devices.reshape(shape[names[0]], 2, shape[names[1]] // 2, shape[names[2]]),
        ("shard", "cx", "core", "tp"),
    )
    tokens = P("shard", ("cx", "core", "tp"), None)
    vector = P(None, "shard")
    attn = P(None, "shard", None)
    placed = (
        tokens,
        P("shard", None),
        vector,
        vector,
        attn,
        vector,
        attn,
        vector,
        vector,
        vector,
        P(None, None, ("shard", "tp")),
        P(None, ("shard", "tp")),
        P(None, ("shard", "tp"), None),
        vector,
        tokens,
    )
    return jax.shard_map(
        local,
        mesh=split,
        in_specs=placed,
        out_specs=(
            tokens,
            tokens,
            vector,
            vector,
            attn,
            vector,
            attn,
            vector,
            vector,
            vector,
            P(None, None, ("shard", "tp")),
            P(None, ("shard", "tp")),
            P(None, ("shard", "tp"), None),
            vector,
        ),
        check_vma=False,
    )
```

```python
from functools import partial, reduce

import jax
import jax.numpy as jnp
from jax import lax
from jax.experimental import pallas as pl
from jax.experimental.pallas import tpu as pltpu
from jax.sharding import Mesh
from jax.sharding import PartitionSpec as P

HEADS = 12
HEAD = 64
LAYERS = 2
BLK = 256
NEG = -1e30
TILES = 2
EPS = 1e-06
F32 = jnp.float32
BF16 = jnp.bfloat16


def dot(left, right, dims=((1,), (0,))):
    return lax.dot_general(left, right, (dims, ((), ())), preferred_element_type=F32)


def swap(value, axis):
    return lax.ppermute(value, axis, ((0, 1), (1, 0)))


def block_place(block, dev, half):
    return (((block // 2) ^ dev) * 2) + ((block % 2) ^ half)


def doc_range(first, ends, length):
    last = first + BLK - 1
    start, stop = jnp.int32(0), jnp.int32(length)
    for end in ends:
        start = jnp.maximum(start, jnp.where(first >= end, end, 0))
        stop = jnp.minimum(stop, jnp.where(last < end, end, length))
    return start // BLK, (stop + BLK - 1) // BLK


def seg_of(places, ends):
    seg = (places >= ends[0]).astype(jnp.int32)
    for end in ends[1:]:
        seg = seg + (places >= end).astype(jnp.int32)
    return seg


def three_heads(pair, single):
    blank = jnp.zeros_like(single)
    return (
        jnp.concatenate((pair[:HEAD], blank), axis=0),
        jnp.concatenate((blank, pair[HEAD:]), axis=0),
        jnp.concatenate((single, blank), axis=0),
    )


def norm_rows(rows, gain, bias):
    centred = rows - jnp.mean(rows, axis=-1, keepdims=True)
    inv_std = lax.rsqrt(jnp.mean(centred * centred, axis=-1, keepdims=True) + EPS)
    return centred * inv_std * gain + bias


def whole(shape):
    return pl.BlockSpec(shape, lambda *at: (0,) * len(shape))


HBM = pl.BlockSpec(memory_space=pl.ANY)


def attention_forward_kernel(norm, info, *refs):
    parts, (w_ref, bias_ref, gain_ref, shift_ref) = refs[:4], refs[4:8]
    at_out, qkv_out, out_ref, lse_ref, a_ref, at_ref, qkv_ref, v01_t, v2_t, sems, out_sems = refs[8:]
    length = qkv_ref.shape[0]
    ends = (info[0], info[1], info[2])
    dev, half = info[3], info[4]
    each = parts[0].shape[0]
    copies = [pltpu.make_async_copy(part, a_ref.at[at], sems.at[at]) for at, part in enumerate(parts)]
    for copy in copies:
        copy.start()
    for part in range(4):
        copies[part].wait()

        def project(at, nothing):
            rows = pl.ds(pl.multiple_of(at * BLK, BLK), BLK)
            goal = pl.ds(pl.multiple_of(part * each + at * BLK, BLK), BLK)
            values = a_ref[part, rows, :]
            if norm:
                values = norm_rows(values.astype(F32), gain_ref[...], shift_ref[...]).astype(BF16)
            found = dot(values, w_ref[...]) + bias_ref[...]
            at_ref[:, goal] = values.T
            qkv_ref[goal, 0:384] = found[:, 0:384].astype(BF16)
            qkv_ref[goal, 384:576] = (found[:, 384:576] * HEAD**-0.5).astype(BF16)
            v01_t[:, goal] = qkv_ref[goal, 256:384].T
            v2_t[:, goal] = qkv_ref[goal, 128:256].T
            return nothing

        lax.fori_loop(0, each // BLK, project, 0)
    out_copies = [
        pltpu.make_async_copy(at_ref, at_out, out_sems.at[0]),
        pltpu.make_async_copy(qkv_ref, qkv_out, out_sems.at[1]),
    ]
    for copy in out_copies:
        copy.start()

    blocks = length // BLK
    lse_ref[...] = jnp.zeros_like(lse_ref)

    def per_block(step, nothing):
        mine = pl.ds(pl.multiple_of(step * BLK, BLK), BLK)
        first = block_place(step, dev, half) * BLK
        seg_q = seg_of(first + lax.broadcasted_iota(jnp.int32, (1, BLK), 1), ends)
        queries = three_heads(qkv_ref[mine, 384:512].T, qkv_ref[mine, 512:576].T)
        low, high = doc_range(first, ends, length)

        def body(pair, carry):
            tiles = []
            for more in range(TILES):
                block = low + TILES * pair + more
                place = block_place(jnp.minimum(block, blocks - 1), dev, half)
                rows = pl.ds(pl.multiple_of(place * BLK, BLK), BLK)
                places = block * BLK + lax.broadcasted_iota(jnp.int32, (BLK, 1), 0)
                tiles.append((rows, seg_of(places, (*ends, length)) == seg_q))

            def score(head):
                lanes = slice(128, 256) if head == 2 else slice(0, 128)
                return [jnp.where(allowed, dot(qkv_ref[rows, lanes], queries[head]), NEG) for rows, allowed in tiles]

            def weigh(head, scores):
                top, total, acc = carry[head]
                new_top = jnp.maximum(top, jnp.max(reduce(jnp.maximum, scores), axis=0, keepdims=True))
                shrink = jnp.exp(top - new_top)
                exps = [jnp.exp(one - new_top) for one in scores]
                total = total * shrink + jnp.sum(reduce(jnp.add, exps), axis=0, keepdims=True)
                return new_top, total, acc * shrink, [exp.astype(BF16) for exp in exps]

            def gather(head, weighed):
                top, total, acc, exps = weighed
                for (rows, _), exp in zip(tiles, exps):
                    values = v2_t[HEAD:128, rows] if head == 2 else v01_t[head * HEAD : (head + 1) * HEAD, rows]
                    acc = acc + dot(values, exp)
                return top, total, acc

            s0 = score(0)
            s1 = score(1)
            w0 = weigh(0, s0)
            s2 = score(2)
            w1 = weigh(1, s1)
            r0 = gather(0, w0)
            w2 = weigh(2, s2)
            r1 = gather(1, w1)
            r2 = gather(2, w2)
            return r0, r1, r2

        start = tuple(
            (
                jnp.full((1, BLK), NEG, F32),
                jnp.zeros((1, BLK), F32),
                jnp.zeros((HEAD, BLK), F32),
            )
            for _ in range(3)
        )
        final = lax.fori_loop(0, (high - low + TILES - 1) // TILES, body, start)
        cols = pl.ds(pl.multiple_of((step % 2) * BLK, BLK), BLK)
        for head in range(3):
            top, total, acc = final[head]
            out_ref[step // 2, head * HEAD : (head + 1) * HEAD, cols] = (acc / total).astype(BF16)
            lse_ref[head : head + 1, mine] = top + jnp.log(total)
        return nothing

    lax.fori_loop(0, blocks, per_block, 0)
    for copy in out_copies:
        copy.wait()


def attention_forward(info, parts, w_qkv, bias, gain, shift, norm):
    each, width = parts[0].shape
    length = 4 * each
    return pl.pallas_call(
        partial(attention_forward_kernel, norm),
        name="attention_forward",
        grid_spec=pltpu.PrefetchScalarGridSpec(
            num_scalar_prefetch=1,
            grid=(1,),
            in_specs=[HBM] * 4 + [whole(w_qkv.shape), whole(bias.shape), whole(gain.shape), whole(shift.shape)],
            out_specs=[HBM, HBM, whole((4, 192, each)), whole((8, length))],
            scratch_shapes=[
                pltpu.VMEM((4, each, width), BF16),
                pltpu.VMEM((width, length), BF16),
                pltpu.VMEM((length, 576), BF16),
                pltpu.VMEM((128, length), BF16),
                pltpu.VMEM((128, length), BF16),
                pltpu.SemaphoreType.DMA((4,)),
                pltpu.SemaphoreType.DMA((2,)),
            ],
        ),
        out_shape=(
            jax.ShapeDtypeStruct((width, length), BF16),
            jax.ShapeDtypeStruct((length, 576), BF16),
            jax.ShapeDtypeStruct((4, 192, each), BF16),
            jax.ShapeDtypeStruct((8, length), F32),
        ),
        compiler_params=pltpu.CompilerParams(vmem_limit_bytes=48 << 20),
        cost_estimate=pl.CostEstimate(
            flops=14 * 10**9, transcendentals=3 * length * 1024, bytes_accessed=12 << 20
        ),
    )(info, *parts, w_qkv, bias, gain, shift)


def attention_backward_kernel(
    info, qkv_ref, out_ref, lse_ref, w_ref, g0, g1, g2, g3,
    du_out, core_out, far_out, own_out, sums_ref,
    q01_t, q2_t, delta, dq_t, grad_t, du_ref, core_ref, far_ref, own_ref, sems,
):
    length = qkv_ref.shape[0]
    each = length // 4
    ends = (info[0], info[1], info[2])
    dev, half = info[3], info[4]
    blocks = length // BLK
    q01_t[...] = qkv_ref[:, 384:512].T
    q2_t[...] = qkv_ref[:, 512:576].T
    dq_t[...] = jnp.zeros_like(dq_t)
    for part, grad in enumerate((g0, g1, g2, g3)):
        grad_t[part] = grad[...]
        for head in range(3):
            rows = slice(head * HEAD, (head + 1) * HEAD)
            both = out_ref[part, rows].astype(F32) * grad[rows].astype(F32)
            delta[head : head + 1, part * each : (part + 1) * each] = jnp.sum(both, axis=0, keepdims=True)

    def per_block(step, nothing):
        mine = pl.ds(pl.multiple_of(step * BLK, BLK), BLK)
        first = block_place(step, dev, half) * BLK
        seg_k = seg_of(first + lax.broadcasted_iota(jnp.int32, (BLK, 1), 0), ends)
        k01 = qkv_ref[mine, 0:128]
        k2v2 = qkv_ref[mine, 128:256]
        v01 = qkv_ref[mine, 256:384]
        k01_t = k01.T
        k2_t = k2v2.T[:HEAD]
        keys_t = (k01_t[:HEAD], k01_t[HEAD:], k2_t)
        low, high = doc_range(first, ends, length)

        def body(pair, carry):
            blank = jnp.zeros((HEAD, BLK), BF16)
            tiles = []
            for more in range(TILES):
                block = low + TILES * pair + more
                place = block_place(jnp.minimum(block, blocks - 1), dev, half)
                cols = pl.ds(pl.multiple_of(place * BLK, BLK), BLK)
                part_cols = pl.ds(pl.multiple_of((place % 2) * BLK, BLK), BLK)
                places = block * BLK + lax.broadcasted_iota(jnp.int32, (1, BLK), 1)
                allowed = seg_k == seg_of(places, (*ends, length))
                queries = three_heads(q01_t[:, cols], q2_t[:, cols])
                grads = grad_t[place // 2, :, part_cols]
                dos = (
                    jnp.concatenate((grads[:HEAD], blank), axis=0),
                    jnp.concatenate((blank, grads[HEAD:128]), axis=0),
                    jnp.concatenate((blank, grads[128:192]), axis=0),
                )
                tiles.append((cols, allowed, queries, dos))

            def first_dots(at):
                cols, allowed, queries, dos = tiles[at // 3]
                head = at % 3
                return (
                    dot(k2v2 if head == 2 else k01, queries[head]),
                    dot(k2v2 if head == 2 else v01, dos[head]),
                )

            def weigh(at, found):
                cols, allowed, queries, dos = tiles[at // 3]
                head = at % 3
                scores, grad_probs = found
                probs = jnp.where(allowed, jnp.exp(scores - lse_ref[head : head + 1, cols]), 0.0)
                grad_scores = (probs * (grad_probs - delta[head : head + 1, cols])).astype(BF16)
                return probs.astype(BF16), grad_scores

            def last_dots(at, found, sums):
                cols, allowed, queries, dos = tiles[at // 3]
                head = at % 3
                probs, grad_scores = found
                more_k = dot(grad_scores, queries[head], ((1,), (1,)))
                more_v = dot(probs, dos[head], ((1,), (1,)))
                more_q = dot(keys_t[head], grad_scores)
                dk01, dk2v2, dv01 = sums
                if head == 2:
                    dk2v2 = dk2v2 + more_k + more_v
                else:
                    dk01 = dk01 + more_k
                    dv01 = dv01 + more_v
                return (dk01, dk2v2, dv01), more_q

            count = 3 * TILES
            sums = carry
            more_q = []
            begun = {0: first_dots(0), 1: first_dots(1)}
            weighed = {}
            for at in range(count):
                if at + 2 < count:
                    begun[at + 2] = first_dots(at + 2)
                weighed[at] = weigh(at, begun[at])
                if at > 0:
                    sums, found = last_dots(at - 1, weighed[at - 1], sums)
                    more_q.append(found)
            sums, found = last_dots(count - 1, weighed[count - 1], sums)
            more_q.append(found)
            for tile in range(TILES):
                cols = tiles[tile][0]
                dq_t[:, cols] = dq_t[:, cols] + jnp.concatenate(more_q[3 * tile : 3 * tile + 3], axis=0)
            return sums

        zero = jnp.zeros((BLK, 128), F32)
        dk01, dk2v2, dv01 = lax.fori_loop(0, (high - low + TILES - 1) // TILES, body, (zero, zero, zero))
        du_ref[mine, 0:128] = dk01.astype(BF16)
        du_ref[mine, 128:256] = dk2v2.astype(BF16)
        du_ref[mine, 256:384] = dv01.astype(BF16)
        return nothing

    lax.fori_loop(0, blocks, per_block, 0)
    sums_ref[...] = jnp.zeros_like(sums_ref)
    scale = HEAD**-0.5

    def finish_rows(at, total):
        rows = pl.ds(pl.multiple_of(at * BLK, BLK), BLK)
        du_ref[rows, 384:512] = (dq_t[0:128, rows] * scale).T.astype(BF16)
        du_ref[rows, 512:576] = (dq_t[128:192, rows] * scale).T.astype(BF16)
        return total + jnp.sum(du_ref[rows, :].astype(F32), axis=0, keepdims=True)

    sums_ref[0:1, :] = lax.fori_loop(0, blocks, finish_rows, jnp.zeros((1, 576), F32))
    copies = [pltpu.make_async_copy(du_ref, du_out, sems.at[0])]
    copies[0].start()
    plan = ((1, core_ref.at[0], core_out.at[0]), (3, core_ref.at[1], core_out.at[1]), (2, far_ref, far_out), (0, own_ref, own_out))
    for at, (part, target, goal) in enumerate(plan):
        kind = target.dtype
        target[...] = dot(du_ref[part * each : (part + 1) * each, :], w_ref[...], ((1,), (1,))).astype(kind)
        copies.append(pltpu.make_async_copy(target, goal, sems.at[at + 1]))
        copies[-1].start()
    for copy in copies:
        copy.wait()


def attention_backward(info, qkv, out, lse, w_qkv, grads):
    length, each, width = qkv.shape[0], qkv.shape[0] // 4, w_qkv.shape[0]
    return pl.pallas_call(
        attention_backward_kernel,
        name="attention_backward",
        grid_spec=pltpu.PrefetchScalarGridSpec(
            num_scalar_prefetch=1,
            grid=(1,),
            in_specs=[whole(qkv.shape), whole(out.shape), whole(lse.shape), whole(w_qkv.shape)]
            + [whole((192, each))] * 4,
            out_specs=[HBM, HBM, HBM, HBM, whole((8, 576))],
            scratch_shapes=[
                pltpu.VMEM((128, length), BF16),
                pltpu.VMEM((64, length), BF16),
                pltpu.VMEM((8, length), F32),
                pltpu.VMEM((192, length), F32),
                pltpu.VMEM((4, 192, each), BF16),
                pltpu.VMEM((length, 576), BF16),
                pltpu.VMEM((2, each, width), BF16),
                pltpu.VMEM((each, width), F32),
                pltpu.VMEM((each, width), F32),
                pltpu.SemaphoreType.DMA((5,)),
            ],
        ),
        out_shape=(
            jax.ShapeDtypeStruct(qkv.shape, BF16),
            jax.ShapeDtypeStruct((2, each, width), BF16),
            jax.ShapeDtypeStruct((each, width), F32),
            jax.ShapeDtypeStruct((each, width), F32),
            jax.ShapeDtypeStruct((8, 576), F32),
        ),
        compiler_params=pltpu.CompilerParams(vmem_limit_bytes=56 << 20),
        cost_estimate=pl.CostEstimate(
            flops=20 * 10**9, transcendentals=3 * length * 1024, bytes_accessed=16 << 20
        ),
    )(info, qkv, out, lse, w_qkv, *grads)


def attention_weights_kernel(at_ref, du_ref, vec_ref, own_ref, core_ref, far_ref, out_ref, spread):
    blank = jnp.zeros((128 - vec_ref.shape[0], vec_ref.shape[1]), F32)
    out_ref[:, 768:896] = jnp.concatenate((vec_ref[...], blank), axis=0).T.astype(BF16)
    out_ref[:, 0:576] = dot(at_ref[...], du_ref[...]).astype(BF16)
    total = own_ref[...].astype(F32) + core_ref[...].astype(F32) + far_ref[...].astype(F32)
    quarter = own_ref.shape[0]
    for piece in range(4):
        rows = pl.ds(piece, quarter, stride=4)
        spread[0, rows, :] = total[:, piece * 192 : piece * 192 + 128]
        spread[1, rows, :] = jnp.concatenate(
            (total[:, piece * 192 + 128 : (piece + 1) * 192], jnp.zeros((quarter, 64), F32)), axis=1
        )
    out_ref[:, 576:704] = spread[0].astype(BF16)
    out_ref[:, 704:768] = spread[1, :, 0:64].astype(BF16)


def attention_weights(a_t, du, vectors, own, core, far):
    width = a_t.shape[0]
    return pl.pallas_call(
        attention_weights_kernel,
        name="attention_weights",
        grid=(1,),
        in_specs=[whole(v.shape) for v in (a_t, du, vectors, own, core, far)],
        out_specs=whole((width, width + 128)),
        out_shape=jax.ShapeDtypeStruct((width, width + 128), BF16),
        scratch_shapes=[pltpu.VMEM((2, width, 128), F32)],
        compiler_params=pltpu.CompilerParams(vmem_limit_bytes=48 << 20),
        cost_estimate=pl.CostEstimate(flops=18 * 10**8, transcendentals=0, bytes_accessed=8 << 20),
    )(a_t, du, vectors, own, core, far)


def out_kernel(info, p0, p1, p2, p3, w_ref, x_ref, vec_ref, ctx_ref, mid_ref, c_ref, ctx):
    dev = info[3]
    loc, toks = p0.shape
    for rel, part in enumerate((p0, p1, p2, p3)):
        ctx[dev ^ rel] = part[...]
    ctx_ref[...] = ctx[...].reshape(4 * loc, toks)

    def rows_of(at, nothing):
        rows = pl.ds(pl.multiple_of(at * 128, 128), 128)
        found = dot(ctx_ref[:, rows].T, w_ref[...])
        middle = x_ref[rows, :] + found + vec_ref[0:1, :]
        mid_ref[rows, :] = middle
        c_ref[rows, :] = norm_rows(middle, vec_ref[1:2, :], vec_ref[2:3, :]).astype(BF16)
        return nothing

    lax.fori_loop(0, toks // 128, rows_of, 0)


def out_forward(info, parts, w_out, current, vectors):
    loc, toks = parts[0].shape
    width = w_out.shape[1]
    return pl.pallas_call(
        out_kernel,
        name="out_forward",
        grid_spec=pltpu.PrefetchScalarGridSpec(
            num_scalar_prefetch=1,
            grid=(1,),
            in_specs=[whole((loc, toks))] * 4 + [whole(w_out.shape), whole(current.shape), whole(vectors.shape)],
            out_specs=[whole((width, toks)), whole((toks, width)), whole((toks, width))],
            scratch_shapes=[pltpu.VMEM((4, loc, toks), BF16)],
        ),
        out_shape=(
            jax.ShapeDtypeStruct((width, toks), BF16),
            jax.ShapeDtypeStruct((toks, width), F32),
            jax.ShapeDtypeStruct((toks, width), BF16),
        ),
        compiler_params=pltpu.CompilerParams(vmem_limit_bytes=48 << 20),
        cost_estimate=pl.CostEstimate(flops=10**9, transcendentals=0, bytes_accessed=7 << 20),
    )(info, *parts, w_out, current, vectors)


def norm_back(grad, values, gain):
    centred = values - jnp.mean(values, axis=-1, keepdims=True)
    inv_std = lax.rsqrt(jnp.mean(centred * centred, axis=-1, keepdims=True) + EPS)
    normed = centred * inv_std
    scaled = grad * gain
    grad_in = inv_std * (
        scaled
        - jnp.mean(scaled, axis=-1, keepdims=True)
        - normed * jnp.mean(scaled * normed, axis=-1, keepdims=True)
    )
    return grad_in, jnp.sum(grad * normed, axis=0, keepdims=True), jnp.sum(grad, axis=0, keepdims=True)


def norm_back_kernel(own, core, far, x_ref, gain_ref, mid_ref, grad_ref, sums_ref):
    toks, width = x_ref.shape

    def rows_of(at, sums):
        rows = pl.ds(pl.multiple_of(at * 64, 64), 64)
        found = own[rows, :] + core[0, rows, :].astype(F32) + far[rows, :].astype(F32)
        grad_in, gain_sum, bias_sum = norm_back(found, x_ref[rows, :], gain_ref[...])
        grad_ref[rows, :] = mid_ref[rows, :] + grad_in
        return sums[0] + gain_sum, sums[1] + bias_sum

    zero = jnp.zeros((1, width), F32)
    sums = lax.fori_loop(0, toks // 64, rows_of, (zero, zero))
    sums_ref[...] = jnp.zeros_like(sums_ref)
    sums_ref[0:1, :] = sums[0]
    sums_ref[1:2, :] = sums[1]


def norm_backward(own, core, far, values, gain, middle_grad):
    toks, width = values.shape
    return pl.pallas_call(
        norm_back_kernel,
        name="norm_backward",
        grid=(1,),
        in_specs=[
            whole((toks, width)),
            pl.BlockSpec((1, toks, width), lambda i: (0, 0, 0)),
            whole((toks, width)),
            whole((toks, width)),
            whole(gain.shape),
            whole((toks, width)),
        ],
        out_specs=[whole((toks, width)), whole((8, width))],
        out_shape=(jax.ShapeDtypeStruct((toks, width), F32), jax.ShapeDtypeStruct((8, width), F32)),
        compiler_params=pltpu.CompilerParams(vmem_limit_bytes=48 << 20),
        cost_estimate=pl.CostEstimate(flops=10**7, transcendentals=0, bytes_accessed=9 << 20),
    )(own, core, far, values, gain, middle_grad)


GELU_A = (2.0 / 3.141592653589793) ** 0.5
GELU_B = 0.044715


def gelu(t):
    square = t * t
    tanh = jnp.tanh(t * (GELU_A + GELU_A * GELU_B * square))
    half = 0.5 * t
    side = 0.5 + 0.5 * tanh
    slope = side + (half - half * tanh * tanh) * (GELU_A + 3.0 * GELU_A * GELU_B * square)
    return t * side, slope


def fetch(parts, held, sems):
    units = parts[0].shape[0]
    copies = [
        pltpu.make_async_copy(part, held.at[at // 2, pl.ds((at % 2) * units, units)], sems.at[at])
        for at, part in enumerate(parts)
    ]
    for copy in copies:
        copy.start()
    return copies


def feed_kernel(norm, c_ref, mid_ref, vec_ref, *refs):
    parts, refs = refs[:8], refs[8:]
    if norm:
        slope_out, act_out, x_ref, a_ref, slope_ref, act_ref, held, sems, out_sems = refs
    else:
        slope_out, act_out, x_ref, slope_ref, act_ref, held, sems, out_sems = refs
    toks, width = mid_ref.shape
    units = held.shape[1]
    copies = fetch(parts, held, sems)
    x_ref[...] = mid_ref[...] + vec_ref[0:1, :]
    outs = []

    def before(at):
        copies[2 * at].wait()
        copies[2 * at + 1].wait()
        bias = held[at, :, 2 * width : 2 * width + 128].T[0:1].astype(F32)
        return dot(c_ref[...], held[at, :, 0:width], ((1,), (1,))) + bias

    def after(at, pre):
        act, slope = gelu(pre)
        act = act.astype(BF16)
        slope_ref[at] = slope.astype(BF16)
        act_ref[at] = act.T
        outs.append(pltpu.make_async_copy(slope_ref.at[at], slope_out.at[at], out_sems.at[2 * at]))
        outs.append(pltpu.make_async_copy(act_ref.at[at], act_out.at[at], out_sems.at[2 * at + 1]))
        outs[-2].start()
        outs[-1].start()
        x_ref[...] += dot(act, held[at, :, width : 2 * width])

    pre = before(0)
    for at in range(4):
        later = before(at + 1) if at < 3 else None
        after(at, pre)
        pre = later

    if norm:

        def rows_of(at, nothing):
            rows = pl.ds(pl.multiple_of(at * 64, 64), 64)
            a_ref[rows, :] = norm_rows(x_ref[rows, :], vec_ref[1:2, :], vec_ref[2:3, :]).astype(BF16)
            return nothing

        lax.fori_loop(0, toks // 64, rows_of, 0)
    for copy in outs:
        copy.wait()


def feed_forward(c, middle, vectors, parts, norm):
    toks, width = middle.shape
    units = 2 * parts[0].shape[0]
    out_shape = [
        jax.ShapeDtypeStruct((4, toks, units), BF16),
        jax.ShapeDtypeStruct((4, units, toks), BF16),
        jax.ShapeDtypeStruct((toks, width), F32),
    ]
    if norm:
        out_shape.append(jax.ShapeDtypeStruct((toks, width), BF16))
    return pl.pallas_call(
        partial(feed_kernel, norm),
        name="feed_forward",
        grid=(1,),
        in_specs=[whole(c.shape), whole(middle.shape), whole(vectors.shape)] + [HBM] * 8,
        out_specs=[HBM, HBM] + [whole(shape.shape) for shape in out_shape[2:]],
        out_shape=out_shape,
        scratch_shapes=[
            pltpu.VMEM((4, toks, units), BF16),
            pltpu.VMEM((4, units, toks), BF16),
            pltpu.VMEM((4, units, parts[0].shape[1]), BF16),
            pltpu.SemaphoreType.DMA((8,)),
            pltpu.SemaphoreType.DMA((8,)),
        ],
        compiler_params=pltpu.CompilerParams(vmem_limit_bytes=56 << 20),
        cost_estimate=pl.CostEstimate(flops=5 * 10**9, transcendentals=2 * 10**6, bytes_accessed=20 << 20),
    )(c, middle, vectors, *parts)


def feed_back_kernel(info, grad_ref, slope_in, mid_ref, gain_ref, w_ref, *refs):
    parts, refs = refs[:8], refs[8:]
    dh_out, dm_ref, dmid_ref, da_ref, sums_ref, d0, d1, d2, d3 = refs[:9]
    slope_ref, dh_ref, held, dc, sems, slope_sems, out_sems = refs[9:]
    dev = info[3]
    toks, width = mid_ref.shape
    loc = d0.shape[0]
    copies = fetch(parts, held, sems)
    slopes = [pltpu.make_async_copy(slope_in.at[at], slope_ref.at[at], slope_sems.at[at]) for at in range(4)]
    for copy in slopes:
        copy.start()
    dm_ref[...] = grad_ref[...].astype(BF16)
    outs = []

    def before(at):
        copies[2 * at].wait()
        copies[2 * at + 1].wait()
        return dot(dm_ref[...], held[at, :, width : 2 * width], ((1,), (1,)))

    def after(at, dact):
        slopes[at].wait()
        dpre = (dact * slope_ref[at].astype(F32)).astype(BF16)
        dh_ref[at] = dpre
        outs.append(pltpu.make_async_copy(dh_ref.at[at], dh_out.at[at], out_sems.at[at]))
        outs[-1].start()
        term = dot(dpre, held[at, :, 0:width])
        if at == 0:
            dc[...] = term
        else:
            dc[...] += term

    dact = before(0)
    for at in range(4):
        later = before(at + 1) if at < 3 else None
        after(at, dact)
        dact = later

    def rows_of(at, sums):
        rows = pl.ds(pl.multiple_of(at * 64, 64), 64)
        grad_in, gain_sum, bias_sum = norm_back(dc[rows, :], mid_ref[rows, :], gain_ref[...])
        grad_mid = grad_ref[rows, :] + grad_in
        dmid_ref[rows, :] = grad_mid
        branch = grad_mid.astype(BF16)
        da_ref[rows, :] = branch
        out_sum = jnp.sum(branch.astype(F32), axis=0, keepdims=True)
        down_sum = jnp.sum(dm_ref[rows, :].astype(F32), axis=0, keepdims=True)
        return sums[0] + gain_sum, sums[1] + bias_sum, sums[2] + out_sum, sums[3] + down_sum

    zero = jnp.zeros((1, width), F32)
    sums = lax.fori_loop(0, toks // 64, rows_of, (zero,) * 4)
    sums_ref[...] = jnp.zeros_like(sums_ref)
    for at in range(4):
        sums_ref[at : at + 1, :] = sums[at]
    for rel, target in enumerate((d0, d1, d2, d3)):
        rows = pl.ds(pl.multiple_of((dev ^ rel) * loc, 64), loc)
        target[...] = dot(w_ref[rows, :], da_ref[...], ((1,), (1,))).astype(BF16)
    for copy in outs:
        copy.wait()


def feed_backward(info, grad, slope, middle, gain, w_out, parts):
    toks, width = middle.shape
    loc = width // 4
    units = 2 * parts[0].shape[0]
    shapes = [
        jax.ShapeDtypeStruct(slope.shape, BF16),
        jax.ShapeDtypeStruct((toks, width), BF16),
        jax.ShapeDtypeStruct((toks, width), F32),
        jax.ShapeDtypeStruct((toks, width), BF16),
        jax.ShapeDtypeStruct((8, width), F32),
    ] + [jax.ShapeDtypeStruct((loc, toks), BF16)] * 4
    return pl.pallas_call(
        feed_back_kernel,
        name="feed_backward",
        grid_spec=pltpu.PrefetchScalarGridSpec(
            num_scalar_prefetch=1,
            grid=(1,),
            in_specs=[whole(grad.shape), HBM, whole(middle.shape), whole(gain.shape), whole(w_out.shape)] + [HBM] * 8,
            out_specs=[HBM] + [whole(shape.shape) for shape in shapes[1:]],
            scratch_shapes=[
                pltpu.VMEM((4, toks, units), BF16),
                pltpu.VMEM((4, toks, units), BF16),
                pltpu.VMEM((4, units, parts[0].shape[1]), BF16),
                pltpu.VMEM((toks, width), F32),
                pltpu.SemaphoreType.DMA((8,)),
                pltpu.SemaphoreType.DMA((4,)),
                pltpu.SemaphoreType.DMA((4,)),
            ],
        ),
        out_shape=shapes,
        compiler_params=pltpu.CompilerParams(vmem_limit_bytes=60 << 20),
        cost_estimate=pl.CostEstimate(flops=6 * 10**9, transcendentals=2 * 10**6, bytes_accessed=24 << 20),
    )(info, grad, slope, middle, gain, w_out, *parts)


def feed_weights_kernel(add, dh_ref, act_ref, c_ref, dm_ref, *refs):
    width = c_ref.shape[1]
    out_ref = refs[-1]
    dh = dh_ref[0].T
    up = dot(dh, c_ref[...])
    down = dot(act_ref[0], dm_ref[...])
    bias = jnp.broadcast_to(jnp.sum(dh.astype(F32), axis=1, keepdims=True), (dh.shape[0], 128))
    if add:
        up = up + refs[0][:, 0:width].astype(F32)
        down = down + refs[0][:, width : 2 * width].astype(F32)
        bias = bias + refs[0][:, 2 * width :].astype(F32)
    out_ref[:, 0:width] = up.astype(BF16)
    out_ref[:, width : 2 * width] = down.astype(BF16)
    out_ref[:, 2 * width :] = bias.astype(BF16)


def feed_weights(dh, act, c, dm, quarter, add=None):
    units, toks, width = dh.shape[2], c.shape[0], c.shape[1]
    wide = 2 * width + 128
    step = 256
    out = pl.BlockSpec((step, wide), lambda i: (i, 0))
    return pl.pallas_call(
        partial(feed_weights_kernel, add is not None),
        name="feed_weights",
        grid=(units // step,),
        in_specs=[
            pl.BlockSpec((1, toks, step), lambda i: (quarter, 0, i)),
            pl.BlockSpec((1, step, toks), lambda i: (quarter, i, 0)),
            whole(c.shape),
            whole(dm.shape),
        ]
        + ([out] if add is not None else []),
        out_specs=out,
        out_shape=jax.ShapeDtypeStruct((units, wide), BF16),
        compiler_params=pltpu.CompilerParams(vmem_limit_bytes=48 << 20),
        cost_estimate=pl.CostEstimate(flops=24 * 10**8, transcendentals=0, bytes_accessed=6 << 20),
    )(dh, act, c, dm, *([add] if add is not None else []))


def finish_kernel(fill, info, *refs):
    attn, hidden, refs = refs[:4], refs[4:8], refs[8:]
    if fill:
        refs = refs[4:]
    qkv_ref, out_ref, up_ref, down_ref, bias_ref, vec_ref, qkv_at, out_at, hid_at = refs
    vectors = sum(part[:, 768:896].astype(F32) for part in attn)
    vec_ref[...] = vectors.T[0 : vec_ref.shape[0]]
    dev = info[3]
    spot = info[5]
    rows = attn[0].shape[0]
    loc = 192
    for rel in range(4):
        qkv_at[dev ^ rel] = attn[rel][:, 0:576].astype(F32)
        out_at[dev ^ rel, 0] = attn[rel][:, 576:704].astype(F32)
        out_at[dev ^ rel, 1, :, 0:64] = attn[rel][:, 704:768].astype(F32)
        hid_at[spot ^ rel] = hidden[rel][...].astype(F32)
    width = 4 * loc
    quarter = rows // 4
    units = hidden[0].shape[0]
    for at in range(4):
        cols = slice(at * loc, (at + 1) * loc)
        found = qkv_at[at]
        qkv_ref[0, :, at * loc : (at + 1) * loc] = found[:, 384:576]
        qkv_ref[0, :, width + at * loc : width + (at + 1) * loc] = found[:, 0:192]
        v_at = 2 * width + at * loc
        qkv_ref[0, :, v_at : v_at + 128] = found[:, 256:384]
        qkv_ref[0, :, v_at + 128 : v_at + 192] = found[:, 192:256]
        for piece in range(4):
            goal = slice(at * quarter, (at + 1) * quarter)
            lane = piece * loc
            out_ref[0, goal, lane : lane + 128] = out_at[at, 0, pl.ds(piece, quarter, stride=4), :]
            out_ref[0, goal, lane + 128 : lane + 192] = out_at[at, 1, pl.ds(piece, quarter, stride=4), :][:, 0:64]
        down_ref[0, at * units : (at + 1) * units, :] = hid_at[at, :, width : 2 * width]
        bias_ref[0, at * units : (at + 1) * units, :] = hid_at[at, :, 2 * width :]
    up = jnp.concatenate([hid_at[at, :, 0:width] for at in range(4)], axis=0)
    up_ref[0] = up.T


def finish(info, layer, attn, hidden, before):
    rows, width = attn[0].shape[0], attn[0].shape[1] - 128
    units = hidden[0].shape[0]
    shapes = [
        (LAYERS, rows, 3 * width),
        (LAYERS, rows, width),
        (LAYERS, width, 4 * units),
        (LAYERS, 4 * units, width),
        (LAYERS, 4 * units, 128),
    ]
    specs = [pl.BlockSpec((1, *shape[1:]), lambda i, info: (layer, 0, 0)) for shape in shapes]
    specs.append(whole((16, rows)))
    shapes.append((16, rows))
    fill = before is not None
    given = list(before[:4]) if fill else []
    return pl.pallas_call(
        partial(finish_kernel, fill),
        name="finish",
        grid_spec=pltpu.PrefetchScalarGridSpec(
            num_scalar_prefetch=1,
            grid=(1,),
            in_specs=[whole(attn[0].shape)] * 4 + [whole(hidden[0].shape)] * 4 + [HBM] * len(given),
            out_specs=specs,
            scratch_shapes=[
                pltpu.VMEM((4, rows, 576), F32),
                pltpu.VMEM((4, 2, rows, 128), F32),
                pltpu.VMEM((4, units, 2 * width + 128), F32),
            ],
        ),
        out_shape=[jax.ShapeDtypeStruct(shape, F32) for shape in shapes],
        input_output_aliases={9 + at: at for at in range(len(given))},
        compiler_params=pltpu.CompilerParams(vmem_limit_bytes=56 << 20),
        cost_estimate=pl.CostEstimate(flops=10**6, transcendentals=0, bytes_accessed=8 << 20),
    )(info, *attn, *hidden, *given)


PLANE = ("cx", "core", "tp")


def turned(value, first):
    pairs = []
    for x in range(2):
        for core in range(2):
            for y in range(2):
                flip_x = (core == 0) == first
                target = ((1 - x) if flip_x else x, core, y if flip_x else 1 - y)
                pairs.append((x * 4 + core * 2 + y, target[0] * 4 + target[1] * 2 + target[2]))
    return lax.ppermute(value, PLANE, pairs)


def after(value, *others):
    return lax.optimization_barrier((value, *others))[0]


def diagonal(value):
    return lax.ppermute(value, ("cx", "core"), ((0, 3), (1, 2), (2, 1), (3, 0)))


def around(own):
    far = swap(own, "cx")
    return own, swap(own, "core"), far, swap(far, "core")


def local(
    hidden_in,
    doc_lengths,
    ln1_gain,
    ln1_bias,
    qkv_weight,
    qv_bias,
    out_weight,
    out_bias,
    ln2_gain,
    ln2_bias,
    up_weight,
    up_bias,
    down_weight,
    down_bias,
    output_grad,
):
    shards = lax.axis_size("shard")
    ix, ic, iy = lax.axis_index("cx"), lax.axis_index("core"), lax.axis_index("tp")
    dev = ix * 2 + ic
    seqs, toks, width = hidden_in.shape
    rows = ln1_gain.shape[1]
    units = up_bias.shape[1] // 4
    loc = width // 4
    quarter = rows // 4

    def to_sequence(tokens):
        own = lax.dynamic_index_in_dim(tokens, iy, 0, keepdims=False)
        other = lax.dynamic_index_in_dim(tokens, 1 - iy, 0, keepdims=False)
        return jnp.concatenate((own, swap(other, "tp")), axis=0)

    def from_sequence(tokens):
        own, other = tokens[:toks], swap(tokens[toks:], "tp")
        return jnp.where(iy == 0, jnp.stack((own, other)), jnp.stack((other, own)))

    lengths = lax.dynamic_index_in_dim(doc_lengths, iy, 0, keepdims=False)
    end0 = lengths[0]
    end1 = end0 + lengths[1]
    end2 = end1 + lengths[2]
    info = jnp.stack((end0, end1, end2, dev, iy, ic * 2 + ix, dev, dev)).astype(jnp.int32)
    row_ids = jnp.arange(2 * toks, dtype=jnp.int32)
    places = dev * (2 * toks) + ((row_ids // toks) ^ iy) * toks + row_ids % toks
    keep = (places < end2).astype(F32)[:, None]

    def columns(array, start):
        return lax.dynamic_slice_in_dim(array, start, loc, 1)

    small = jnp.concatenate(
        [ln1_gain, ln1_bias, out_bias, ln2_gain, ln2_bias, down_bias, qv_bias.reshape(2 * LAYERS, rows)], axis=0
    )
    small = jnp.pad(small, ((0, 128 - small.shape[0]), (0, 0))).T

    def attention_piece(layer):
        weight = qkv_weight[layer]
        q, k, v = (columns(weight, which * width + loc * dev) for which in range(3))
        out = lax.dynamic_slice_in_dim(out_weight[layer], quarter * dev, quarter, 0).reshape(rows, loc)
        pieces = [k[:, :128], k[:, 128:], v[:, 128:], v[:, :128], q, out]
        if layer == 0:
            pieces.append(small)
        return jnp.concatenate(pieces, axis=1)

    def hidden_piece(layer):
        start = ic * 2 * units + ix * units
        up = lax.dynamic_slice_in_dim(up_weight[layer], start, units, 1).T
        down = lax.dynamic_slice_in_dim(down_weight[layer], start, units, 0)
        bias = lax.dynamic_slice_in_dim(up_bias[layer], start, units, 0)
        bias = jnp.broadcast_to(bias[:, None], (units, 128))
        return jnp.concatenate((up, down, bias), axis=1)

    def over_shards(piece):
        return lax.all_gather(piece, "shard", axis=0, tiled=True)

    def spread_hidden(own, one, *others):
        own, one = lax.optimization_barrier((own, one, *others))[:2]
        return own, one, turned(own, False), turned(one, False)

    def both_cores(parts):
        return tuple(parts) + tuple(swap(part, "core") for part in parts)

    def sum_shards(value):
        if shards != 4:
            return lax.psum_scatter(value, "shard", scatter_dimension=0, tiled=True)
        each = value.reshape(shards, -1, value.shape[1])
        index = lax.axis_index("shard")
        total = lax.dynamic_index_in_dim(each, index, 0, keepdims=False).astype(F32)
        for by in range(1, shards):
            piece = lax.dynamic_index_in_dim(each, (index + by) % shards, 0, keepdims=False)
            piece = lax.ppermute(piece, "shard", [(i, (i + by) % shards) for i in range(shards)])
            total = total + piece.astype(F32)
        return total.astype(value.dtype)

    hidden_own = to_sequence(hidden_in)
    grad = to_sequence(output_grad).astype(F32) * keep
    first_parts = around(hidden_own)
    attn0 = over_shards(attention_piece(0))
    feed0 = over_shards(after(hidden_piece(0), attn0, grad, *first_parts))

    def second_weights(*others):
        attn = attention_piece(1)
        piece = jnp.concatenate((hidden_piece(1), attn[:units], attn[units:]), axis=1)
        gathered = over_shards(after(piece, *others))
        wide = 2 * width + 128
        halves = [gathered[:, at : at + width].reshape(shards, 1, units, width) for at in (wide, wide + width)]
        return jnp.concatenate(halves, axis=1).reshape(width, width), gathered[:, :wide]

    def out_weights(own):
        full = jnp.zeros((shards, 4, quarter, width), BF16)
        for rel, part in enumerate(around(own)):
            full = lax.dynamic_update_slice(full, part, (0, dev ^ rel, 0, 0))
        return full.reshape(width, width)

    def out_own(gathered):
        return gathered[:, 3 * loc : 4 * loc].reshape(shards, 1, quarter, width)

    weights = []

    smalls = attn0[:, 4 * loc :].T.astype(F32)
    names = [[smalls[which * LAYERS + layer][None] for which in range(6)] for layer in range(LAYERS)]
    qv = smalls[6 * LAYERS : 8 * LAYERS].reshape(LAYERS, 2, shards, rows)
    qv = jnp.transpose(qv, (0, 2, 1, 3)).reshape(LAYERS, 2 * width)

    current = hidden_own.astype(F32)
    attn_parts = first_parts
    saved = []
    for layer in range(LAYERS):
        gain_one, bias_one, bias_out, gain_two, bias_two, bias_down = names[layer]
        w_qkv = (attn0 if layer == 0 else attn1)[:, : 3 * loc]
        q_bias = lax.dynamic_slice_in_dim(qv[layer], loc * dev, loc, 0)
        v_bias = lax.dynamic_slice_in_dim(qv[layer], width + loc * dev, loc, 0)
        bias = jnp.concatenate((jnp.zeros((192,), F32), v_bias[128:], v_bias[:128], q_bias))[None]
        attn_t, qkv, attended, lse = attention_forward(info, attn_parts, w_qkv, bias, gain_one, bias_one, layer == 0)
        if layer == 0:
            attn1, feed1 = second_weights(attended, feed0)
            w_out = out_own(attn0)
            attended, w_out = lax.optimization_barrier((attended, w_out))
            w_out = out_weights(w_out)
        else:
            own, one, two, three = w_feed1
            early_core = (swap(own, "core"), swap(one, "core"))
            attended, w_out, own, one, two, three, *early_core = lax.optimization_barrier(
                (attended, w_out1, own, one, two, three, *early_core)
            )
        parts = (
            attended[0],
            swap(attended[1], "core"),
            swap(attended[2], "cx"),
            diagonal(attended[3]),
        )
        if layer == 1:
            late_core = [swap(after(part, *parts), "core") for part in (two, three)]
            w_feed = (own, one, two, three, *early_core, *late_core)
        if layer == 0:
            own, *others = lax.optimization_barrier((feed0, *parts, w_out))
            one = turned(own, True)
            two = turned(own, False)
        vectors = jnp.concatenate((bias_out, gain_two, bias_two), axis=0)
        context, middle, mlp_in = out_forward(info, parts, w_out, current, vectors)
        if layer == 0:
            three = turned(after(one, mlp_in), False)
            w_feed = both_cores((own, one, two, three))
            vectors = jnp.concatenate((bias_down, names[1][0], names[1][1]), axis=0)
            mlp_in, feed1 = lax.optimization_barrier((mlp_in, feed1))
            slope, act, result, attn_own = feed_forward(mlp_in, middle, vectors, w_feed, True)
            one = turned(feed1, True)
            attn_parts = around(after(attn_own, one))
            w_out1 = out_weights(after(out_own(attn1), *attn_parts))
            w_feed1 = spread_hidden(feed1, one, *attn_parts)
        else:
            slope, act, result = feed_forward(mlp_in, middle, bias_down, w_feed, False)
        weights.append((w_qkv, w_out, w_feed))
        saved.append((current, attn_t, qkv, attended, lse, context, middle, mlp_in, slope, act))
        current = result
    hidden_out = from_sequence((current * keep).astype(BF16))

    n = shards * units

    attn_sums = [None] * LAYERS
    feed_sums = [None] * LAYERS
    by_attention, by_core = (), ()
    for layer in reversed(range(LAYERS)):
        x_in, attn_t, qkv, attended, lse, context, middle, mlp_in, slope, act = saved[layer]
        gain_one, _, _, gain_two, _, _ = names[layer]
        w_qkv, w_out, w_feed = weights[layer]
        dh, dm, middle_grad, branch_grad, sums_two, d0, d1, d2, d3 = feed_backward(
            info, grad, slope, middle, gain_two, w_out, w_feed
        )
        attn_grads = (d0, swap(d1, "core"), swap(d2, "cx"), diagonal(d3))
        other_late = swap(feed_weights(dh, act, mlp_in, dm, 3), "core")
        late = feed_weights(dh, act, mlp_in, dm, 1, other_late)
        w_out_grad = dot(context, branch_grad).astype(BF16).reshape(shards, 4, quarter, width)
        pieces = [lax.dynamic_index_in_dim(w_out_grad, dev ^ rel, 1, keepdims=False) for rel in range(4)]
        got = swap(jnp.stack((pieces[1], pieces[3])), "core")
        to_far_out = (pieces[2].astype(F32) + got[1].astype(F32)).astype(BF16)
        ready = [*attn_grads, late, to_far_out, *by_attention]
        if layer == 0:
            other_early = swap(feed_weights(dh, act, mlp_in, dm, 2), "core")
            early = feed_weights(dh, act, mlp_in, dm, 0, other_early)
            far = swap(to_far_out, "cx")
            ready += [early, far]
        *attn_grads, late, to_far_out = lax.optimization_barrier(tuple(ready))[:6]
        du, to_core, to_far, own, sums_u = attention_backward(info, qkv, attended, lse, w_qkv, attn_grads)
        late = turned(late, False)
        to_core = after(to_core, late, *by_core)
        from_core = swap(to_core, "core")
        to_far = (to_far + from_core[1].astype(F32)).astype(BF16)
        if layer == 0:
            part = (early[n:].astype(F32) + late[n:].astype(F32)).astype(BF16)
            kept = early[:n].astype(F32) + late[:n].astype(F32)
            arrived = turned(part, True)
            to_far = after(to_far, arrived)
        from_far = swap(to_far, "cx")
        if layer > 0:
            far = swap(after(to_far_out, to_far), "cx")
            du, dh_late, early_late = lax.optimization_barrier((du, dh, late, to_far))[:3]
            other_early = swap(feed_weights(dh_late, act, mlp_in, dm, 2), "core")
            early = feed_weights(dh_late, act, mlp_in, dm, 0, other_early)
            part = (early[n:].astype(F32) + early_late[n:].astype(F32)).astype(BF16)
            kept = early[:n].astype(F32) + early_late[:n].astype(F32)
        du_sum = sums_u[0]
        v_sum = jnp.concatenate((du_sum[256:384], du_sum[192:256]))
        q_row = lax.dynamic_update_slice_in_dim(jnp.zeros((width,), F32), du_sum[384:], loc * dev, 0)
        v_row = lax.dynamic_update_slice_in_dim(jnp.zeros((width,), F32), v_sum, loc * dev, 0)
        qv_rows = jnp.concatenate((q_row, v_row)).reshape(shards, 2, rows).transpose(1, 0, 2).reshape(2, width)
        vectors = jnp.concatenate((sums_two, qv_rows, jnp.zeros((6, width), F32)), axis=0)
        if layer == 0:
            vectors = jnp.concatenate((vectors[:10], sums_one[:2], vectors[12:]), axis=0)
        flat = [piece.reshape(shards * quarter, width) for piece in (pieces[0], got[0], far)]
        joined = attention_weights(attn_t, du, vectors, *flat)
        attn_sum = lax.psum_scatter(joined, "shard", scatter_dimension=0, tiled=True)
        if layer > 0:
            by_attention = (attn_sum,)
            from_far, part = lax.optimization_barrier((from_far, part))
            arrived = turned(part, True)
        attn_sum = (attn_sum.astype(F32) + swap(attn_sum, "tp").astype(F32)).astype(BF16)
        attn_sums[layer] = around(attn_sum)
        part = (kept + arrived.astype(F32)).astype(BF16)
        grad, sums_one = norm_backward(own, from_core, from_far, x_in, gain_one, middle_grad)
        if layer > 0:
            hidden = lax.psum_scatter(part, "shard", scatter_dimension=0, tiled=True)
        else:
            hidden = sum_shards(part)
            halves = sums_one[:2].reshape(2, shards, 2, units).transpose(1, 3, 0, 2).reshape(n, 4)
            lone = sum_shards(jnp.pad(halves, ((0, 0), (0, 124))))
            hidden = lax.dynamic_update_slice(hidden, lone[:, :4].astype(BF16), (0, 2 * width + 1))
        core, far = swap(hidden, "core"), swap(hidden, "cx")
        feed_sums[layer] = (hidden, far, core, swap(far, "core"))
        by_core = (hidden,)

    hidden_grad = from_sequence(grad.astype(BF16)).astype(F32)

    done = None
    columns_of = [None] * LAYERS
    biases = [None] * LAYERS
    for layer in reversed(range(LAYERS)):
        done = finish(info, layer, attn_sums[layer], feed_sums[layer], done)
        columns_of[layer] = done[5]
        biases[layer] = done[4][layer, :, 0]
    lone = feed_sums[0]
    lone = sum(part[:, 2 * width + 1 : 2 * width + 5].astype(F32) for part in lone)
    lone = lone + swap(lone, "tp")
    lone = lone.reshape(units, 2, 2).transpose(1, 2, 0).reshape(2, rows)
    first_gain = jnp.stack((lone[0], columns_of[0][10]))
    first_bias = jnp.stack((lone[1], columns_of[0][11]))
    rest = [jnp.stack((columns_of[0][at], columns_of[1][at])) for at in range(4)]
    qv_out = jnp.stack([jnp.concatenate((columns_of[layer][8], columns_of[layer][9])) for layer in range(LAYERS)])

    return (
        hidden_out,
        hidden_grad,
        first_gain,
        first_bias,
        done[0],
        qv_out,
        done[1],
        rest[2],
        rest[0],
        rest[1],
        done[2],
        jnp.stack(biases),
        done[3],
        rest[3],
    )


def solution(mesh):
    names = tuple(mesh.axis_names)
    shape = dict(mesh.shape)
    split = Mesh(
        mesh.devices.reshape(shape[names[0]], 2, shape[names[1]] // 2, shape[names[2]]),
        ("shard", "cx", "core", "tp"),
    )
    tokens = P("shard", ("cx", "core", "tp"), None)
    vector = P(None, "shard")
    attn = P(None, "shard", None)
    placed = (
        tokens,
        P("shard", None),
        vector,
        vector,
        attn,
        vector,
        attn,
        vector,
        vector,
        vector,
        P(None, None, ("shard", "tp")),
        P(None, ("shard", "tp")),
        P(None, ("shard", "tp"), None),
        vector,
        tokens,
    )
    return jax.shard_map(
        local,
        mesh=split,
        in_specs=placed,
        out_specs=(
            tokens,
            tokens,
            vector,
            vector,
            attn,
            vector,
            attn,
            vector,
            vector,
            vector,
            P(None, None, ("shard", "tp")),
            P(None, ("shard", "tp")),
            P(None, ("shard", "tp"), None),
            vector,
        ),
        check_vma=False,
    )
```

```python
from functools import partial, reduce

import jax
import jax.numpy as jnp
from jax import lax
from jax.experimental import pallas as pl
from jax.experimental.pallas import tpu as pltpu
from jax.sharding import Mesh
from jax.sharding import PartitionSpec as P

HEADS = 12
HEAD = 64
LAYERS = 2
BLK = 256
NEG = -1e30
TILES = 2
EPS = 1e-06
F32 = jnp.float32
BF16 = jnp.bfloat16


def dot(left, right, dims=((1,), (0,))):
    return lax.dot_general(left, right, (dims, ((), ())), preferred_element_type=F32)


def swap(value, axis):
    return lax.ppermute(value, axis, ((0, 1), (1, 0)))


def block_place(block, dev, half):
    return (((block // 2) ^ dev) * 2) + ((block % 2) ^ half)


def doc_range(first, ends, length):
    last = first + BLK - 1
    start, stop = jnp.int32(0), jnp.int32(length)
    for end in ends:
        start = jnp.maximum(start, jnp.where(first >= end, end, 0))
        stop = jnp.minimum(stop, jnp.where(last < end, end, length))
    return start // BLK, (stop + BLK - 1) // BLK


def seg_of(places, ends):
    seg = (places >= ends[0]).astype(jnp.int32)
    for end in ends[1:]:
        seg = seg + (places >= end).astype(jnp.int32)
    return seg


def three_heads(pair, single):
    blank = jnp.zeros_like(single)
    return (
        jnp.concatenate((pair[:HEAD], blank), axis=0),
        jnp.concatenate((blank, pair[HEAD:]), axis=0),
        jnp.concatenate((single, blank), axis=0),
    )


def norm_rows(rows, gain, bias):
    centred = rows - jnp.mean(rows, axis=-1, keepdims=True)
    inv_std = lax.rsqrt(jnp.mean(centred * centred, axis=-1, keepdims=True) + EPS)
    return centred * inv_std * gain + bias


def whole(shape):
    return pl.BlockSpec(shape, lambda *at: (0,) * len(shape))


HBM = pl.BlockSpec(memory_space=pl.ANY)


def attention_forward_kernel(norm, info, *refs):
    parts, (w_ref, bias_ref, gain_ref, shift_ref) = refs[:4], refs[4:8]
    at_out, qkv_out, out_ref, lse_ref, a_ref, at_ref, qkv_ref, v01_t, v2_t, sems, out_sems = refs[8:]
    length = qkv_ref.shape[0]
    ends = (info[0], info[1], info[2])
    dev, half = info[3], info[4]
    each = parts[0].shape[0]
    copies = [pltpu.make_async_copy(part, a_ref.at[at], sems.at[at]) for at, part in enumerate(parts)]
    for copy in copies:
        copy.start()
    for part in range(4):
        copies[part].wait()

        def project(at, nothing):
            rows = pl.ds(pl.multiple_of(at * BLK, BLK), BLK)
            goal = pl.ds(pl.multiple_of(part * each + at * BLK, BLK), BLK)
            values = a_ref[part, rows, :]
            if norm:
                values = norm_rows(values.astype(F32), gain_ref[...], shift_ref[...]).astype(BF16)
            found = dot(values, w_ref[:, 0:576]) + bias_ref[...]
            at_ref[:, goal] = values.T
            qkv_ref[goal, 0:384] = found[:, 0:384].astype(BF16)
            qkv_ref[goal, 384:576] = (found[:, 384:576] * HEAD**-0.5).astype(BF16)
            v01_t[:, goal] = qkv_ref[goal, 256:384].T
            v2_t[:, goal] = qkv_ref[goal, 128:256].T
            return nothing

        lax.fori_loop(0, each // BLK, project, 0)
    out_copies = [
        pltpu.make_async_copy(at_ref, at_out, out_sems.at[0]),
        pltpu.make_async_copy(qkv_ref, qkv_out, out_sems.at[1]),
    ]
    for copy in out_copies:
        copy.start()

    blocks = length // BLK
    lse_ref[...] = jnp.zeros_like(lse_ref)

    def per_block(step, nothing):
        mine = pl.ds(pl.multiple_of(step * BLK, BLK), BLK)
        first = block_place(step, dev, half) * BLK
        seg_q = seg_of(first + lax.broadcasted_iota(jnp.int32, (1, BLK), 1), ends)
        queries = three_heads(qkv_ref[mine, 384:512].T, qkv_ref[mine, 512:576].T)
        low, high = doc_range(first, ends, length)

        def body(pair, carry):
            tiles = []
            for more in range(TILES):
                block = low + TILES * pair + more
                place = block_place(jnp.minimum(block, blocks - 1), dev, half)
                rows = pl.ds(pl.multiple_of(place * BLK, BLK), BLK)
                places = block * BLK + lax.broadcasted_iota(jnp.int32, (BLK, 1), 0)
                tiles.append((rows, seg_of(places, (*ends, length)) == seg_q))

            def score(head):
                lanes = slice(128, 256) if head == 2 else slice(0, 128)
                return [jnp.where(allowed, dot(qkv_ref[rows, lanes], queries[head]), NEG) for rows, allowed in tiles]

            def weigh(head, scores):
                top, total, acc = carry[head]
                new_top = jnp.maximum(top, jnp.max(reduce(jnp.maximum, scores), axis=0, keepdims=True))
                shrink = jnp.exp(top - new_top)
                exps = [jnp.exp(one - new_top) for one in scores]
                total = total * shrink + jnp.sum(reduce(jnp.add, exps), axis=0, keepdims=True)
                return new_top, total, acc * shrink, [exp.astype(BF16) for exp in exps]

            def gather(head, weighed):
                top, total, acc, exps = weighed
                for (rows, _), exp in zip(tiles, exps):
                    values = v2_t[HEAD:128, rows] if head == 2 else v01_t[head * HEAD : (head + 1) * HEAD, rows]
                    acc = acc + dot(values, exp)
                return top, total, acc

            s0 = score(0)
            s1 = score(1)
            w0 = weigh(0, s0)
            s2 = score(2)
            w1 = weigh(1, s1)
            r0 = gather(0, w0)
            w2 = weigh(2, s2)
            r1 = gather(1, w1)
            r2 = gather(2, w2)
            return r0, r1, r2

        start = tuple(
            (
                jnp.full((1, BLK), NEG, F32),
                jnp.zeros((1, BLK), F32),
                jnp.zeros((HEAD, BLK), F32),
            )
            for _ in range(3)
        )
        final = lax.fori_loop(0, (high - low + TILES - 1) // TILES, body, start)
        cols = pl.ds(pl.multiple_of((step % 2) * BLK, BLK), BLK)
        for head in range(3):
            top, total, acc = final[head]
            out_ref[step // 2, head * HEAD : (head + 1) * HEAD, cols] = (acc / total).astype(BF16)
            lse_ref[head : head + 1, mine] = top + jnp.log(total)
        return nothing

    lax.fori_loop(0, blocks, per_block, 0)
    for copy in out_copies:
        copy.wait()


def attention_forward(info, parts, w_qkv, bias, gain, shift, norm):
    each, width = parts[0].shape
    length = 4 * each
    return pl.pallas_call(
        partial(attention_forward_kernel, norm),
        name="attention_forward",
        grid_spec=pltpu.PrefetchScalarGridSpec(
            num_scalar_prefetch=1,
            grid=(1,),
            in_specs=[HBM] * 4 + [whole(w_qkv.shape), whole(bias.shape), whole(gain.shape), whole(shift.shape)],
            out_specs=[HBM, HBM, whole((4, 192, each)), whole((8, length))],
            scratch_shapes=[
                pltpu.VMEM((4, each, width), BF16),
                pltpu.VMEM((width, length), BF16),
                pltpu.VMEM((length, 576), BF16),
                pltpu.VMEM((128, length), BF16),
                pltpu.VMEM((128, length), BF16),
                pltpu.SemaphoreType.DMA((4,)),
                pltpu.SemaphoreType.DMA((2,)),
            ],
        ),
        out_shape=(
            jax.ShapeDtypeStruct((width, length), BF16),
            jax.ShapeDtypeStruct((length, 576), BF16),
            jax.ShapeDtypeStruct((4, 192, each), BF16),
            jax.ShapeDtypeStruct((8, length), F32),
        ),
        compiler_params=pltpu.CompilerParams(vmem_limit_bytes=48 << 20),
        cost_estimate=pl.CostEstimate(
            flops=14 * 10**9, transcendentals=3 * length * 1024, bytes_accessed=12 << 20
        ),
    )(info, *parts, w_qkv, bias, gain, shift)


def attention_backward_kernel(
    info, qkv_ref, out_ref, lse_ref, w_ref, g0, g1, g2, g3,
    du_out, core_out, far_out, own_out, sums_ref,
    q01_t, q2_t, delta, dq_t, grad_t, du_ref, core_ref, far_ref, own_ref, sems,
):
    length = qkv_ref.shape[0]
    each = length // 4
    ends = (info[0], info[1], info[2])
    dev, half = info[3], info[4]
    blocks = length // BLK
    q01_t[...] = qkv_ref[:, 384:512].T
    q2_t[...] = qkv_ref[:, 512:576].T
    dq_t[...] = jnp.zeros_like(dq_t)
    for part, grad in enumerate((g0, g1, g2, g3)):
        grad_t[part] = grad[...]
        for head in range(3):
            rows = slice(head * HEAD, (head + 1) * HEAD)
            both = out_ref[part, rows].astype(F32) * grad[rows].astype(F32)
            delta[head : head + 1, part * each : (part + 1) * each] = jnp.sum(both, axis=0, keepdims=True)

    def per_block(step, nothing):
        mine = pl.ds(pl.multiple_of(step * BLK, BLK), BLK)
        first = block_place(step, dev, half) * BLK
        seg_k = seg_of(first + lax.broadcasted_iota(jnp.int32, (BLK, 1), 0), ends)
        k01 = qkv_ref[mine, 0:128]
        k2v2 = qkv_ref[mine, 128:256]
        v01 = qkv_ref[mine, 256:384]
        k01_t = k01.T
        k2_t = k2v2.T[:HEAD]
        keys_t = (k01_t[:HEAD], k01_t[HEAD:], k2_t)
        low, high = doc_range(first, ends, length)

        def body(pair, carry):
            blank = jnp.zeros((HEAD, BLK), BF16)
            tiles = []
            for more in range(TILES):
                block = low + TILES * pair + more
                place = block_place(jnp.minimum(block, blocks - 1), dev, half)
                cols = pl.ds(pl.multiple_of(place * BLK, BLK), BLK)
                part_cols = pl.ds(pl.multiple_of((place % 2) * BLK, BLK), BLK)
                places = block * BLK + lax.broadcasted_iota(jnp.int32, (1, BLK), 1)
                allowed = seg_k == seg_of(places, (*ends, length))
                queries = three_heads(q01_t[:, cols], q2_t[:, cols])
                grads = grad_t[place // 2, :, part_cols]
                dos = (
                    jnp.concatenate((grads[:HEAD], blank), axis=0),
                    jnp.concatenate((blank, grads[HEAD:128]), axis=0),
                    jnp.concatenate((blank, grads[128:192]), axis=0),
                )
                tiles.append((cols, allowed, queries, dos))

            def first_dots(at):
                cols, allowed, queries, dos = tiles[at // 3]
                head = at % 3
                return (
                    dot(k2v2 if head == 2 else k01, queries[head]),
                    dot(k2v2 if head == 2 else v01, dos[head]),
                )

            def weigh(at, found):
                cols, allowed, queries, dos = tiles[at // 3]
                head = at % 3
                scores, grad_probs = found
                probs = jnp.where(allowed, jnp.exp(scores - lse_ref[head : head + 1, cols]), 0.0)
                grad_scores = (probs * (grad_probs - delta[head : head + 1, cols])).astype(BF16)
                return probs.astype(BF16), grad_scores

            def last_dots(at, found, sums):
                cols, allowed, queries, dos = tiles[at // 3]
                head = at % 3
                probs, grad_scores = found
                more_k = dot(grad_scores, queries[head], ((1,), (1,)))
                more_v = dot(probs, dos[head], ((1,), (1,)))
                more_q = dot(keys_t[head], grad_scores)
                dk01, dk2v2, dv01 = sums
                if head == 2:
                    dk2v2 = dk2v2 + more_k + more_v
                else:
                    dk01 = dk01 + more_k
                    dv01 = dv01 + more_v
                return (dk01, dk2v2, dv01), more_q

            count = 3 * TILES
            sums = carry
            more_q = []
            begun = {0: first_dots(0), 1: first_dots(1)}
            weighed = {}
            for at in range(count):
                if at + 2 < count:
                    begun[at + 2] = first_dots(at + 2)
                weighed[at] = weigh(at, begun[at])
                if at > 0:
                    sums, found = last_dots(at - 1, weighed[at - 1], sums)
                    more_q.append(found)
            sums, found = last_dots(count - 1, weighed[count - 1], sums)
            more_q.append(found)
            for tile in range(TILES):
                cols = tiles[tile][0]
                dq_t[:, cols] = dq_t[:, cols] + jnp.concatenate(more_q[3 * tile : 3 * tile + 3], axis=0)
            return sums

        zero = jnp.zeros((BLK, 128), F32)
        dk01, dk2v2, dv01 = lax.fori_loop(0, (high - low + TILES - 1) // TILES, body, (zero, zero, zero))
        du_ref[mine, 0:128] = dk01.astype(BF16)
        du_ref[mine, 128:256] = dk2v2.astype(BF16)
        du_ref[mine, 256:384] = dv01.astype(BF16)
        return nothing

    lax.fori_loop(0, blocks, per_block, 0)
    sums_ref[...] = jnp.zeros_like(sums_ref)
    scale = HEAD**-0.5

    def finish_rows(at, total):
        rows = pl.ds(pl.multiple_of(at * BLK, BLK), BLK)
        du_ref[rows, 384:512] = (dq_t[0:128, rows] * scale).T.astype(BF16)
        du_ref[rows, 512:576] = (dq_t[128:192, rows] * scale).T.astype(BF16)
        return total + jnp.sum(du_ref[rows, :].astype(F32), axis=0, keepdims=True)

    sums_ref[0:1, :] = lax.fori_loop(0, blocks, finish_rows, jnp.zeros((1, 576), F32))
    copies = [pltpu.make_async_copy(du_ref, du_out, sems.at[0])]
    copies[0].start()
    plan = ((1, core_ref.at[0], core_out.at[0]), (3, core_ref.at[1], core_out.at[1]), (2, far_ref, far_out), (0, own_ref, own_out))
    for at, (part, target, goal) in enumerate(plan):
        kind = target.dtype
        target[...] = dot(du_ref[part * each : (part + 1) * each, :], w_ref[:, 0:576], ((1,), (1,))).astype(kind)
        copies.append(pltpu.make_async_copy(target, goal, sems.at[at + 1]))
        copies[-1].start()
    for copy in copies:
        copy.wait()


def attention_backward(info, qkv, out, lse, w_qkv, grads):
    length, each, width = qkv.shape[0], qkv.shape[0] // 4, w_qkv.shape[0]
    return pl.pallas_call(
        attention_backward_kernel,
        name="attention_backward",
        grid_spec=pltpu.PrefetchScalarGridSpec(
            num_scalar_prefetch=1,
            grid=(1,),
            in_specs=[whole(qkv.shape), whole(out.shape), whole(lse.shape), whole(w_qkv.shape)]
            + [whole((192, each))] * 4,
            out_specs=[HBM, HBM, HBM, HBM, whole((8, 576))],
            scratch_shapes=[
                pltpu.VMEM((128, length), BF16),
                pltpu.VMEM((64, length), BF16),
                pltpu.VMEM((8, length), F32),
                pltpu.VMEM((192, length), F32),
                pltpu.VMEM((4, 192, each), BF16),
                pltpu.VMEM((length, 576), BF16),
                pltpu.VMEM((2, each, width), BF16),
                pltpu.VMEM((each, width), F32),
                pltpu.VMEM((each, width), F32),
                pltpu.SemaphoreType.DMA((5,)),
            ],
        ),
        out_shape=(
            jax.ShapeDtypeStruct(qkv.shape, BF16),
            jax.ShapeDtypeStruct((2, each, width), BF16),
            jax.ShapeDtypeStruct((each, width), F32),
            jax.ShapeDtypeStruct((each, width), F32),
            jax.ShapeDtypeStruct((8, 576), F32),
        ),
        compiler_params=pltpu.CompilerParams(vmem_limit_bytes=56 << 20),
        cost_estimate=pl.CostEstimate(
            flops=20 * 10**9, transcendentals=3 * length * 1024, bytes_accessed=16 << 20
        ),
    )(info, qkv, out, lse, w_qkv, *grads)


def attention_weights_kernel(at_ref, du_ref, vec_ref, own_ref, core_ref, far_ref, out_ref, spread):
    blank = jnp.zeros((128 - vec_ref.shape[0], vec_ref.shape[1]), F32)
    out_ref[:, 768:896] = jnp.concatenate((vec_ref[...], blank), axis=0).T.astype(BF16)
    out_ref[:, 0:576] = dot(at_ref[...], du_ref[...]).astype(BF16)
    total = own_ref[...].astype(F32) + core_ref[...].astype(F32) + far_ref[...].astype(F32)
    quarter = own_ref.shape[0]
    for piece in range(4):
        rows = pl.ds(piece, quarter, stride=4)
        spread[0, rows, :] = total[:, piece * 192 : piece * 192 + 128]
        spread[1, rows, :] = jnp.concatenate(
            (total[:, piece * 192 + 128 : (piece + 1) * 192], jnp.zeros((quarter, 64), F32)), axis=1
        )
    out_ref[:, 576:704] = spread[0].astype(BF16)
    out_ref[:, 704:768] = spread[1, :, 0:64].astype(BF16)


def attention_weights(a_t, du, vectors, own, core, far):
    width = a_t.shape[0]
    return pl.pallas_call(
        attention_weights_kernel,
        name="attention_weights",
        grid=(1,),
        in_specs=[whole(v.shape) for v in (a_t, du, vectors, own, core, far)],
        out_specs=whole((width, width + 128)),
        out_shape=jax.ShapeDtypeStruct((width, width + 128), BF16),
        scratch_shapes=[pltpu.VMEM((2, width, 128), F32)],
        compiler_params=pltpu.CompilerParams(vmem_limit_bytes=48 << 20),
        cost_estimate=pl.CostEstimate(flops=18 * 10**8, transcendentals=0, bytes_accessed=8 << 20),
    )(a_t, du, vectors, own, core, far)


def out_kernel(info, p0, p1, p2, p3, w_ref, x_ref, vec_ref, ctx_ref, mid_ref, c_ref, ctx):
    dev = info[3]
    loc, toks = p0.shape
    for rel, part in enumerate((p0, p1, p2, p3)):
        ctx[dev ^ rel] = part[...]
    ctx_ref[...] = ctx[...].reshape(4 * loc, toks)

    def rows_of(at, nothing):
        rows = pl.ds(pl.multiple_of(at * 128, 128), 128)
        found = dot(ctx_ref[:, rows].T, w_ref[...])
        middle = x_ref[rows, :] + found + vec_ref[0:1, :]
        mid_ref[rows, :] = middle
        c_ref[rows, :] = norm_rows(middle, vec_ref[1:2, :], vec_ref[2:3, :]).astype(BF16)
        return nothing

    lax.fori_loop(0, toks // 128, rows_of, 0)


def out_forward(info, parts, w_out, current, vectors):
    loc, toks = parts[0].shape
    width = w_out.shape[1]
    return pl.pallas_call(
        out_kernel,
        name="out_forward",
        grid_spec=pltpu.PrefetchScalarGridSpec(
            num_scalar_prefetch=1,
            grid=(1,),
            in_specs=[whole((loc, toks))] * 4 + [whole(w_out.shape), whole(current.shape), whole(vectors.shape)],
            out_specs=[whole((width, toks)), whole((toks, width)), whole((toks, width))],
            scratch_shapes=[pltpu.VMEM((4, loc, toks), BF16)],
        ),
        out_shape=(
            jax.ShapeDtypeStruct((width, toks), BF16),
            jax.ShapeDtypeStruct((toks, width), F32),
            jax.ShapeDtypeStruct((toks, width), BF16),
        ),
        compiler_params=pltpu.CompilerParams(vmem_limit_bytes=48 << 20),
        cost_estimate=pl.CostEstimate(flops=10**9, transcendentals=0, bytes_accessed=7 << 20),
    )(info, *parts, w_out, current, vectors)


def norm_back(grad, values, gain):
    centred = values - jnp.mean(values, axis=-1, keepdims=True)
    inv_std = lax.rsqrt(jnp.mean(centred * centred, axis=-1, keepdims=True) + EPS)
    normed = centred * inv_std
    scaled = grad * gain
    grad_in = inv_std * (
        scaled
        - jnp.mean(scaled, axis=-1, keepdims=True)
        - normed * jnp.mean(scaled * normed, axis=-1, keepdims=True)
    )
    return grad_in, jnp.sum(grad * normed, axis=0, keepdims=True), jnp.sum(grad, axis=0, keepdims=True)


def norm_back_kernel(own, core, far, x_ref, gain_ref, mid_ref, grad_ref, low_ref, sums_ref):
    toks, width = x_ref.shape
    step = pl.program_id(0)

    @pl.when(step == 0)
    def _():
        sums_ref[...] = jnp.zeros_like(sums_ref)

    def rows_of(at, sums):
        rows = pl.ds(pl.multiple_of(at * 64, 64), 64)
        found = own[rows, :] + core[0, rows, :].astype(F32) + far[rows, :].astype(F32)
        grad_in, gain_sum, bias_sum = norm_back(found, x_ref[rows, :], gain_ref[...])
        grad = mid_ref[rows, :] + grad_in
        grad_ref[rows, :] = grad
        low_ref[rows, :] = grad.astype(BF16)
        return sums[0] + gain_sum, sums[1] + bias_sum

    zero = jnp.zeros((1, width), F32)
    sums = lax.fori_loop(0, toks // 64, rows_of, (zero, zero))
    sums_ref[0:1, :] += sums[0]
    sums_ref[1:2, :] += sums[1]


def norm_backward(own, core, far, values, gain, middle_grad):
    toks, width = values.shape
    rows = pl.BlockSpec((toks // 4, width), lambda i: (i, 0))
    return pl.pallas_call(
        norm_back_kernel,
        name="norm_backward",
        grid=(4,),
        in_specs=[rows, pl.BlockSpec((1, toks // 4, width), lambda i: (0, i, 0)), rows, rows, whole(gain.shape), rows],
        out_specs=[rows, rows, whole((8, width))],
        out_shape=(
            jax.ShapeDtypeStruct((toks, width), F32),
            jax.ShapeDtypeStruct((toks, width), BF16),
            jax.ShapeDtypeStruct((8, width), F32),
        ),
        compiler_params=pltpu.CompilerParams(vmem_limit_bytes=48 << 20),
        cost_estimate=pl.CostEstimate(flops=10**7, transcendentals=0, bytes_accessed=9 << 20),
    )(own, core, far, values, gain, middle_grad)


GELU_A = (2.0 / 3.141592653589793) ** 0.5
GELU_B = 0.044715


def gelu(t):
    square = t * t
    tanh = jnp.tanh(t * (GELU_A + GELU_A * GELU_B * square))
    half = 0.5 * t
    side = 0.5 + 0.5 * tanh
    slope = side + (half - half * tanh * tanh) * (GELU_A + 3.0 * GELU_A * GELU_B * square)
    return t * side, slope


def fetch(parts, held, sems):
    units = parts[0].shape[0]
    copies = [
        pltpu.make_async_copy(part, held.at[at // 2, pl.ds((at % 2) * units, units)], sems.at[at])
        for at, part in enumerate(parts)
    ]
    for copy in copies:
        copy.start()
    return copies


def feed_kernel(c_ref, mid_ref, vec_ref, *refs):
    parts, refs = refs[:8], refs[8:]
    slope_out, own_out, other_out, x_ref, a_ref, slope_ref, act_ref, held, sems, out_sems = refs
    toks, width = mid_ref.shape
    copies = fetch(parts, held, sems)
    x_ref[...] = mid_ref[...] + vec_ref[0:1, :]
    outs = []

    def before(at):
        copies[2 * at].wait()
        copies[2 * at + 1].wait()
        bias = held[at, :, 2 * width : 2 * width + 128].T[0:1].astype(F32)
        return dot(c_ref[...], held[at, :, 0:width], ((1,), (1,))) + bias

    def after(at, pre):
        act, slope = gelu(pre)
        act = act.astype(BF16)
        slope_ref[at] = slope.astype(BF16)
        act_ref[at] = act.T
        outs.append(pltpu.make_async_copy(slope_ref.at[at], slope_out.at[at], out_sems.at[2 * at]))
        goal = (own_out, other_out)[at // 2].at[at % 2]
        outs.append(pltpu.make_async_copy(act_ref.at[at], goal, out_sems.at[2 * at + 1]))
        outs[-2].start()
        outs[-1].start()
        x_ref[...] += dot(act, held[at, :, width : 2 * width])

    pre = before(0)
    for at in range(4):
        later = before(at + 1) if at < 3 else None
        after(at, pre)
        pre = later

    def rows_of(at, nothing):
        rows = pl.ds(pl.multiple_of(at * 64, 64), 64)
        a_ref[rows, :] = norm_rows(x_ref[rows, :], vec_ref[1:2, :], vec_ref[2:3, :]).astype(BF16)
        return nothing

    lax.fori_loop(0, toks // 64, rows_of, 0)
    for copy in outs:
        copy.wait()


def feed_forward(c, middle, vectors, parts):
    toks, width = middle.shape
    units = 2 * parts[0].shape[0]
    return pl.pallas_call(
        feed_kernel,
        name="feed_forward",
        grid=(1,),
        in_specs=[whole(c.shape), whole(middle.shape), whole(vectors.shape)] + [HBM] * 8,
        out_specs=[HBM, HBM, HBM, whole((toks, width)), whole((toks, width))],
        out_shape=[
            jax.ShapeDtypeStruct((4, toks, units), BF16),
            jax.ShapeDtypeStruct((2, units, toks), BF16),
            jax.ShapeDtypeStruct((2, units, toks), BF16),
            jax.ShapeDtypeStruct((toks, width), F32),
            jax.ShapeDtypeStruct((toks, width), BF16),
        ],
        scratch_shapes=[
            pltpu.VMEM((4, toks, units), BF16),
            pltpu.VMEM((4, units, toks), BF16),
            pltpu.VMEM((4, units, parts[0].shape[1]), BF16),
            pltpu.SemaphoreType.DMA((8,)),
            pltpu.SemaphoreType.DMA((8,)),
        ],
        compiler_params=pltpu.CompilerParams(vmem_limit_bytes=56 << 20),
        cost_estimate=pl.CostEstimate(flops=5 * 10**9, transcendentals=2 * 10**6, bytes_accessed=20 << 20),
    )(c, middle, vectors, *parts)


def finish_back(dev, grad_ref, mid_ref, gain_ref, w_ref, dm_ref, dc, dmid_ref, da_ref, sums_ref, targets):
    toks, width = mid_ref.shape
    loc = targets[0].shape[0]

    def rows_of(at, sums):
        rows = pl.ds(pl.multiple_of(at * 64, 64), 64)
        grad_in, gain_sum, bias_sum = norm_back(dc[rows, :], mid_ref[rows, :], gain_ref[...])
        grad_mid = grad_ref[rows, :] + grad_in
        dmid_ref[rows, :] = grad_mid
        branch = grad_mid.astype(BF16)
        da_ref[rows, :] = branch
        out_sum = jnp.sum(branch.astype(F32), axis=0, keepdims=True)
        down_sum = jnp.sum(dm_ref[rows, :].astype(F32), axis=0, keepdims=True)
        return sums[0] + gain_sum, sums[1] + bias_sum, sums[2] + out_sum, sums[3] + down_sum

    zero = jnp.zeros((1, width), F32)
    sums = lax.fori_loop(0, toks // 64, rows_of, (zero,) * 4)
    sums_ref[...] = jnp.zeros_like(sums_ref)
    for at in range(4):
        sums_ref[at : at + 1, :] = sums[at]
    for rel, target in enumerate(targets):
        rows = pl.ds(pl.multiple_of((dev ^ rel) * loc, 64), loc)
        target[...] = dot(w_ref[rows, :], da_ref[...], ((1,), (1,))).astype(BF16)


def back_outputs(toks, width, units):
    return [
        jax.ShapeDtypeStruct((2, toks, units), BF16),
        jax.ShapeDtypeStruct((2, toks, units), BF16),
        jax.ShapeDtypeStruct((toks, width), F32),
        jax.ShapeDtypeStruct((toks, width), BF16),
        jax.ShapeDtypeStruct((8, width), F32),
    ] + [jax.ShapeDtypeStruct((width // 4, toks), BF16)] * 4


def feed_back_kernel(info, grad_ref, dm_ref, slope_in, mid_in, gain_ref, w_in, *refs):
    parts, refs = refs[:8], refs[8:]
    own_out, other_out, dmid_ref, da_ref, sums_ref, *targets = refs[:9]
    slope_ref, dh_ref, held, dc, mid_ref, w_ref, sems, slope_sems, out_sems, in_sems = refs[9:]
    width = mid_ref.shape[1]
    copies = fetch(parts, held, sems)
    slopes = [pltpu.make_async_copy(slope_in.at[at], slope_ref.at[at], slope_sems.at[at]) for at in range(4)]
    late_in = [pltpu.make_async_copy(mid_in, mid_ref, in_sems.at[0]), pltpu.make_async_copy(w_in, w_ref, in_sems.at[1])]
    for copy in slopes + late_in:
        copy.start()
    outs = []
    goals = (own_out.at[0], own_out.at[1], other_out.at[0], other_out.at[1])

    def before(at):
        copies[2 * at].wait()
        copies[2 * at + 1].wait()
        return dot(dm_ref[...], held[at, :, width : 2 * width], ((1,), (1,)))

    def after(at, dact):
        slopes[at].wait()
        dpre = (dact * slope_ref[at].astype(F32)).astype(BF16)
        dh_ref[at] = dpre
        outs.append(pltpu.make_async_copy(dh_ref.at[at], goals[at], out_sems.at[at]))
        outs[-1].start()
        term = dot(dpre, held[at, :, 0:width])
        if at == 0:
            dc[...] = term
        else:
            dc[...] += term

    dact = before(0)
    for at in range(4):
        later = before(at + 1) if at < 3 else None
        after(at, dact)
        dact = later
    for copy in late_in:
        copy.wait()
    finish_back(info[3], grad_ref, mid_ref, gain_ref, w_ref, dm_ref, dc, dmid_ref, da_ref, sums_ref, targets)
    for copy in outs:
        copy.wait()


def feed_backward(info, grad, dm, slope, middle, gain, w_out, parts):
    toks, width = middle.shape
    units = 2 * parts[0].shape[0]
    shapes = back_outputs(toks, width, units)
    return pl.pallas_call(
        feed_back_kernel,
        name="feed_backward",
        grid_spec=pltpu.PrefetchScalarGridSpec(
            num_scalar_prefetch=1,
            grid=(1,),
            in_specs=[whole(grad.shape), whole(dm.shape), HBM, HBM, whole(gain.shape), HBM] + [HBM] * 8,
            out_specs=[HBM] * 2 + [whole(shape.shape) for shape in shapes[2:]],
            scratch_shapes=[
                pltpu.VMEM((4, toks, units), BF16),
                pltpu.VMEM((4, toks, units), BF16),
                pltpu.VMEM((4, units, parts[0].shape[1]), BF16),
                pltpu.VMEM((toks, width), F32),
                pltpu.VMEM((toks, width), F32),
                pltpu.VMEM((width, width), BF16),
                pltpu.SemaphoreType.DMA((8,)),
                pltpu.SemaphoreType.DMA((4,)),
                pltpu.SemaphoreType.DMA((4,)),
                pltpu.SemaphoreType.DMA((2,)),
            ],
        ),
        out_shape=shapes,
        compiler_params=pltpu.CompilerParams(vmem_limit_bytes=60 << 20),
        cost_estimate=pl.CostEstimate(flops=6 * 10**9, transcendentals=2 * 10**6, bytes_accessed=24 << 20),
    )(info, grad, dm, slope, middle, gain, w_out, *parts)


def feed_both_kernel(info, c_ref, grad_ref, dm_ref, mid_ref, vec_ref, w_in, *refs):
    parts, refs = refs[:8], refs[8:]
    own_out, other_out, dmid_ref, da_ref, sums_ref, *targets = refs[:9]
    act_own, act_other, x_ref = refs[9:12]
    act_ref, dh_ref, held, dc, w_ref, sems, out_sems, in_sem = refs[12:]
    toks, width = mid_ref.shape
    copies = fetch(parts, held, sems)
    late_in = pltpu.make_async_copy(w_in, w_ref, in_sem.at[0])
    late_in.start()
    x_ref[...] = mid_ref[...] + vec_ref[0:1, :]
    outs = []
    goals = (own_out.at[0], own_out.at[1], other_out.at[0], other_out.at[1])

    def before(at):
        copies[2 * at].wait()
        copies[2 * at + 1].wait()
        bias = held[at, :, 2 * width : 2 * width + 128].T[0:1].astype(F32)
        pre = dot(c_ref[...], held[at, :, 0:width], ((1,), (1,))) + bias
        return pre, dot(dm_ref[...], held[at, :, width : 2 * width], ((1,), (1,)))

    def after(at, found):
        pre, dact = found
        act, slope = gelu(pre)
        act = act.astype(BF16)
        act_ref[at] = act.T
        dpre = (dact * slope).astype(BF16)
        dh_ref[at] = dpre
        goal = (act_own, act_other)[at // 2].at[at % 2]
        outs.append(pltpu.make_async_copy(dh_ref.at[at], goals[at], out_sems.at[2 * at]))
        outs.append(pltpu.make_async_copy(act_ref.at[at], goal, out_sems.at[2 * at + 1]))
        outs[-2].start()
        outs[-1].start()
        x_ref[...] += dot(act, held[at, :, width : 2 * width])
        term = dot(dpre, held[at, :, 0:width])
        if at == 0:
            dc[...] = term
        else:
            dc[...] += term

    found = before(0)
    for at in range(4):
        later = before(at + 1) if at < 3 else None
        after(at, found)
        found = later
    late_in.wait()
    finish_back(info[3], grad_ref, mid_ref, vec_ref.at[1:2], w_ref, dm_ref, dc, dmid_ref, da_ref, sums_ref, targets)
    for copy in outs:
        copy.wait()


def feed_both(info, c, grad, dm, middle, vectors, w_out, parts):
    toks, width = middle.shape
    units = 2 * parts[0].shape[0]
    shapes = back_outputs(toks, width, units) + [
        jax.ShapeDtypeStruct((2, units, toks), BF16),
        jax.ShapeDtypeStruct((2, units, toks), BF16),
        jax.ShapeDtypeStruct((toks, width), F32),
    ]
    return pl.pallas_call(
        feed_both_kernel,
        name="feed_both",
        grid_spec=pltpu.PrefetchScalarGridSpec(
            num_scalar_prefetch=1,
            grid=(1,),
            in_specs=[whole(v.shape) for v in (c, grad, dm, middle, vectors)] + [HBM] * 9,
            out_specs=[HBM] * 2 + [whole(shape.shape) for shape in shapes[2:9]] + [HBM, HBM, whole((toks, width))],
            scratch_shapes=[
                pltpu.VMEM((4, units, toks), BF16),
                pltpu.VMEM((4, toks, units), BF16),
                pltpu.VMEM((4, units, parts[0].shape[1]), BF16),
                pltpu.VMEM((toks, width), F32),
                pltpu.VMEM((width, width), BF16),
                pltpu.SemaphoreType.DMA((8,)),
                pltpu.SemaphoreType.DMA((8,)),
                pltpu.SemaphoreType.DMA((1,)),
            ],
        ),
        out_shape=shapes,
        compiler_params=pltpu.CompilerParams(vmem_limit_bytes=60 << 20),
        cost_estimate=pl.CostEstimate(flops=10**10, transcendentals=2 * 10**6, bytes_accessed=24 << 20),
    )(info, c, grad, dm, middle, vectors, w_out, *parts)


def feed_weights_kernel(dh, dh2, act, act2, c, c2, dm, dm2, out_ref):
    width = c.shape[1]
    one, two = dh[0].T, dh2[0].T
    out_ref[:, 0:width] = (dot(one, c[...]) + dot(two, c2[...])).astype(BF16)
    out_ref[:, width : 2 * width] = (dot(act[0], dm[...]) + dot(act2[0], dm2[...])).astype(BF16)
    bias = jnp.sum(one.astype(F32), axis=1, keepdims=True) + jnp.sum(two.astype(F32), axis=1, keepdims=True)
    out_ref[:, 2 * width :] = jnp.broadcast_to(bias, (bias.shape[0], 128)).astype(BF16)


def feed_weights(half, dh, dh2, act, act2, c, c2, dm, dm2):
    toks, units, width = dh.shape[1], dh.shape[2], c.shape[1]
    wide = 2 * width + 128
    step = 256
    act_spec = pl.BlockSpec((1, step, toks), lambda i: (half, i, 0))
    return pl.pallas_call(
        feed_weights_kernel,
        name="feed_weights",
        grid=(units // step,),
        in_specs=[
            pl.BlockSpec((1, toks, step), lambda i: (half, 0, i)),
            pl.BlockSpec((1, toks, step), lambda i: (half, 0, i)),
            act_spec,
            act_spec,
        ]
        + [pl.BlockSpec(v.shape, lambda i: (0, 0)) for v in (c, c2, dm, dm2)],
        out_specs=pl.BlockSpec((step, wide), lambda i: (i, 0)),
        out_shape=jax.ShapeDtypeStruct((units, wide), BF16),
        compiler_params=pltpu.CompilerParams(vmem_limit_bytes=48 << 20),
        cost_estimate=pl.CostEstimate(flops=24 * 10**8, transcendentals=0, bytes_accessed=9 << 20),
    )(dh, dh2, act, act2, c, c2, dm, dm2)


def finish_kernel(last, info, *refs):
    attn, hidden, refs = refs[:4], refs[4:8], refs[8:]
    if last:
        (other_vec, other_bias), refs = refs[:2], refs[6:]
        qkv_ref, out_ref, up_ref, down_ref = refs[:4]
        vectors_out, qv_out, bias_out = refs[4:10], refs[10], refs[11]
        qkv_at, out_at, hid_at = refs[12:]
    else:
        qkv_ref, out_ref, up_ref, down_ref, vec_ref, bias_ref, qkv_at, out_at, hid_at = refs
    dev = info[3]
    spot = info[5]
    rows = attn[0].shape[0]
    loc = 192
    for rel in range(4):
        qkv_at[dev ^ rel] = attn[rel][:, 0:576].astype(F32)
        out_at[dev ^ rel, 0] = attn[rel][:, 576:704].astype(F32)
        out_at[dev ^ rel, 1, :, 0:64] = attn[rel][:, 704:768].astype(F32)
        hid_at[spot ^ rel] = hidden[rel][...].astype(F32)
    width = 4 * loc
    quarter = rows // 4
    units = hidden[0].shape[0]
    for at in range(4):
        found = qkv_at[at]
        qkv_ref[0, :, at * loc : (at + 1) * loc] = found[:, 384:576]
        qkv_ref[0, :, width + at * loc : width + (at + 1) * loc] = found[:, 0:192]
        v_at = 2 * width + at * loc
        qkv_ref[0, :, v_at : v_at + 128] = found[:, 256:384]
        qkv_ref[0, :, v_at + 128 : v_at + 192] = found[:, 192:256]
        for piece in range(4):
            goal = slice(at * quarter, (at + 1) * quarter)
            lane = piece * loc
            out_ref[0, goal, lane : lane + 128] = out_at[at, 0, pl.ds(piece, quarter, stride=4), :]
            out_ref[0, goal, lane + 128 : lane + 192] = out_at[at, 1, pl.ds(piece, quarter, stride=4), :][:, 0:64]
        down_ref[0, at * units : (at + 1) * units, :] = hid_at[at, :, width : 2 * width]
    up = jnp.concatenate([hid_at[at, :, 0:width] for at in range(4)], axis=0)
    up_ref[0] = up.T
    bias = jnp.concatenate([hid_at[at, :, 2 * width :] for at in range(4)], axis=0).T[0:8]
    vectors = sum(part[:, 768:896].astype(F32) for part in attn).T[0:16]
    if not last:
        vec_ref[...] = vectors
        bias_ref[...] = bias
        return
    bias_out[0:1, :] = bias[0:1]
    bias_out[1:2, :] = other_bias[0:1, :]
    order = (((12, 0), (10, 0)), ((13, 0), (11, 0)), ((0, 0), (0, 1)), ((1, 0), (1, 1)), ((2, 0), (2, 1)), ((3, 0), (3, 1)))
    for target, picks in zip(vectors_out, order):
        for layer, (row, from_other) in enumerate(picks):
            source = other_vec[row : row + 1, :] if from_other else vectors[row : row + 1]
            target[layer : layer + 1, :] = source
    for half in range(2):
        lanes = slice(half * rows, (half + 1) * rows)
        qv_out[0:1, lanes] = vectors[8 + half : 9 + half]
        qv_out[1:2, lanes] = other_vec[8 + half : 9 + half, :]


def finish(info, layer, attn, hidden, before):
    rows, width = attn[0].shape[0], attn[0].shape[1] - 128
    units = hidden[0].shape[0]
    shapes = [
        (LAYERS, rows, 3 * width),
        (LAYERS, rows, width),
        (LAYERS, width, 4 * units),
        (LAYERS, 4 * units, width),
    ]
    specs = [pl.BlockSpec((1, *shape[1:]), lambda i, info: (layer, 0, 0)) for shape in shapes]
    last = before is not None
    more = [(LAYERS, rows)] * 6 + [(LAYERS, 2 * rows), (LAYERS, 4 * units)] if last else [(16, rows), (8, 4 * units)]
    given = [*before[4:6], *before[:4]] if last else []
    return pl.pallas_call(
        partial(finish_kernel, last),
        name="finish",
        grid_spec=pltpu.PrefetchScalarGridSpec(
            num_scalar_prefetch=1,
            grid=(1,),
            in_specs=[whole(attn[0].shape)] * 4
            + [whole(hidden[0].shape)] * 4
            + ([whole(v.shape) for v in given[:2]] + [HBM] * 4 if last else []),
            out_specs=specs + [whole(shape) for shape in more],
            scratch_shapes=[
                pltpu.VMEM((4, rows, 576), F32),
                pltpu.VMEM((4, 2, rows, 128), F32),
                pltpu.VMEM((4, units, 2 * width + 128), F32),
            ],
        ),
        out_shape=[jax.ShapeDtypeStruct(shape, F32) for shape in shapes + more],
        input_output_aliases={11 + at: at for at in range(4)} if last else {},
        compiler_params=pltpu.CompilerParams(vmem_limit_bytes=56 << 20),
        cost_estimate=pl.CostEstimate(flops=10**6, transcendentals=0, bytes_accessed=8 << 20),
    )(info, *attn, *hidden, *given)


PLANE = ("cx", "core", "tp")


def turned(value, first):
    pairs = []
    for x in range(2):
        for core in range(2):
            for y in range(2):
                flip_x = (core == 0) == first
                target = ((1 - x) if flip_x else x, core, y if flip_x else 1 - y)
                pairs.append((x * 4 + core * 2 + y, target[0] * 4 + target[1] * 2 + target[2]))
    return lax.ppermute(value, PLANE, pairs)


def after(value, *others):
    return lax.optimization_barrier((value, *others))[0]


def diagonal(value):
    return lax.ppermute(value, ("cx", "core"), ((0, 3), (1, 2), (2, 1), (3, 0)))


def around(own):
    far = swap(own, "cx")
    return own, swap(own, "core"), far, swap(far, "core")


def local(
    hidden_in,
    doc_lengths,
    ln1_gain,
    ln1_bias,
    qkv_weight,
    qv_bias,
    out_weight,
    out_bias,
    ln2_gain,
    ln2_bias,
    up_weight,
    up_bias,
    down_weight,
    down_bias,
    output_grad,
):
    shards = lax.axis_size("shard")
    ix, ic, iy = lax.axis_index("cx"), lax.axis_index("core"), lax.axis_index("tp")
    dev = ix * 2 + ic
    seqs, toks, width = hidden_in.shape
    rows = ln1_gain.shape[1]
    units = up_bias.shape[1] // 4
    loc = width // 4
    quarter = rows // 4

    def to_sequence(tokens):
        own = lax.dynamic_index_in_dim(tokens, iy, 0, keepdims=False)
        other = lax.dynamic_index_in_dim(tokens, 1 - iy, 0, keepdims=False)
        return jnp.concatenate((own, swap(other, "tp")), axis=0)

    def from_sequence(tokens):
        own, other = tokens[:toks], swap(tokens[toks:], "tp")
        return jnp.where(iy == 0, jnp.stack((own, other)), jnp.stack((other, own)))

    lengths = lax.dynamic_index_in_dim(doc_lengths, iy, 0, keepdims=False)
    end0 = lengths[0]
    end1 = end0 + lengths[1]
    end2 = end1 + lengths[2]
    info = jnp.stack((end0, end1, end2, dev, iy, ic * 2 + ix, dev, dev)).astype(jnp.int32)
    row_ids = jnp.arange(2 * toks, dtype=jnp.int32)
    places = dev * (2 * toks) + ((row_ids // toks) ^ iy) * toks + row_ids % toks
    keep = (places < end2).astype(F32)[:, None]

    def columns(array, start):
        return lax.dynamic_slice_in_dim(array, start, loc, 1)

    small = jnp.concatenate(
        [ln1_gain, ln1_bias, out_bias, ln2_gain, ln2_bias, down_bias, qv_bias.reshape(2 * LAYERS, rows)], axis=0
    )
    small = jnp.pad(small, ((0, 128 - small.shape[0]), (0, 0))).T

    def attention_piece(layer):
        weight = qkv_weight[layer]
        q, k, v = (columns(weight, which * width + loc * dev) for which in range(3))
        out = lax.dynamic_slice_in_dim(out_weight[layer], quarter * dev, quarter, 0).reshape(rows, loc)
        pieces = [k[:, :128], k[:, 128:], v[:, 128:], v[:, :128], q, out]
        if layer == 0:
            pieces.append(small)
        return jnp.concatenate(pieces, axis=1)

    def hidden_piece(layer):
        start = ic * 2 * units + ix * units
        up = lax.dynamic_slice_in_dim(up_weight[layer], start, units, 1).T
        down = lax.dynamic_slice_in_dim(down_weight[layer], start, units, 0)
        bias = lax.dynamic_slice_in_dim(up_bias[layer], start, units, 0)
        bias = jnp.broadcast_to(bias[:, None], (units, 128))
        return jnp.concatenate((up, down, bias), axis=1)

    def over_shards(piece):
        return lax.all_gather(piece, "shard", axis=0, tiled=True)

    def send_shards(value, count):
        if shards != 4:
            return ()
        index = lax.axis_index("shard")
        return tuple(
            lax.ppermute(
                lax.dynamic_slice_in_dim(value, (index + by) % shards * count, count, 0),
                "shard",
                [(i, (i + by) % shards) for i in range(shards)],
            )
            for by in range(1, shards)
        )

    def sum_shards(value, count, arriving):
        if shards != 4:
            return lax.psum_scatter(value, "shard", scatter_dimension=0, tiled=True)
        own = lax.dynamic_slice_in_dim(value, lax.axis_index("shard") * count, count, 0).astype(F32)
        return (own + sum(piece.astype(F32) for piece in arriving)).astype(value.dtype)

    def around_hidden(own):
        core, far = swap(own, "core"), swap(own, "cx")
        return own, far, core, swap(far, "core")

    hidden_own = to_sequence(hidden_in)
    first_piece, attn_piece = hidden_piece(0), attention_piece(0)
    first_parts = around(after(hidden_own, first_piece, attn_piece))
    feed0 = over_shards(first_piece)
    attn0 = over_shards(after(attn_piece, feed0, *first_parts))
    feed_piece, attn_piece = hidden_piece(1), attention_piece(1)
    feed1 = over_shards(after(feed_piece, attn0))
    one0, two0 = turned(feed0, True), turned(feed0, False)

    def out_weights(own):
        full = jnp.zeros((shards, 4, quarter, width), BF16)
        for rel, part in enumerate(around(own)):
            full = lax.dynamic_update_slice(full, part, (0, dev ^ rel, 0, 0))
        return full.reshape(width, width)

    def out_own(gathered):
        return gathered[:, 3 * loc : 4 * loc].reshape(shards, 1, quarter, width)

    weights = []

    smalls = attn0[:, 4 * loc :].T.astype(F32)
    names = [[smalls[which * LAYERS + layer][None] for which in range(6)] for layer in range(LAYERS)]
    qv = smalls[6 * LAYERS : 8 * LAYERS].reshape(LAYERS, 2, shards, rows)
    qv = jnp.transpose(qv, (0, 2, 1, 3)).reshape(LAYERS, 2 * width)

    current = hidden_own.astype(F32)
    attn_parts = first_parts
    saved = []
    for layer in range(LAYERS):
        gain_one, bias_one, bias_out, gain_two, bias_two, bias_down = names[layer]
        w_qkv = attn0 if layer == 0 else attn1
        q_bias = lax.dynamic_slice_in_dim(qv[layer], loc * dev, loc, 0)
        v_bias = lax.dynamic_slice_in_dim(qv[layer], width + loc * dev, loc, 0)
        bias = jnp.concatenate((jnp.zeros((192,), F32), v_bias[128:], v_bias[:128], q_bias))[None]
        if layer == 0:
            one0, two0, attn_piece, *attn_parts = lax.optimization_barrier((one0, two0, attn_piece, *attn_parts))
            three0 = turned(one0, False)
            early_core = [swap(part, "core") for part in (feed0, one0, two0)]
        attn_t, qkv, attended, lse = attention_forward(info, attn_parts, w_qkv, bias, gain_one, bias_one, layer == 0)
        if layer == 0:
            attn1 = over_shards(after(attn_piece, attended))
            w_out = out_weights(out_own(attn0))
            attended, w_out, three0, *early_core = lax.optimization_barrier((attended, w_out, three0, *early_core))
            w_feed = (feed0, one0, two0, three0, *early_core, swap(three0, "core"))
        else:
            own, one, two, three = w_feed1
            early_core = (swap(own, "core"), swap(one, "core"))
            attended, w_out, raw_grad, own, one, two, three, *early_core = lax.optimization_barrier(
                (attended, w_out1, raw_grad, own, one, two, three, *early_core)
            )
            grad = raw_grad.astype(F32) * keep
            low_grad = grad.astype(BF16)
            low_other = swap(low_grad, "core")
        parts = (
            attended[0],
            swap(attended[1], "core"),
            swap(attended[2], "cx"),
            diagonal(attended[3]),
        )
        if layer == 1:
            late_core = [swap(after(part, *parts), "core") for part in (two, three)]
            w_feed = (own, one, two, three, *early_core, *late_core)
        vectors = jnp.concatenate((bias_out, gain_two, bias_two), axis=0)
        context, middle, mlp_in = out_forward(info, parts, w_out, current, vectors)
        if layer == 0:
            vectors = jnp.concatenate((bias_down, names[1][0], names[1][1]), axis=0)
            mlp_in, feed1 = lax.optimization_barrier((mlp_in, feed1))
            one1 = turned(feed1, True)
            slope, act, act_other, result, attn_own = feed_forward(mlp_in, middle, vectors, w_feed)
            act_other, mlp_other = swap(act_other, "core"), swap(mlp_in, "core")
            attn_own = after(attn_own, one1)
            attn_parts = around(attn_own)
            own_out1 = out_own(attn1)
            own_out1, act_other, mlp_other, given, *attn_parts = lax.optimization_barrier(
                (own_out1, act_other, mlp_other, output_grad, *attn_parts)
            )
            raw_grad = to_sequence(given)
            w_out1 = out_weights(own_out1)
            feed1, one1 = lax.optimization_barrier((feed1, one1, *attn_parts))[:2]
            w_feed1 = (feed1, one1, turned(feed1, False), turned(one1, False))
        else:
            slope = act = act_other = result = None
            mlp_other = swap(mlp_in, "core")
        weights.append((w_qkv, w_out, w_feed))
        saved.append((current, attn_t, qkv, attended, lse, context, middle, mlp_in, mlp_other, slope, act, act_other))
        current = result
    n = shards * units

    for layer in reversed(range(LAYERS)):
        x_in, attn_t, qkv, attended, lse, context, middle, mlp_in, mlp_other, slope, act, act_other = saved[layer]
        gain_one, _, _, gain_two, _, _ = names[layer]
        w_qkv, w_out, w_feed = weights[layer]
        if layer == 0:
            found = feed_backward(info, grad, low_grad, slope, middle, gain_two, w_out, w_feed)
        else:
            vectors = jnp.concatenate((names[1][5], gain_two), axis=0)
            *found, act, act_other, result = feed_both(info, mlp_in, grad, low_grad, middle, vectors, w_out, w_feed)
            act_other = swap(act_other, "core")
        dh, dh_other, middle_grad, branch_grad, sums_two, d0, d1, d2, d3 = found
        attn_grads = (d0, swap(d1, "core"), swap(d2, "cx"), diagonal(d3))
        tokens = (mlp_in, mlp_other, low_grad, low_other)
        dh_other = swap(dh_other, "core")
        *attn_grads, dh_other = lax.optimization_barrier((*attn_grads, dh_other))
        late = feed_weights(1, dh, dh_other, act, act_other, *tokens)
        w_out_grad = dot(context, branch_grad).astype(BF16).reshape(shards, 4, quarter, width)
        pieces = [lax.dynamic_index_in_dim(w_out_grad, dev ^ rel, 1, keepdims=False) for rel in range(4)]
        got = swap(jnp.stack((pieces[1], pieces[3])), "core")
        far = swap((pieces[2].astype(F32) + got[1].astype(F32)).astype(BF16), "cx")
        ready = [*attn_grads, late, far]
        if layer == 0:
            early = feed_weights(0, dh, dh_other, act, act_other, *tokens)
            ready += [early]
        *attn_grads, late, far = lax.optimization_barrier(tuple(ready))[:6]
        du, to_core, to_far, own, sums_u = attention_backward(info, qkv, attended, lse, w_qkv, attn_grads)
        late = turned(late, False)
        to_core = after(to_core, late)
        from_core = swap(to_core, "core")
        to_far = (to_far + from_core[1].astype(F32)).astype(BF16)
        if layer == 0:
            part = (early[n:].astype(F32) + late[n:].astype(F32)).astype(BF16)
            arrived = turned(part, True)
        from_far = swap(to_far, "cx")
        if layer > 0:
            du, dh_now, early_late = lax.optimization_barrier((du, dh, late, to_far))[:3]
            early = feed_weights(0, dh_now, dh_other, act, act_other, *tokens)
            part = (early[n:].astype(F32) + early_late[n:].astype(F32)).astype(BF16)
        du_sum = sums_u[0]
        v_sum = jnp.concatenate((du_sum[256:384], du_sum[192:256]))
        q_row = lax.dynamic_update_slice_in_dim(jnp.zeros((width,), F32), du_sum[384:], loc * dev, 0)
        v_row = lax.dynamic_update_slice_in_dim(jnp.zeros((width,), F32), v_sum, loc * dev, 0)
        qv_rows = jnp.concatenate((q_row, v_row)).reshape(shards, 2, rows).transpose(1, 0, 2).reshape(2, width)
        vectors = jnp.concatenate((sums_two, qv_rows, jnp.zeros((6, width), F32)), axis=0)
        if layer == 0:
            vectors = jnp.concatenate((vectors[:10], sums_one[:2], vectors[12:]), axis=0)
        flat = [piece.reshape(shards * quarter, width) for piece in (pieces[0], got[0], far)]
        if layer > 0:
            joined = attention_weights(attn_t, after(du, part), vectors, *flat)
            attn_sum1 = lax.psum_scatter(joined, "shard", scatter_dimension=0, tiled=True)
            hidden_out = from_sequence((after(result, to_far) * keep).astype(BF16))
            from_far, part, hidden_out = lax.optimization_barrier((from_far, part, hidden_out))
            arrived = turned(part, True)
        else:
            joined = attention_weights(attn_t, after(du, from_core, part), vectors, *flat)
            attn_sum = lax.psum_scatter(joined, "shard", scatter_dimension=0, tiled=True)
        grad, low_grad, sums_one = norm_backward(own, from_core, from_far, x_in, gain_one, middle_grad)
        if layer > 0:
            low_other = swap(low_grad, "core")
            grad, low_grad, arrived = lax.optimization_barrier((grad, low_grad, arrived))
            part = early[:n].astype(F32) + early_late[:n].astype(F32) + arrived.astype(F32)
            feed_sum1 = lax.psum_scatter(part.astype(BF16), "shard", scatter_dimension=0, tiled=True)
        else:
            part = (early[:n].astype(F32) + late[:n].astype(F32) + arrived.astype(F32)).astype(BF16)
            halves = sums_one[:2].reshape(2, shards, 2, units).transpose(1, 3, 0, 2).reshape(n, 4)
            part = lax.dynamic_update_slice(part, halves.astype(BF16), (0, 2 * width + 1))
            attn_sum1 = (attn_sum1.astype(F32) + swap(attn_sum1, "tp").astype(F32)).astype(BF16)
            part, attn_sum1, feed_sum1 = lax.optimization_barrier((part, attn_sum1, feed_sum1))
            arriving = send_shards(part, units)
            attn_parts1, hidden_parts1 = around(attn_sum1), around_hidden(feed_sum1)
            arriving = lax.optimization_barrier((*arriving, *attn_parts1, *hidden_parts1))[: len(arriving)]
            feed_sum = sum_shards(part, units, arriving)
            done = finish(info, 1, attn_parts1, hidden_parts1, None)
            attn_sum = after(attn_sum, feed_sum)
            attn_sum = (attn_sum.astype(F32) + swap(attn_sum, "tp").astype(F32)).astype(BF16)

    hidden_grad = from_sequence(low_grad).astype(F32)

    feed_sums = around_hidden(feed_sum)
    lone = sum(part[:, 2 * width + 1 : 2 * width + 5].astype(F32) for part in feed_sums)
    lone = lone + swap(lone, "tp")
    lone = lone.reshape(units, 2, 2).transpose(1, 2, 0).reshape(2, rows)
    done = finish(info, 0, around(attn_sum), feed_sums, done)
    first_gain = jnp.stack((lone[0], done[4][1]))
    first_bias = jnp.stack((lone[1], done[5][1]))

    return (
        hidden_out,
        hidden_grad,
        first_gain,
        first_bias,
        done[0],
        done[10],
        done[1],
        done[8],
        done[6],
        done[7],
        done[2],
        done[11],
        done[3],
        done[9],
    )


def solution(mesh):
    names = tuple(mesh.axis_names)
    shape = dict(mesh.shape)
    split = Mesh(
        mesh.devices.reshape(shape[names[0]], 2, shape[names[1]] // 2, shape[names[2]]),
        ("shard", "cx", "core", "tp"),
    )
    tokens = P("shard", ("cx", "core", "tp"), None)
    vector = P(None, "shard")
    attn = P(None, "shard", None)
    placed = (
        tokens,
        P("shard", None),
        vector,
        vector,
        attn,
        vector,
        attn,
        vector,
        vector,
        vector,
        P(None, None, ("shard", "tp")),
        P(None, ("shard", "tp")),
        P(None, ("shard", "tp"), None),
        vector,
        tokens,
    )
    return jax.shard_map(
        local,
        mesh=split,
        in_specs=placed,
        out_specs=(
            tokens,
            tokens,
            vector,
            vector,
            attn,
            vector,
            attn,
            vector,
            vector,
            vector,
            P(None, None, ("shard", "tp")),
            P(None, ("shard", "tp")),
            P(None, ("shard", "tp"), None),
            vector,
        ),
        check_vma=False,
    )
```

```python
from functools import partial, reduce

import jax
import jax.numpy as jnp
from jax import lax
from jax.experimental import pallas as pl
from jax.experimental.pallas import tpu as pltpu
from jax.sharding import Mesh
from jax.sharding import PartitionSpec as P

HEADS = 12
HEAD = 64
LAYERS = 2
BLK = 256
NEG = -1e30
EPS = 1e-06
F32 = jnp.float32
BF16 = jnp.bfloat16


def dot(left, right, dims=((1,), (0,))):
    return lax.dot_general(left, right, (dims, ((), ())), preferred_element_type=F32)


def swap(value, axis):
    return lax.ppermute(value, axis, ((0, 1), (1, 0)))


def block_place(block, dev, half):
    return (((block // 2) ^ dev) * 2) + ((block % 2) ^ half)


def doc_range(first, ends, length):
    last = first + BLK - 1
    start, stop = jnp.int32(0), jnp.int32(length)
    for end in ends:
        start = jnp.maximum(start, jnp.where(first >= end, end, 0))
        stop = jnp.minimum(stop, jnp.where(last < end, end, length))
    return start // BLK, (stop + BLK - 1) // BLK


def seg_of(places, ends):
    seg = (places >= ends[0]).astype(jnp.int32)
    for end in ends[1:]:
        seg = seg + (places >= end).astype(jnp.int32)
    return seg


def three_heads(pair, single):
    blank = jnp.zeros_like(single)
    return (
        jnp.concatenate((pair[:HEAD], blank), axis=0),
        jnp.concatenate((blank, pair[HEAD:]), axis=0),
        jnp.concatenate((single, blank), axis=0),
    )


def norm_rows(rows, gain, bias):
    centred = rows - jnp.mean(rows, axis=-1, keepdims=True)
    inv_std = lax.rsqrt(jnp.mean(centred * centred, axis=-1, keepdims=True) + EPS)
    return centred * inv_std * gain + bias


def whole(shape):
    return pl.BlockSpec(shape, lambda *at: (0,) * len(shape))


HBM = pl.BlockSpec(memory_space=pl.ANY)


def attention_forward_kernel(norm, info, *refs):
    parts, (w_ref, bias_ref, gain_ref, shift_ref) = refs[:4], refs[4:8]
    at_out, qkv_out, out_ref, lse_ref, a_ref, at_ref, qkv_ref, v_t, sems, out_sems = refs[8:]
    length = qkv_ref.shape[0]
    ends = (info[0], info[1], info[2])
    dev, half = info[3], info[4]
    each = parts[0].shape[0]
    copies = [pltpu.make_async_copy(part, a_ref.at[at], sems.at[at]) for at, part in enumerate(parts)]
    for copy in copies:
        copy.start()
    for part in range(4):
        copies[part].wait()

        def project(at, nothing):
            rows = pl.ds(pl.multiple_of(at * BLK, BLK), BLK)
            goal = pl.ds(pl.multiple_of(part * each + at * BLK, BLK), BLK)
            values = a_ref[part, rows, :]
            if norm:
                values = norm_rows(values.astype(F32), gain_ref[...], shift_ref[...]).astype(BF16)
            found = dot(values, w_ref[:, 0:576]) + bias_ref[...]
            at_ref[:, goal] = values.T
            qkv_ref[goal, 0:384] = found[:, 0:384].astype(BF16)
            qkv_ref[goal, 384:576] = (found[:, 384:576] * HEAD**-0.5).astype(BF16)
            pair = qkv_ref[goal, 256:384].T
            ones = jnp.ones((16, BLK), BF16)
            for head, found in enumerate((pair[:HEAD], pair[HEAD:], qkv_ref[goal, 128:256].T[HEAD:])):
                v_t[head, 0:HEAD, goal] = found
                v_t[head, HEAD : HEAD + 16, goal] = ones
            return nothing

        lax.fori_loop(0, each // BLK, project, 0)
    out_copies = [
        pltpu.make_async_copy(at_ref, at_out, out_sems.at[0]),
        pltpu.make_async_copy(qkv_ref, qkv_out, out_sems.at[1]),
    ]
    for copy in out_copies:
        copy.start()

    blocks = length // BLK
    lse_ref[...] = jnp.zeros_like(lse_ref)

    def per_block(step, nothing):
        mine = pl.ds(pl.multiple_of(step * BLK, BLK), BLK)
        first = block_place(step, dev, half) * BLK
        seg_q = seg_of(first + lax.broadcasted_iota(jnp.int32, (1, BLK), 1), ends)
        queries = three_heads(qkv_ref[mine, 384:512].T, qkv_ref[mine, 512:576].T)
        low, high = doc_range(first, ends, length)

        def body(count, begin, at, carry):
            tiles = []
            for more in range(count):
                block = begin + count * at + more
                place = block_place(block, dev, half)
                rows = pl.ds(pl.multiple_of(place * BLK, BLK), BLK)
                places = block * BLK + lax.broadcasted_iota(jnp.int32, (BLK, 1), 0)
                tiles.append((rows, seg_of(places, ends) == seg_q))

            def score(head):
                lanes = slice(128, 256) if head == 2 else slice(0, 128)
                return [jnp.where(allowed, dot(qkv_ref[rows, lanes], queries[head]), NEG) for rows, allowed in tiles]

            def weigh(head, scores):
                top, acc = carry[head]
                new_top = jnp.maximum(top, jnp.max(reduce(jnp.maximum, scores), axis=0, keepdims=True))
                shrink = jnp.exp(top - new_top)
                exps = [jnp.exp(one - new_top) for one in scores]
                return new_top, acc * shrink, [exp.astype(BF16) for exp in exps]

            def gather(head, weighed):
                top, acc, exps = weighed
                for (rows, _), exp in zip(tiles, exps):
                    acc = acc + dot(v_t[head, :, rows], exp)
                return top, acc

            s0 = score(0)
            s1 = score(1)
            w0 = weigh(0, s0)
            s2 = score(2)
            w1 = weigh(1, s1)
            r0 = gather(0, w0)
            w2 = weigh(2, s2)
            r1 = gather(1, w1)
            r2 = gather(2, w2)
            return r0, r1, r2

        start = tuple(
            (
                jnp.full((1, BLK), NEG, F32),
                jnp.zeros((HEAD + 16, BLK), F32),
            )
            for _ in range(3)
        )
        pairs, odd = (high - low) // 2, (high - low) % 2
        final = lax.fori_loop(0, pairs, partial(body, 2, low), start)
        final = lax.fori_loop(0, odd, partial(body, 1, high - 1), final)
        cols = pl.ds(pl.multiple_of((step % 2) * BLK, BLK), BLK)
        for head in range(3):
            top, acc = final[head]
            total = acc[HEAD : HEAD + 1]
            out_ref[step // 2, head * HEAD : (head + 1) * HEAD, cols] = (acc[:HEAD] / total).astype(BF16)
            lse_ref[head : head + 1, mine] = top + jnp.log(total)
        return nothing

    lax.fori_loop(0, blocks, per_block, 0)
    for copy in out_copies:
        copy.wait()


def attention_forward(info, parts, w_qkv, bias, gain, shift, norm):
    each, width = parts[0].shape
    length = 4 * each
    return pl.pallas_call(
        partial(attention_forward_kernel, norm),
        name="attention_forward",
        grid_spec=pltpu.PrefetchScalarGridSpec(
            num_scalar_prefetch=1,
            grid=(1,),
            in_specs=[HBM] * 4 + [whole(w_qkv.shape), whole(bias.shape), whole(gain.shape), whole(shift.shape)],
            out_specs=[HBM, HBM, whole((4, 192, each)), whole((8, length))],
            scratch_shapes=[
                pltpu.VMEM((4, each, width), BF16),
                pltpu.VMEM((width, length), BF16),
                pltpu.VMEM((length, 576), BF16),
                pltpu.VMEM((3, HEAD + 16, length), BF16),
                pltpu.SemaphoreType.DMA((4,)),
                pltpu.SemaphoreType.DMA((2,)),
            ],
        ),
        out_shape=(
            jax.ShapeDtypeStruct((width, length), BF16),
            jax.ShapeDtypeStruct((length, 576), BF16),
            jax.ShapeDtypeStruct((4, 192, each), BF16),
            jax.ShapeDtypeStruct((8, length), F32),
        ),
        compiler_params=pltpu.CompilerParams(vmem_limit_bytes=48 << 20),
        cost_estimate=pl.CostEstimate(
            flops=14 * 10**9, transcendentals=3 * length * 1024, bytes_accessed=12 << 20
        ),
    )(info, *parts, w_qkv, bias, gain, shift)


def attention_backward_kernel(norm, info, qkv_ref, out_ref, lse_ref, w_ref, g0, g1, g2, g3, *refs):
    if norm:
        tokens, refs = refs[:4], refs[4:]
        norm_sums, refs = refs[5], refs[:5] + refs[6:]
        x_ref, da_ref, x_sems = refs[-3:]
        token_copies = [pltpu.make_async_copy(part, x_ref.at[at], x_sems.at[at]) for at, part in enumerate(tokens)]
        for copy in token_copies:
            copy.start()
        refs = refs[:-3]
    du_out, core_out, far_out, own_out, sums_ref = refs[:5]
    q01_t, q2_t, delta, dq_t, grad_t, du_ref, core_ref, far_ref, own_ref, sems = refs[5:]
    length = qkv_ref.shape[0]
    each = length // 4
    ends = (info[0], info[1], info[2])
    dev, half = info[3], info[4]
    blocks = length // BLK
    q01_t[...] = qkv_ref[:, 384:512].T
    q2_t[...] = qkv_ref[:, 512:576].T
    dq_t[...] = jnp.zeros_like(dq_t)
    for part, grad in enumerate((g0, g1, g2, g3)):
        grad_t[part] = grad[...]
        for head in range(3):
            rows = slice(head * HEAD, (head + 1) * HEAD)
            both = out_ref[part, rows].astype(F32) * grad[rows].astype(F32)
            delta[head : head + 1, part * each : (part + 1) * each] = jnp.sum(both, axis=0, keepdims=True)

    def per_block(step, nothing):
        mine = pl.ds(pl.multiple_of(step * BLK, BLK), BLK)
        first = block_place(step, dev, half) * BLK
        seg_k = seg_of(first + lax.broadcasted_iota(jnp.int32, (BLK, 1), 0), ends)
        k01 = qkv_ref[mine, 0:128]
        k2v2 = qkv_ref[mine, 128:256]
        v01 = qkv_ref[mine, 256:384]
        k01_t = k01.T
        k2_t = k2v2.T[:HEAD]
        keys_t = (k01_t[:HEAD], k01_t[HEAD:], k2_t)
        low, high = doc_range(first, ends, length)

        def body(width, begin, at, carry):
            blank = jnp.zeros((HEAD, BLK), BF16)
            tiles = []
            for more in range(width):
                block = begin + width * at + more
                place = block_place(block, dev, half)
                cols = pl.ds(pl.multiple_of(place * BLK, BLK), BLK)
                part_cols = pl.ds(pl.multiple_of((place % 2) * BLK, BLK), BLK)
                places = block * BLK + lax.broadcasted_iota(jnp.int32, (1, BLK), 1)
                allowed = seg_k == seg_of(places, ends)
                queries = three_heads(q01_t[:, cols], q2_t[:, cols])
                grads = grad_t[place // 2, :, part_cols]
                dos = (
                    jnp.concatenate((grads[:HEAD], blank), axis=0),
                    jnp.concatenate((blank, grads[HEAD:128]), axis=0),
                    jnp.concatenate((blank, grads[128:192]), axis=0),
                )
                tiles.append((cols, allowed, queries, dos))

            def first_dots(at):
                cols, allowed, queries, dos = tiles[at // 3]
                head = at % 3
                return (
                    dot(k2v2 if head == 2 else k01, queries[head]),
                    dot(k2v2 if head == 2 else v01, dos[head]),
                )

            def weigh(at, found):
                cols, allowed, queries, dos = tiles[at // 3]
                head = at % 3
                scores, grad_probs = found
                probs = jnp.where(allowed, jnp.exp(scores - lse_ref[head : head + 1, cols]), 0.0)
                grad_scores = (probs * (grad_probs - delta[head : head + 1, cols])).astype(BF16)
                return probs.astype(BF16), grad_scores

            def last_dots(at, found, sums):
                cols, allowed, queries, dos = tiles[at // 3]
                head = at % 3
                probs, grad_scores = found
                more_k = dot(grad_scores, queries[head], ((1,), (1,)))
                more_v = dot(probs, dos[head], ((1,), (1,)))
                more_q = dot(keys_t[head], grad_scores)
                dk01, dk2v2, dv01 = sums
                if head == 2:
                    dk2v2 = dk2v2 + more_k + more_v
                else:
                    dk01 = dk01 + more_k
                    dv01 = dv01 + more_v
                return (dk01, dk2v2, dv01), more_q

            count = 3 * width
            sums = carry
            more_q = []
            begun = {0: first_dots(0), 1: first_dots(1)}
            weighed = {}
            for at in range(count):
                if at + 2 < count:
                    begun[at + 2] = first_dots(at + 2)
                weighed[at] = weigh(at, begun[at])
                if at > 0:
                    sums, found = last_dots(at - 1, weighed[at - 1], sums)
                    more_q.append(found)
            sums, found = last_dots(count - 1, weighed[count - 1], sums)
            more_q.append(found)
            for tile in range(width):
                cols = tiles[tile][0]
                dq_t[:, cols] = dq_t[:, cols] + jnp.concatenate(more_q[3 * tile : 3 * tile + 3], axis=0)
            return sums

        zero = jnp.zeros((BLK, 128), F32)
        pairs, odd = (high - low) // 2, (high - low) % 2
        sums = lax.fori_loop(0, pairs, partial(body, 2, low), (zero, zero, zero))
        dk01, dk2v2, dv01 = lax.fori_loop(0, odd, partial(body, 1, high - 1), sums)
        du_ref[mine, 0:128] = dk01.astype(BF16)
        du_ref[mine, 128:256] = dk2v2.astype(BF16)
        du_ref[mine, 256:384] = dv01.astype(BF16)
        return nothing

    lax.fori_loop(0, blocks, per_block, 0)
    sums_ref[...] = jnp.zeros_like(sums_ref)
    scale = HEAD**-0.5

    def finish_rows(at, total):
        rows = pl.ds(pl.multiple_of(at * BLK, BLK), BLK)
        du_ref[rows, 384:512] = (dq_t[0:128, rows] * scale).T.astype(BF16)
        du_ref[rows, 512:576] = (dq_t[128:192, rows] * scale).T.astype(BF16)
        return total + jnp.sum(du_ref[rows, :].astype(F32), axis=0, keepdims=True)

    sums_ref[0:1, :] = lax.fori_loop(0, blocks, finish_rows, jnp.zeros((1, 576), F32))
    copies = [pltpu.make_async_copy(du_ref, du_out, sems.at[0])]
    copies[0].start()
    plan = ((1, core_ref.at[0], core_out.at[0]), (3, core_ref.at[1], core_out.at[1]), (2, far_ref, far_out), (0, own_ref, own_out))
    if norm:
        for copy in token_copies:
            copy.wait()
        width = da_ref.shape[1]
        totals = (jnp.zeros((1, width), F32), jnp.zeros((1, width), F32))
    for at, (part, target, goal) in enumerate(plan):
        kind = target.dtype
        found = dot(du_ref[part * each : (part + 1) * each, :], w_ref[:, 0:576], ((1,), (1,)))
        if norm:
            da_ref[...] = found

            def rows_of(step, sums, part=part):
                rows = pl.ds(pl.multiple_of(step * 64, 64), 64)
                grad = da_ref[rows, :]
                normed = norm_rows(x_ref[part, rows, :].astype(F32), 1.0, 0.0)
                return (
                    sums[0] + jnp.sum(grad * normed, axis=0, keepdims=True),
                    sums[1] + jnp.sum(grad, axis=0, keepdims=True),
                )

            totals = lax.fori_loop(0, each // 64, rows_of, totals)
            found = da_ref[...]
        target[...] = found.astype(kind)
        copies.append(pltpu.make_async_copy(target, goal, sems.at[at + 1]))
        copies[-1].start()
    if norm:
        norm_sums[...] = jnp.zeros_like(norm_sums)
        norm_sums[0:1, :] = totals[0]
        norm_sums[1:2, :] = totals[1]
    for copy in copies:
        copy.wait()


def attention_backward(info, qkv, out, lse, w_qkv, grads, tokens=()):
    norm = len(tokens) > 0
    length, each, width = qkv.shape[0], qkv.shape[0] // 4, w_qkv.shape[0]
    return pl.pallas_call(
        partial(attention_backward_kernel, norm),
        name="attention_backward",
        grid_spec=pltpu.PrefetchScalarGridSpec(
            num_scalar_prefetch=1,
            grid=(1,),
            in_specs=[whole(qkv.shape), whole(out.shape), whole(lse.shape), whole(w_qkv.shape)]
            + [whole((192, each))] * 4
            + [HBM] * len(tokens),
            out_specs=[HBM, HBM, HBM, HBM, whole((8, 576))] + [whole((8, width))] * norm,
            scratch_shapes=[
                pltpu.VMEM((128, length), BF16),
                pltpu.VMEM((64, length), BF16),
                pltpu.VMEM((8, length), F32),
                pltpu.VMEM((192, length), F32),
                pltpu.VMEM((4, 192, each), BF16),
                pltpu.VMEM((length, 576), BF16),
                pltpu.VMEM((2, each, width), BF16),
                pltpu.VMEM((each, width), F32),
                pltpu.VMEM((each, width), F32),
                pltpu.SemaphoreType.DMA((5,)),
            ]
            + [pltpu.VMEM((4, each, width), BF16), pltpu.VMEM((each, width), F32), pltpu.SemaphoreType.DMA((4,))] * norm,
        ),
        out_shape=(
            jax.ShapeDtypeStruct(qkv.shape, BF16),
            jax.ShapeDtypeStruct((2, each, width), BF16),
            jax.ShapeDtypeStruct((each, width), F32),
            jax.ShapeDtypeStruct((each, width), F32),
            jax.ShapeDtypeStruct((8, 576), F32),
        )
        + (jax.ShapeDtypeStruct((8, width), F32),) * norm,
        compiler_params=pltpu.CompilerParams(vmem_limit_bytes=56 << 20),
        cost_estimate=pl.CostEstimate(
            flops=20 * 10**9, transcendentals=3 * length * 1024, bytes_accessed=16 << 20
        ),
    )(info, qkv, out, lse, w_qkv, *grads, *tokens)


def attention_weights_kernel(at_ref, du_ref, vec_ref, own_ref, core_ref, far_ref, out_ref, spread):
    blank = jnp.zeros((128 - vec_ref.shape[0], vec_ref.shape[1]), F32)
    out_ref[:, 768:896] = jnp.concatenate((vec_ref[...], blank), axis=0).T.astype(BF16)
    out_ref[:, 0:576] = dot(at_ref[...], du_ref[...]).astype(BF16)
    total = own_ref[...].astype(F32) + core_ref[...].astype(F32) + far_ref[...].astype(F32)
    quarter = own_ref.shape[0]
    for piece in range(4):
        rows = pl.ds(piece, quarter, stride=4)
        spread[0, rows, :] = total[:, piece * 192 : piece * 192 + 128]
        spread[1, rows, :] = jnp.concatenate(
            (total[:, piece * 192 + 128 : (piece + 1) * 192], jnp.zeros((quarter, 64), F32)), axis=1
        )
    out_ref[:, 576:704] = spread[0].astype(BF16)
    out_ref[:, 704:768] = spread[1, :, 0:64].astype(BF16)


def attention_weights(a_t, du, vectors, own, core, far):
    width = a_t.shape[0]
    return pl.pallas_call(
        attention_weights_kernel,
        name="attention_weights",
        grid=(1,),
        in_specs=[whole(v.shape) for v in (a_t, du, vectors, own, core, far)],
        out_specs=whole((width, width + 128)),
        out_shape=jax.ShapeDtypeStruct((width, width + 128), BF16),
        scratch_shapes=[pltpu.VMEM((2, width, 128), F32)],
        compiler_params=pltpu.CompilerParams(vmem_limit_bytes=48 << 20),
        cost_estimate=pl.CostEstimate(flops=18 * 10**8, transcendentals=0, bytes_accessed=8 << 20),
    )(a_t, du, vectors, own, core, far)


def out_kernel(info, p0, p1, p2, p3, w_ref, x_ref, vec_ref, ctx_ref, mid_ref, c_ref, ctx):
    dev = info[3]
    loc, toks = p0.shape
    for rel, part in enumerate((p0, p1, p2, p3)):
        ctx[dev ^ rel] = part[...]
    ctx_ref[...] = ctx[...].reshape(4 * loc, toks)

    def rows_of(at, nothing):
        rows = pl.ds(pl.multiple_of(at * 128, 128), 128)
        found = dot(ctx_ref[:, rows].T, w_ref[...])
        middle = x_ref[rows, :] + found + vec_ref[0:1, :]
        mid_ref[rows, :] = middle
        c_ref[rows, :] = norm_rows(middle, vec_ref[1:2, :], vec_ref[2:3, :]).astype(BF16)
        return nothing

    lax.fori_loop(0, toks // 128, rows_of, 0)


def out_forward(info, parts, w_out, current, vectors):
    loc, toks = parts[0].shape
    width = w_out.shape[1]
    return pl.pallas_call(
        out_kernel,
        name="out_forward",
        grid_spec=pltpu.PrefetchScalarGridSpec(
            num_scalar_prefetch=1,
            grid=(1,),
            in_specs=[whole((loc, toks))] * 4 + [whole(w_out.shape), whole(current.shape), whole(vectors.shape)],
            out_specs=[whole((width, toks)), whole((toks, width)), whole((toks, width))],
            scratch_shapes=[pltpu.VMEM((4, loc, toks), BF16)],
        ),
        out_shape=(
            jax.ShapeDtypeStruct((width, toks), BF16),
            jax.ShapeDtypeStruct((toks, width), F32),
            jax.ShapeDtypeStruct((toks, width), BF16),
        ),
        compiler_params=pltpu.CompilerParams(vmem_limit_bytes=48 << 20),
        cost_estimate=pl.CostEstimate(flops=10**9, transcendentals=0, bytes_accessed=7 << 20),
    )(info, *parts, w_out, current, vectors)


def norm_back(grad, values, gain):
    centred = values - jnp.mean(values, axis=-1, keepdims=True)
    inv_std = lax.rsqrt(jnp.mean(centred * centred, axis=-1, keepdims=True) + EPS)
    normed = centred * inv_std
    scaled = grad * gain
    grad_in = inv_std * (
        scaled
        - jnp.mean(scaled, axis=-1, keepdims=True)
        - normed * jnp.mean(scaled * normed, axis=-1, keepdims=True)
    )
    return grad_in, jnp.sum(grad * normed, axis=0, keepdims=True), jnp.sum(grad, axis=0, keepdims=True)


def norm_back_kernel(own, core, far, x_ref, gain_ref, mid_ref, grad_ref, low_ref, sums_ref):
    toks, width = x_ref.shape
    step = pl.program_id(0)

    @pl.when(step == 0)
    def _():
        sums_ref[...] = jnp.zeros_like(sums_ref)

    def rows_of(at, sums):
        rows = pl.ds(pl.multiple_of(at * 64, 64), 64)
        found = own[rows, :] + core[0, rows, :].astype(F32) + far[rows, :].astype(F32)
        grad_in, gain_sum, bias_sum = norm_back(found, x_ref[rows, :], gain_ref[...])
        grad = mid_ref[rows, :] + grad_in
        grad_ref[rows, :] = grad
        low_ref[rows, :] = grad.astype(BF16)
        return sums[0] + gain_sum, sums[1] + bias_sum

    zero = jnp.zeros((1, width), F32)
    sums = lax.fori_loop(0, toks // 64, rows_of, (zero, zero))
    sums_ref[0:1, :] += sums[0]
    sums_ref[1:2, :] += sums[1]


def norm_backward(own, core, far, values, gain, middle_grad):
    toks, width = values.shape
    rows = pl.BlockSpec((toks // 4, width), lambda i: (i, 0))
    return pl.pallas_call(
        norm_back_kernel,
        name="norm_backward",
        grid=(4,),
        in_specs=[rows, pl.BlockSpec((1, toks // 4, width), lambda i: (0, i, 0)), rows, rows, whole(gain.shape), rows],
        out_specs=[rows, rows, whole((8, width))],
        out_shape=(
            jax.ShapeDtypeStruct((toks, width), F32),
            jax.ShapeDtypeStruct((toks, width), BF16),
            jax.ShapeDtypeStruct((8, width), F32),
        ),
        compiler_params=pltpu.CompilerParams(vmem_limit_bytes=48 << 20),
        cost_estimate=pl.CostEstimate(flops=10**7, transcendentals=0, bytes_accessed=9 << 20),
    )(own, core, far, values, gain, middle_grad)


GELU_A = (2.0 / 3.141592653589793) ** 0.5
GELU_B = 0.044715


def gelu(t):
    square = t * t
    tanh = jnp.tanh(t * (GELU_A + GELU_A * GELU_B * square))
    half = 0.5 * t
    side = 0.5 + 0.5 * tanh
    slope = side + (half - half * tanh * tanh) * (GELU_A + 3.0 * GELU_A * GELU_B * square)
    return t * side, slope


def fetch(parts, held, sems):
    units = parts[0].shape[0]
    copies = [
        pltpu.make_async_copy(part, held.at[at // 2, pl.ds((at % 2) * units, units)], sems.at[at])
        for at, part in enumerate(parts)
    ]
    for copy in copies:
        copy.start()
    return copies


def feed_kernel(c_ref, mid_ref, vec_ref, *refs):
    parts, refs = refs[:8], refs[8:]
    slope_out, own_out, other_out, x_ref, a_ref, slope_ref, act_ref, held, sems, out_sems = refs
    toks, width = mid_ref.shape
    copies = fetch(parts, held, sems)
    x_ref[...] = mid_ref[...] + vec_ref[0:1, :]
    outs = []

    def before(at):
        copies[2 * at].wait()
        copies[2 * at + 1].wait()
        bias = held[at, :, 2 * width : 2 * width + 128].T[0:1].astype(F32)
        return dot(c_ref[...], held[at, :, 0:width], ((1,), (1,))) + bias

    def after(at, pre):
        act, slope = gelu(pre)
        act = act.astype(BF16)
        slope_ref[at] = slope.astype(BF16)
        act_ref[at] = act.T
        outs.append(pltpu.make_async_copy(slope_ref.at[at], slope_out.at[at], out_sems.at[2 * at]))
        goal = (own_out, other_out)[at // 2].at[at % 2]
        outs.append(pltpu.make_async_copy(act_ref.at[at], goal, out_sems.at[2 * at + 1]))
        outs[-2].start()
        outs[-1].start()
        x_ref[...] += dot(act, held[at, :, width : 2 * width])

    pre = before(0)
    for at in range(4):
        later = before(at + 1) if at < 3 else None
        after(at, pre)
        pre = later

    def rows_of(at, nothing):
        rows = pl.ds(pl.multiple_of(at * 64, 64), 64)
        a_ref[rows, :] = norm_rows(x_ref[rows, :], vec_ref[1:2, :], vec_ref[2:3, :]).astype(BF16)
        return nothing

    lax.fori_loop(0, toks // 64, rows_of, 0)
    for copy in outs:
        copy.wait()


def feed_forward(c, middle, vectors, parts):
    toks, width = middle.shape
    units = 2 * parts[0].shape[0]
    return pl.pallas_call(
        feed_kernel,
        name="feed_forward",
        grid=(1,),
        in_specs=[whole(c.shape), whole(middle.shape), whole(vectors.shape)] + [HBM] * 8,
        out_specs=[HBM, HBM, HBM, whole((toks, width)), whole((toks, width))],
        out_shape=[
            jax.ShapeDtypeStruct((4, toks, units), BF16),
            jax.ShapeDtypeStruct((2, units, toks), BF16),
            jax.ShapeDtypeStruct((2, units, toks), BF16),
            jax.ShapeDtypeStruct((toks, width), F32),
            jax.ShapeDtypeStruct((toks, width), BF16),
        ],
        scratch_shapes=[
            pltpu.VMEM((4, toks, units), BF16),
            pltpu.VMEM((4, units, toks), BF16),
            pltpu.VMEM((4, units, parts[0].shape[1]), BF16),
            pltpu.SemaphoreType.DMA((8,)),
            pltpu.SemaphoreType.DMA((8,)),
        ],
        compiler_params=pltpu.CompilerParams(vmem_limit_bytes=56 << 20),
        cost_estimate=pl.CostEstimate(flops=5 * 10**9, transcendentals=2 * 10**6, bytes_accessed=20 << 20),
    )(c, middle, vectors, *parts)


def finish_back(dev, grad_ref, mid_ref, gain_ref, w_ref, dm_ref, dc, dmid_ref, da_ref, sums_ref, targets):
    toks, width = mid_ref.shape
    loc = targets[0].shape[0]

    def rows_of(at, sums):
        rows = pl.ds(pl.multiple_of(at * 64, 64), 64)
        grad_in, gain_sum, bias_sum = norm_back(dc[rows, :], mid_ref[rows, :], gain_ref[...])
        grad_mid = grad_ref[rows, :].astype(F32) + grad_in
        dmid_ref[rows, :] = grad_mid
        branch = grad_mid.astype(BF16)
        da_ref[rows, :] = branch
        out_sum = jnp.sum(branch.astype(F32), axis=0, keepdims=True)
        down_sum = jnp.sum(dm_ref[rows, :].astype(F32), axis=0, keepdims=True)
        return sums[0] + gain_sum, sums[1] + bias_sum, sums[2] + out_sum, sums[3] + down_sum

    zero = jnp.zeros((1, width), F32)
    sums = lax.fori_loop(0, toks // 64, rows_of, (zero,) * 4)
    sums_ref[...] = jnp.zeros_like(sums_ref)
    for at in range(4):
        sums_ref[at : at + 1, :] = sums[at]
    for rel, target in enumerate(targets):
        rows = pl.ds(pl.multiple_of((dev ^ rel) * loc, 64), loc)
        target[...] = dot(w_ref[rows, :], da_ref[...], ((1,), (1,))).astype(BF16)


def back_outputs(toks, width, units):
    return [
        jax.ShapeDtypeStruct((2, toks, units), BF16),
        jax.ShapeDtypeStruct((2, toks, units), BF16),
        jax.ShapeDtypeStruct((toks, width), F32),
        jax.ShapeDtypeStruct((toks, width), BF16),
        jax.ShapeDtypeStruct((8, width), F32),
    ] + [jax.ShapeDtypeStruct((width // 4, toks), BF16)] * 4


def feed_back_kernel(info, grad_ref, dm_ref, slope_in, mid_in, gain_ref, w_in, *refs):
    parts, refs = refs[:8], refs[8:]
    own_out, other_out, dmid_ref, da_ref, sums_ref, *targets = refs[:9]
    slope_ref, dh_ref, held, dc, mid_ref, w_ref, sems, slope_sems, out_sems, in_sems = refs[9:]
    width = mid_ref.shape[1]
    copies = fetch(parts, held, sems)
    slopes = [pltpu.make_async_copy(slope_in.at[at], slope_ref.at[at], slope_sems.at[at]) for at in range(4)]
    late_in = [pltpu.make_async_copy(mid_in, mid_ref, in_sems.at[0]), pltpu.make_async_copy(w_in, w_ref, in_sems.at[1])]
    for copy in slopes + late_in:
        copy.start()
    outs = []
    goals = (own_out.at[0], own_out.at[1], other_out.at[0], other_out.at[1])

    def before(at):
        copies[2 * at].wait()
        copies[2 * at + 1].wait()
        return dot(dm_ref[...], held[at, :, width : 2 * width], ((1,), (1,)))

    def after(at, dact):
        slopes[at].wait()
        dpre = (dact * slope_ref[at].astype(F32)).astype(BF16)
        dh_ref[at] = dpre
        outs.append(pltpu.make_async_copy(dh_ref.at[at], goals[at], out_sems.at[at]))
        outs[-1].start()
        term = dot(dpre, held[at, :, 0:width])
        if at == 0:
            dc[...] = term
        else:
            dc[...] += term

    dact = before(0)
    for at in range(4):
        later = before(at + 1) if at < 3 else None
        after(at, dact)
        dact = later
    for copy in late_in:
        copy.wait()
    finish_back(info[3], grad_ref, mid_ref, gain_ref, w_ref, dm_ref, dc, dmid_ref, da_ref, sums_ref, targets)
    for copy in outs:
        copy.wait()


def feed_backward(info, grad, dm, slope, middle, gain, w_out, parts):
    toks, width = middle.shape
    units = 2 * parts[0].shape[0]
    shapes = back_outputs(toks, width, units)
    return pl.pallas_call(
        feed_back_kernel,
        name="feed_backward",
        grid_spec=pltpu.PrefetchScalarGridSpec(
            num_scalar_prefetch=1,
            grid=(1,),
            in_specs=[whole(grad.shape), whole(dm.shape), HBM, HBM, whole(gain.shape), HBM] + [HBM] * 8,
            out_specs=[HBM] * 2 + [whole(shape.shape) for shape in shapes[2:]],
            scratch_shapes=[
                pltpu.VMEM((4, toks, units), BF16),
                pltpu.VMEM((4, toks, units), BF16),
                pltpu.VMEM((4, units, parts[0].shape[1]), BF16),
                pltpu.VMEM((toks, width), F32),
                pltpu.VMEM((toks, width), F32),
                pltpu.VMEM((width, width), BF16),
                pltpu.SemaphoreType.DMA((8,)),
                pltpu.SemaphoreType.DMA((4,)),
                pltpu.SemaphoreType.DMA((4,)),
                pltpu.SemaphoreType.DMA((2,)),
            ],
        ),
        out_shape=shapes,
        compiler_params=pltpu.CompilerParams(vmem_limit_bytes=60 << 20),
        cost_estimate=pl.CostEstimate(flops=6 * 10**9, transcendentals=2 * 10**6, bytes_accessed=24 << 20),
    )(info, grad, dm, slope, middle, gain, w_out, *parts)


def feed_both_kernel(info, c_ref, dm_ref, mid_ref, vec_ref, w_in, *refs):
    parts, refs = refs[:8], refs[8:]
    own_out, other_out, dmid_ref, da_ref, sums_ref, *targets = refs[:9]
    act_own, act_other, x_ref = refs[9:12]
    act_ref, dh_ref, held, dc, w_ref, sems, out_sems, in_sem = refs[12:]
    toks, width = mid_ref.shape
    copies = fetch(parts, held, sems)
    late_in = pltpu.make_async_copy(w_in, w_ref, in_sem.at[0])
    late_in.start()
    x_ref[...] = mid_ref[...] + vec_ref[0:1, :]
    outs = []
    goals = (own_out.at[0], own_out.at[1], other_out.at[0], other_out.at[1])

    def before(at):
        copies[2 * at].wait()
        copies[2 * at + 1].wait()
        bias = held[at, :, 2 * width : 2 * width + 128].T[0:1].astype(F32)
        pre = dot(c_ref[...], held[at, :, 0:width], ((1,), (1,))) + bias
        return pre, dot(dm_ref[...], held[at, :, width : 2 * width], ((1,), (1,)))

    def after(at, found):
        pre, dact = found
        act, slope = gelu(pre)
        act = act.astype(BF16)
        act_ref[at] = act.T
        dpre = (dact * slope).astype(BF16)
        dh_ref[at] = dpre
        goal = (act_own, act_other)[at // 2].at[at % 2]
        outs.append(pltpu.make_async_copy(dh_ref.at[at], goals[at], out_sems.at[2 * at]))
        outs.append(pltpu.make_async_copy(act_ref.at[at], goal, out_sems.at[2 * at + 1]))
        outs[-2].start()
        outs[-1].start()
        x_ref[...] += dot(act, held[at, :, width : 2 * width])
        term = dot(dpre, held[at, :, 0:width])
        if at == 0:
            dc[...] = term
        else:
            dc[...] += term

    found = before(0)
    for at in range(4):
        later = before(at + 1) if at < 3 else None
        after(at, found)
        found = later
    late_in.wait()
    finish_back(info[3], dm_ref, mid_ref, vec_ref.at[1:2], w_ref, dm_ref, dc, dmid_ref, da_ref, sums_ref, targets)
    for copy in outs:
        copy.wait()


def feed_both(info, c, dm, middle, vectors, w_out, parts):
    toks, width = middle.shape
    units = 2 * parts[0].shape[0]
    shapes = back_outputs(toks, width, units) + [
        jax.ShapeDtypeStruct((2, units, toks), BF16),
        jax.ShapeDtypeStruct((2, units, toks), BF16),
        jax.ShapeDtypeStruct((toks, width), F32),
    ]
    return pl.pallas_call(
        feed_both_kernel,
        name="feed_both",
        grid_spec=pltpu.PrefetchScalarGridSpec(
            num_scalar_prefetch=1,
            grid=(1,),
            in_specs=[whole(v.shape) for v in (c, dm, middle, vectors)] + [HBM] * 9,
            out_specs=[HBM] * 2 + [whole(shape.shape) for shape in shapes[2:9]] + [HBM, HBM, whole((toks, width))],
            scratch_shapes=[
                pltpu.VMEM((4, units, toks), BF16),
                pltpu.VMEM((4, toks, units), BF16),
                pltpu.VMEM((4, units, parts[0].shape[1]), BF16),
                pltpu.VMEM((toks, width), F32),
                pltpu.VMEM((width, width), BF16),
                pltpu.SemaphoreType.DMA((8,)),
                pltpu.SemaphoreType.DMA((8,)),
                pltpu.SemaphoreType.DMA((1,)),
            ],
        ),
        out_shape=shapes,
        compiler_params=pltpu.CompilerParams(vmem_limit_bytes=60 << 20),
        cost_estimate=pl.CostEstimate(flops=10**10, transcendentals=2 * 10**6, bytes_accessed=24 << 20),
    )(info, c, dm, middle, vectors, w_out, *parts)


def feed_weights_kernel(dh, dh2, act, act2, c, c2, dm, dm2, out_ref):
    width = c.shape[1]
    one, two = dh[0].T, dh2[0].T
    out_ref[:, 0:width] = (dot(one, c[...]) + dot(two, c2[...])).astype(BF16)
    out_ref[:, width : 2 * width] = (dot(act[0], dm[...]) + dot(act2[0], dm2[...])).astype(BF16)
    bias = jnp.sum(one.astype(F32), axis=1, keepdims=True) + jnp.sum(two.astype(F32), axis=1, keepdims=True)
    out_ref[:, 2 * width :] = jnp.broadcast_to(bias, (bias.shape[0], 128)).astype(BF16)


def feed_weights(half, dh, dh2, act, act2, c, c2, dm, dm2):
    toks, units, width = dh.shape[1], dh.shape[2], c.shape[1]
    wide = 2 * width + 128
    step = 256
    act_spec = pl.BlockSpec((1, step, toks), lambda i: (half, i, 0))
    return pl.pallas_call(
        feed_weights_kernel,
        name="feed_weights",
        grid=(units // step,),
        in_specs=[
            pl.BlockSpec((1, toks, step), lambda i: (half, 0, i)),
            pl.BlockSpec((1, toks, step), lambda i: (half, 0, i)),
            act_spec,
            act_spec,
        ]
        + [pl.BlockSpec(v.shape, lambda i: (0, 0)) for v in (c, c2, dm, dm2)],
        out_specs=pl.BlockSpec((step, wide), lambda i: (i, 0)),
        out_shape=jax.ShapeDtypeStruct((units, wide), BF16),
        compiler_params=pltpu.CompilerParams(vmem_limit_bytes=48 << 20),
        cost_estimate=pl.CostEstimate(flops=24 * 10**8, transcendentals=0, bytes_accessed=9 << 20),
    )(dh, dh2, act, act2, c, c2, dm, dm2)


def finish_kernel(last, info, *refs):
    attn, hidden, refs = refs[:4], refs[4:8], refs[8:]
    if last:
        (other_vec, other_bias), refs = refs[:2], refs[6:]
        qkv_ref, out_ref, up_ref, down_ref = refs[:4]
        vectors_out, qv_out, bias_out = refs[4:10], refs[10], refs[11]
        qkv_at, out_at, hid_at = refs[12:]
    else:
        qkv_ref, out_ref, up_ref, down_ref, vec_ref, bias_ref, qkv_at, out_at, hid_at = refs
    dev = info[3]
    spot = info[5]
    rows = attn[0].shape[0]
    loc = 192
    for rel in range(4):
        qkv_at[dev ^ rel] = attn[rel][:, 0:576].astype(F32)
        out_at[dev ^ rel, 0] = attn[rel][:, 576:704].astype(F32)
        out_at[dev ^ rel, 1, :, 0:64] = attn[rel][:, 704:768].astype(F32)
        hid_at[spot ^ rel] = hidden[rel][...].astype(F32)
    width = 4 * loc
    quarter = rows // 4
    units = hidden[0].shape[0]
    for at in range(4):
        found = qkv_at[at]
        qkv_ref[0, :, at * loc : (at + 1) * loc] = found[:, 384:576]
        qkv_ref[0, :, width + at * loc : width + (at + 1) * loc] = found[:, 0:192]
        v_at = 2 * width + at * loc
        qkv_ref[0, :, v_at : v_at + 128] = found[:, 256:384]
        qkv_ref[0, :, v_at + 128 : v_at + 192] = found[:, 192:256]
        for piece in range(4):
            goal = slice(at * quarter, (at + 1) * quarter)
            lane = piece * loc
            out_ref[0, goal, lane : lane + 128] = out_at[at, 0, pl.ds(piece, quarter, stride=4), :]
            out_ref[0, goal, lane + 128 : lane + 192] = out_at[at, 1, pl.ds(piece, quarter, stride=4), :][:, 0:64]
        down_ref[0, at * units : (at + 1) * units, :] = hid_at[at, :, width : 2 * width]
    up = jnp.concatenate([hid_at[at, :, 0:width] for at in range(4)], axis=0)
    up_ref[0] = up.T
    bias = jnp.concatenate([hid_at[at, :, 2 * width :] for at in range(4)], axis=0).T[0:8]
    vectors = sum(part[:, 768:896].astype(F32) for part in attn).T[0:16]
    if not last:
        vec_ref[...] = vectors
        bias_ref[...] = bias
        return
    bias_out[0:1, :] = bias[0:1]
    bias_out[1:2, :] = other_bias[0:1, :]
    order = (((12, 0), (10, 0)), ((13, 0), (11, 0)), ((0, 0), (0, 1)), ((1, 0), (1, 1)), ((2, 0), (2, 1)), ((3, 0), (3, 1)))
    for target, picks in zip(vectors_out, order):
        for layer, (row, from_other) in enumerate(picks):
            source = other_vec[row : row + 1, :] if from_other else vectors[row : row + 1]
            target[layer : layer + 1, :] = source
    for half in range(2):
        lanes = slice(half * rows, (half + 1) * rows)
        qv_out[0:1, lanes] = vectors[8 + half : 9 + half]
        qv_out[1:2, lanes] = other_vec[8 + half : 9 + half, :]


def finish(info, layer, attn, hidden, before):
    rows, width = attn[0].shape[0], attn[0].shape[1] - 128
    units = hidden[0].shape[0]
    shapes = [
        (LAYERS, rows, 3 * width),
        (LAYERS, rows, width),
        (LAYERS, width, 4 * units),
        (LAYERS, 4 * units, width),
    ]
    specs = [pl.BlockSpec((1, *shape[1:]), lambda i, info: (layer, 0, 0)) for shape in shapes]
    last = before is not None
    more = [(LAYERS, rows)] * 6 + [(LAYERS, 2 * rows), (LAYERS, 4 * units)] if last else [(16, rows), (8, 4 * units)]
    given = [*before[4:6], *before[:4]] if last else []
    return pl.pallas_call(
        partial(finish_kernel, last),
        name="finish",
        grid_spec=pltpu.PrefetchScalarGridSpec(
            num_scalar_prefetch=1,
            grid=(1,),
            in_specs=[whole(attn[0].shape)] * 4
            + [whole(hidden[0].shape)] * 4
            + ([whole(v.shape) for v in given[:2]] + [HBM] * 4 if last else []),
            out_specs=specs + [whole(shape) for shape in more],
            scratch_shapes=[
                pltpu.VMEM((4, rows, 576), F32),
                pltpu.VMEM((4, 2, rows, 128), F32),
                pltpu.VMEM((4, units, 2 * width + 128), F32),
            ],
        ),
        out_shape=[jax.ShapeDtypeStruct(shape, F32) for shape in shapes + more],
        input_output_aliases={11 + at: at for at in range(4)} if last else {},
        compiler_params=pltpu.CompilerParams(vmem_limit_bytes=56 << 20),
        cost_estimate=pl.CostEstimate(flops=10**6, transcendentals=0, bytes_accessed=8 << 20),
    )(info, *attn, *hidden, *given)


PLANE = ("cx", "core", "tp")


def turned(value, first):
    pairs = []
    for x in range(2):
        for core in range(2):
            for y in range(2):
                flip_x = (core == 0) == first
                target = ((1 - x) if flip_x else x, core, y if flip_x else 1 - y)
                pairs.append((x * 4 + core * 2 + y, target[0] * 4 + target[1] * 2 + target[2]))
    return lax.ppermute(value, PLANE, pairs)


def after(value, *others):
    return lax.optimization_barrier((value, *others))[0]


def diagonal(value):
    return lax.ppermute(value, ("cx", "core"), ((0, 3), (1, 2), (2, 1), (3, 0)))


def around(own):
    far = swap(own, "cx")
    return own, swap(own, "core"), far, swap(far, "core")


def local(
    hidden_in,
    doc_lengths,
    ln1_gain,
    ln1_bias,
    qkv_weight,
    qv_bias,
    out_weight,
    out_bias,
    ln2_gain,
    ln2_bias,
    up_weight,
    up_bias,
    down_weight,
    down_bias,
    output_grad,
):
    shards = lax.axis_size("shard")
    ix, ic, iy = lax.axis_index("cx"), lax.axis_index("core"), lax.axis_index("tp")
    dev = ix * 2 + ic
    seqs, toks, width = hidden_in.shape
    rows = ln1_gain.shape[1]
    units = up_bias.shape[1] // 4
    loc = width // 4
    quarter = rows // 4

    def to_sequence(*arrays):
        given = jnp.stack([lax.dynamic_index_in_dim(array, 1 - iy, 0, keepdims=False) for array in arrays])
        given = swap(given, "tp")
        return [
            jnp.concatenate((lax.dynamic_index_in_dim(array, iy, 0, keepdims=False), other), axis=0)
            for array, other in zip(arrays, given)
        ]

    def own_first(own, other):
        return jnp.where(iy == 0, jnp.stack((own, other)), jnp.stack((other, own)))

    def from_sequence(tokens):
        return own_first(tokens[:toks], swap(tokens[toks:], "tp"))

    lengths = lax.dynamic_index_in_dim(doc_lengths, iy, 0, keepdims=False)
    end0 = lengths[0]
    end1 = end0 + lengths[1]
    end2 = end1 + lengths[2]
    info = jnp.stack((end0, end1, end2, dev, iy, ic * 2 + ix, dev, dev)).astype(jnp.int32)
    row_ids = jnp.arange(2 * toks, dtype=jnp.int32)
    places = dev * (2 * toks) + ((row_ids // toks) ^ iy) * toks + row_ids % toks
    keep = (places < end2).astype(F32)[:, None]

    def columns(array, start):
        return lax.dynamic_slice_in_dim(array, start, loc, 1)

    small = jnp.concatenate(
        [ln1_gain, ln1_bias, out_bias, ln2_gain, ln2_bias, down_bias, qv_bias.reshape(2 * LAYERS, rows)], axis=0
    )
    small = jnp.pad(small, ((0, 128 - small.shape[0]), (0, 0))).T

    def attention_piece(layer):
        weight = qkv_weight[layer]
        q, k, v = (columns(weight, which * width + loc * dev) for which in range(3))
        out = lax.dynamic_slice_in_dim(out_weight[layer], quarter * dev, quarter, 0).reshape(rows, loc)
        pieces = [k[:, :128], k[:, 128:], v[:, 128:], v[:, :128], q, out]
        if layer == 0:
            pieces.append(small)
        return jnp.concatenate(pieces, axis=1)

    def hidden_piece(layer):
        start = ic * 2 * units + ix * units
        up = lax.dynamic_slice_in_dim(up_weight[layer], start, units, 1).T
        down = lax.dynamic_slice_in_dim(down_weight[layer], start, units, 0)
        bias = lax.dynamic_slice_in_dim(up_bias[layer], start, units, 0)
        bias = jnp.broadcast_to(bias[:, None], (units, 128))
        return jnp.concatenate((up, down, bias), axis=1)

    def over_shards(piece):
        return lax.all_gather(piece, "shard", axis=0, tiled=True)

    def send_shards(value, count):
        if shards != 4:
            return ()
        index = lax.axis_index("shard")
        return tuple(
            lax.ppermute(
                lax.dynamic_slice_in_dim(value, (index + by) % shards * count, count, 0),
                "shard",
                [(i, (i + by) % shards) for i in range(shards)],
            )
            for by in range(1, shards)
        )

    def sum_shards(value, count, arriving):
        if shards != 4:
            return lax.psum_scatter(value, "shard", scatter_dimension=0, tiled=True)
        own = lax.dynamic_slice_in_dim(value, lax.axis_index("shard") * count, count, 0).astype(F32)
        return (own + sum(piece.astype(F32) for piece in arriving)).astype(value.dtype)

    def around_hidden(own, *others):
        core, far = swap(own, "core"), swap(own, "cx")
        return own, far, core, swap(after(far, *others), "core")

    hidden_own, raw_grad = to_sequence(hidden_in, output_grad)
    first_piece, attn_piece = hidden_piece(0), attention_piece(0)
    first_parts = around(after(hidden_own, first_piece, attn_piece))
    feed0 = over_shards(first_piece)
    attn0 = over_shards(after(attn_piece, feed0, *first_parts))
    feed_piece, attn_piece = hidden_piece(1), attention_piece(1)
    feed1 = over_shards(after(feed_piece, attn0))
    one0, two0 = turned(feed0, True), turned(feed0, False)

    def out_weights(own):
        full = jnp.zeros((shards, 4, quarter, width), BF16)
        for rel, part in enumerate(around(own)):
            full = lax.dynamic_update_slice(full, part, (0, dev ^ rel, 0, 0))
        return full.reshape(width, width)

    def out_own(gathered):
        return gathered[:, 3 * loc : 4 * loc].reshape(shards, 1, quarter, width)

    weights = []

    smalls = attn0[:, 4 * loc :].T.astype(F32)
    names = [[smalls[which * LAYERS + layer][None] for which in range(6)] for layer in range(LAYERS)]
    qv = smalls[6 * LAYERS : 8 * LAYERS].reshape(LAYERS, 2, shards, rows)
    qv = jnp.transpose(qv, (0, 2, 1, 3)).reshape(LAYERS, 2 * width)

    current = hidden_own.astype(F32)
    attn_parts = first_parts
    saved = []
    for layer in range(LAYERS):
        gain_one, bias_one, bias_out, gain_two, bias_two, bias_down = names[layer]
        w_qkv = attn0 if layer == 0 else attn1
        q_bias = lax.dynamic_slice_in_dim(qv[layer], loc * dev, loc, 0)
        v_bias = lax.dynamic_slice_in_dim(qv[layer], width + loc * dev, loc, 0)
        bias = jnp.concatenate((jnp.zeros((192,), F32), v_bias[128:], v_bias[:128], q_bias))[None]
        if layer == 0:
            one0, two0, attn_piece, *attn_parts = lax.optimization_barrier((one0, two0, attn_piece, *attn_parts))
            three0 = turned(one0, False)
            early_core = [swap(part, "core") for part in (feed0, one0, two0)]
        attn_t, qkv, attended, lse = attention_forward(info, attn_parts, w_qkv, bias, gain_one, bias_one, layer == 0)
        if layer == 0:
            attn1 = over_shards(after(attn_piece, attended))
            w_out = out_weights(out_own(attn0))
            attended, w_out, three0, *early_core = lax.optimization_barrier((attended, w_out, three0, *early_core))
            w_feed = (feed0, one0, two0, three0, *early_core, swap(three0, "core"))
        else:
            own, one, two, three = w_feed1
            early_core = (swap(own, "core"), swap(one, "core"))
            attended, w_out, own, one, two, three, *early_core = lax.optimization_barrier(
                (attended, w_out1, own, one, two, three, *early_core)
            )
        parts = (
            attended[0],
            swap(attended[1], "core"),
            swap(attended[2], "cx"),
            diagonal(attended[3]),
        )
        if layer == 1:
            late_core = [swap(after(part, *parts), "core") for part in (two, three)]
            low_grad = raw_grad * keep.astype(BF16)
            low_other = swap(low_grad, "core")
            w_feed = (own, one, two, three, *early_core, *late_core)
        vectors = jnp.concatenate((bias_out, gain_two, bias_two), axis=0)
        context, middle, mlp_in = out_forward(info, parts, w_out, current, vectors)
        if layer == 0:
            vectors = jnp.concatenate((bias_down, names[1][0], names[1][1]), axis=0)
            mlp_in, feed1 = lax.optimization_barrier((mlp_in, feed1))
            one1 = turned(feed1, True)
            slope, act, act_other, result, attn_own = feed_forward(mlp_in, middle, vectors, w_feed)
            act_other, mlp_other = swap(act_other, "core"), swap(mlp_in, "core")
            attn_own = after(attn_own, one1)
            attn_parts = around(attn_own)
            w_out1 = out_weights(out_own(after(attn1, attn_own)))
            w_out1, act_other, mlp_other, *attn_parts = lax.optimization_barrier(
                (w_out1, act_other, mlp_other, *attn_parts)
            )
            feed1, one1 = lax.optimization_barrier((feed1, one1, *attn_parts))[:2]
            w_feed1 = (feed1, one1, turned(feed1, False), turned(one1, False))
        else:
            slope = act = act_other = result = None
            mlp_other = swap(mlp_in, "core")
        weights.append((w_qkv, w_out, w_feed))
        saved.append((current, attn_t, qkv, attended, lse, context, middle, mlp_in, mlp_other, slope, act, act_other))
        current = result
    n = shards * units

    before = ()
    for layer in reversed(range(LAYERS)):
        x_in, attn_t, qkv, attended, lse, context, middle, mlp_in, mlp_other, slope, act, act_other = saved[layer]
        gain_one, _, _, gain_two, _, _ = names[layer]
        w_qkv, w_out, w_feed = weights[layer]
        if layer == 0:
            found = feed_backward(info, grad, low_grad, slope, middle, gain_two, w_out, w_feed)
        else:
            vectors = jnp.concatenate((names[1][5], gain_two), axis=0)
            *found, act, act_other, result = feed_both(info, mlp_in, low_grad, middle, vectors, w_out, w_feed)
            act_other = swap(act_other, "core")
        dh, dh_other, middle_grad, branch_grad, sums_two, d0, d1, d2, d3 = found
        attn_grads = (d0, swap(d1, "core"), swap(d2, "cx"), diagonal(d3))
        tokens = (mlp_in, mlp_other, low_grad, low_other)
        dh_other = swap(dh_other, "core")
        *attn_grads, dh_other = lax.optimization_barrier((*attn_grads, dh_other, *before))[:5]
        late = feed_weights(1, dh, dh_other, act, act_other, *tokens)
        w_out_grad = dot(context, branch_grad).astype(BF16).reshape(shards, 4, quarter, width)
        pieces = [lax.dynamic_index_in_dim(w_out_grad, dev ^ rel, 1, keepdims=False) for rel in range(4)]
        got = swap(jnp.stack((pieces[1], pieces[3])), "core")
        far = swap((pieces[2].astype(F32) + got[1].astype(F32)).astype(BF16), "cx")
        ready = [*attn_grads, late, far]
        if layer == 0:
            attn_sum1 = after(attn_sum1, *attn_grads)
            attn_sum1 = (attn_sum1.astype(F32) + swap(attn_sum1, "tp").astype(F32)).astype(BF16)
            ready.append(attn_sum1)
            early = feed_weights(0, dh, dh_other, act, act_other, *tokens)
            ready.append(early)
        *attn_grads, late, far = lax.optimization_barrier(tuple(ready))[:6]
        du, to_core, to_far, own, sums_u, *norm_sums = attention_backward(
            info, qkv, attended, lse, w_qkv, attn_grads, first_parts if layer == 0 else ()
        )
        late = turned(late, False)
        to_core = after(to_core, late)
        from_core = swap(to_core, "core")
        du_sum = sums_u[0]
        v_sum = jnp.concatenate((du_sum[256:384], du_sum[192:256]))
        q_row = lax.dynamic_update_slice_in_dim(jnp.zeros((width,), F32), du_sum[384:], loc * dev, 0)
        v_row = lax.dynamic_update_slice_in_dim(jnp.zeros((width,), F32), v_sum, loc * dev, 0)
        qv_rows = jnp.concatenate((q_row, v_row)).reshape(shards, 2, rows).transpose(1, 0, 2).reshape(2, width)
        vectors = jnp.concatenate((sums_two, qv_rows, jnp.zeros((6, width), F32)), axis=0)
        if layer == 0:
            vectors = jnp.concatenate((vectors[:10], sums_one[:2], norm_sums[0][:2], vectors[14:]), axis=0)
        flat = [piece.reshape(shards * quarter, width) for piece in (pieces[0], got[0], far)]
        if layer == 0:
            joined = attention_weights(attn_t, du, vectors, *flat)
            attn_sum = lax.psum_scatter(joined, "shard", scatter_dimension=0, tiled=True)
            to_far = after(to_far, joined)
        to_far = (to_far + from_core[1].astype(F32)).astype(BF16)
        if layer == 0:
            attn_sum1, feed_sum1 = lax.optimization_barrier((attn_sum1, feed_sum1, late))[:2]
            attn_parts1, hidden_parts1 = around(attn_sum1), around_hidden(feed_sum1)
            part = (early[n:].astype(F32) + after(late, joined)[n:].astype(F32)).astype(BF16)
            part = after(part, *attn_parts1, *hidden_parts1)
            early_late = late
            arrived = turned(part, True)
            to_far = after(to_far, arrived)
            done = finish(info, 1, attn_parts1, hidden_parts1, None)
        from_far = swap(to_far, "cx")
        if layer == 0:
            from_far = after(from_far, done[5])
        if layer > 0:
            du, dh_now, early_late = lax.optimization_barrier((du, dh, late, to_far))[:3]
            early = feed_weights(0, dh_now, dh_other, act, act_other, *tokens)
            part = (early[n:].astype(F32) + early_late[n:].astype(F32)).astype(BF16)
        if layer > 0:
            hidden_own_out = (after(result, to_far) * keep).astype(BF16)
            hidden_other_out = swap(hidden_own_out[toks:], "tp")
            from_far, part, hidden_other_out = lax.optimization_barrier((from_far, part, hidden_other_out))
            arrived = turned(part, True)
        grad, low_grad, sums_one = norm_backward(own, from_core, from_far, x_in, gain_one, middle_grad)
        if layer > 0:
            low_other = swap(low_grad, "core")
            joined = attention_weights(attn_t, after(du, low_grad), vectors, *flat)
            attn_sum1 = lax.psum_scatter(joined, "shard", scatter_dimension=0, tiled=True)
            grad, low_grad, arrived = lax.optimization_barrier((grad, low_grad, arrived, joined))[:3]
            part = early[:n].astype(F32) + early_late[:n].astype(F32) + arrived.astype(F32)
            part = part.astype(BF16)
            before = (part,)
            feed_sum1 = lax.psum_scatter(part, "shard", scatter_dimension=0, tiled=True)
        else:
            part = (early[:n].astype(F32) + late[:n].astype(F32) + arrived.astype(F32)).astype(BF16)
            arriving = send_shards(part, units)
            attn_sum = after(attn_sum, from_far)
            attn_sum = (attn_sum.astype(F32) + swap(attn_sum, "tp").astype(F32)).astype(BF16)
            attn_parts0 = around(attn_sum)
            arriving = lax.optimization_barrier((*arriving, low_grad))[: len(arriving)]
            feed_sum = sum_shards(part, units, arriving)
            hidden_out = own_first(hidden_own_out[:toks], after(hidden_other_out, part))

    hidden_grad = from_sequence(low_grad).astype(F32)

    done = finish(info, 0, attn_parts0, around_hidden(feed_sum), done)

    return (
        hidden_out,
        hidden_grad,
        done[4],
        done[5],
        done[0],
        done[10],
        done[1],
        done[8],
        done[6],
        done[7],
        done[2],
        done[11],
        done[3],
        done[9],
    )


def solution(mesh):
    names = tuple(mesh.axis_names)
    shape = dict(mesh.shape)
    split = Mesh(
        mesh.devices.reshape(shape[names[0]], 2, shape[names[1]] // 2, shape[names[2]]),
        ("shard", "cx", "core", "tp"),
    )
    tokens = P("shard", ("cx", "core", "tp"), None)
    vector = P(None, "shard")
    attn = P(None, "shard", None)
    placed = (
        tokens,
        P("shard", None),
        vector,
        vector,
        attn,
        vector,
        attn,
        vector,
        vector,
        vector,
        P(None, None, ("shard", "tp")),
        P(None, ("shard", "tp")),
        P(None, ("shard", "tp"), None),
        vector,
        tokens,
    )
    return jax.shard_map(
        local,
        mesh=split,
        in_specs=placed,
        out_specs=(
            tokens,
            tokens,
            vector,
            vector,
            attn,
            vector,
            attn,
            vector,
            vector,
            vector,
            P(None, None, ("shard", "tp")),
            P(None, ("shard", "tp")),
            P(None, ("shard", "tp"), None),
            vector,
        ),
        check_vma=False,
    )
```

```python
from functools import partial, reduce

import jax
import jax.numpy as jnp
from jax import lax
from jax.experimental import pallas as pl
from jax.experimental.pallas import tpu as pltpu
from jax.sharding import Mesh
from jax.sharding import PartitionSpec as P

HEADS = 12
HEAD = 64
LAYERS = 2
BLK = 256
NEG = -1e30
EPS = 1e-06
F32 = jnp.float32
BF16 = jnp.bfloat16


def dot(left, right, dims=((1,), (0,))):
    return lax.dot_general(left, right, (dims, ((), ())), preferred_element_type=F32)


def swap(value, axis):
    return lax.ppermute(value, axis, ((0, 1), (1, 0)))


def block_place(block, dev, half):
    return (((block // 2) ^ dev) * 2) + ((block % 2) ^ half)


def doc_range(first, ends, length):
    last = first + BLK - 1
    start, stop = jnp.int32(0), jnp.int32(length)
    for end in ends:
        start = jnp.maximum(start, jnp.where(first >= end, end, 0))
        stop = jnp.minimum(stop, jnp.where(last < end, end, length))
    return start // BLK, (stop + BLK - 1) // BLK


def seg_of(places, ends):
    seg = (places >= ends[0]).astype(jnp.int32)
    for end in ends[1:]:
        seg = seg + (places >= end).astype(jnp.int32)
    return seg


def three_heads(pair, single):
    blank = jnp.zeros_like(single)
    return (
        jnp.concatenate((pair[:HEAD], blank), axis=0),
        jnp.concatenate((blank, pair[HEAD:]), axis=0),
        jnp.concatenate((single, blank), axis=0),
    )


def norm_rows(rows, gain, bias):
    centred = rows - jnp.mean(rows, axis=-1, keepdims=True)
    inv_std = lax.rsqrt(jnp.mean(centred * centred, axis=-1, keepdims=True) + EPS)
    return centred * inv_std * gain + bias


def whole(shape):
    return pl.BlockSpec(shape, lambda *at: (0,) * len(shape))


HBM = pl.BlockSpec(memory_space=pl.ANY)


def attention_forward_kernel(norm, info, *refs):
    parts, (w_ref, bias_ref, gain_ref, shift_ref) = refs[:4], refs[4:8]
    at_out, qkv_out, out_ref, lse_ref = refs[8:12]
    if norm:
        n_out = refs[12]
    a_ref, at_ref, qkv_ref, v_t, sems, out_sems = refs[13:19] if norm else refs[12:18]
    length = qkv_ref.shape[0]
    ends = (info[0], info[1], info[2])
    dev, half = info[3], info[4]
    each = parts[0].shape[0]
    copies = [pltpu.make_async_copy(part, a_ref.at[at], sems.at[at]) for at, part in enumerate(parts)]
    for copy in copies:
        copy.start()
    for part in range(4):
        copies[part].wait()

        def project(at, nothing):
            rows = pl.ds(pl.multiple_of(at * BLK, BLK), BLK)
            goal = pl.ds(pl.multiple_of(part * each + at * BLK, BLK), BLK)
            values = a_ref[part, rows, :]
            if norm:
                normed = norm_rows(values.astype(F32), 1.0, 0.0)
                a_ref[part, rows, :] = normed.astype(BF16)
                values = (normed * gain_ref[...] + shift_ref[...]).astype(BF16)
            found = dot(values, w_ref[:, 0:576]) + bias_ref[...]
            at_ref[:, goal] = values.T
            qkv_ref[goal, 0:384] = found[:, 0:384].astype(BF16)
            qkv_ref[goal, 384:576] = (found[:, 384:576] * HEAD**-0.5).astype(BF16)
            pair = qkv_ref[goal, 256:384].T
            ones = jnp.ones((16, BLK), BF16)
            for head, found in enumerate((pair[:HEAD], pair[HEAD:], qkv_ref[goal, 128:256].T[HEAD:])):
                v_t[head, 0:HEAD, goal] = found
                v_t[head, HEAD : HEAD + 16, goal] = ones
            return nothing

        lax.fori_loop(0, each // BLK, project, 0)
    out_copies = [
        pltpu.make_async_copy(at_ref, at_out, out_sems.at[0]),
        pltpu.make_async_copy(qkv_ref, qkv_out, out_sems.at[1]),
    ]
    if norm:
        out_copies.append(pltpu.make_async_copy(a_ref, n_out, out_sems.at[2]))
    for copy in out_copies:
        copy.start()

    blocks = length // BLK
    lse_ref[...] = jnp.zeros_like(lse_ref)

    def per_block(step, nothing):
        mine = pl.ds(pl.multiple_of(step * BLK, BLK), BLK)
        first = block_place(step, dev, half) * BLK
        seg_q = seg_of(first + lax.broadcasted_iota(jnp.int32, (1, BLK), 1), ends)
        queries = three_heads(qkv_ref[mine, 384:512].T, qkv_ref[mine, 512:576].T)
        low, high = doc_range(first, ends, length)

        def body(count, begin, at, carry):
            tiles = []
            for more in range(count):
                block = begin + count * at + more
                place = block_place(block, dev, half)
                rows = pl.ds(pl.multiple_of(place * BLK, BLK), BLK)
                places = block * BLK + lax.broadcasted_iota(jnp.int32, (BLK, 1), 0)
                tiles.append((rows, seg_of(places, ends) == seg_q))

            def score(head):
                lanes = slice(128, 256) if head == 2 else slice(0, 128)
                return [jnp.where(allowed, dot(qkv_ref[rows, lanes], queries[head]), NEG) for rows, allowed in tiles]

            def weigh(head, scores):
                top, acc = carry[head]
                new_top = jnp.maximum(top, jnp.max(reduce(jnp.maximum, scores), axis=0, keepdims=True))
                shrink = jnp.exp(top - new_top)
                exps = [jnp.exp(one - new_top) for one in scores]
                return new_top, acc * shrink, [exp.astype(BF16) for exp in exps]

            def gather(head, weighed):
                top, acc, exps = weighed
                for (rows, _), exp in zip(tiles, exps):
                    acc = acc + dot(v_t[head, :, rows], exp)
                return top, acc

            s0 = score(0)
            s1 = score(1)
            w0 = weigh(0, s0)
            s2 = score(2)
            w1 = weigh(1, s1)
            r0 = gather(0, w0)
            w2 = weigh(2, s2)
            r1 = gather(1, w1)
            r2 = gather(2, w2)
            return r0, r1, r2

        start = tuple(
            (
                jnp.full((1, BLK), NEG, F32),
                jnp.zeros((HEAD + 16, BLK), F32),
            )
            for _ in range(3)
        )
        pairs, odd = (high - low) // 2, (high - low) % 2
        final = lax.fori_loop(0, pairs, partial(body, 2, low), start)
        final = lax.fori_loop(0, odd, partial(body, 1, high - 1), final)
        cols = pl.ds(pl.multiple_of((step % 2) * BLK, BLK), BLK)
        for head in range(3):
            top, acc = final[head]
            total = acc[HEAD : HEAD + 1]
            out_ref[step // 2, head * HEAD : (head + 1) * HEAD, cols] = (acc[:HEAD] / total).astype(BF16)
            lse_ref[head : head + 1, mine] = top + jnp.log(total)
        return nothing

    lax.fori_loop(0, blocks, per_block, 0)
    for copy in out_copies:
        copy.wait()


def attention_forward(info, parts, w_qkv, bias, gain, shift, norm):
    each, width = parts[0].shape
    length = 4 * each
    return pl.pallas_call(
        partial(attention_forward_kernel, norm),
        name="attention_forward",
        grid_spec=pltpu.PrefetchScalarGridSpec(
            num_scalar_prefetch=1,
            grid=(1,),
            in_specs=[HBM] * 4 + [whole(w_qkv.shape), whole(bias.shape), whole(gain.shape), whole(shift.shape)],
            out_specs=[HBM, HBM, whole((4, 192, each)), whole((8, length))] + [HBM] * norm,
            scratch_shapes=[
                pltpu.VMEM((4, each, width), BF16),
                pltpu.VMEM((width, length), BF16),
                pltpu.VMEM((length, 576), BF16),
                pltpu.VMEM((3, HEAD + 16, length), BF16),
                pltpu.SemaphoreType.DMA((4,)),
                pltpu.SemaphoreType.DMA((3,)),
            ],
        ),
        out_shape=(
            jax.ShapeDtypeStruct((width, length), BF16),
            jax.ShapeDtypeStruct((length, 576), BF16),
            jax.ShapeDtypeStruct((4, 192, each), BF16),
            jax.ShapeDtypeStruct((8, length), F32),
        )
        + (jax.ShapeDtypeStruct((4, each, width), BF16),) * norm,
        compiler_params=pltpu.CompilerParams(vmem_limit_bytes=48 << 20),
        cost_estimate=pl.CostEstimate(
            flops=14 * 10**9, transcendentals=3 * length * 1024, bytes_accessed=12 << 20
        ),
    )(info, *parts, w_qkv, bias, gain, shift)


def attention_backward_kernel(norm, info, qkv_ref, out_ref, lse_ref, w_ref, g0, g1, g2, g3, *refs):
    if norm:
        tokens, refs = refs[0], refs[1:]
        norm_sums, refs = refs[5], refs[:5] + refs[6:]
        x_ref, da_ref, x_sems = refs[-3:]
        token_copies = [pltpu.make_async_copy(tokens, x_ref, x_sems.at[0])]
        for copy in token_copies:
            copy.start()
        refs = refs[:-3]
    du_out, core_out, far_out, own_out, sums_ref = refs[:5]
    q01_t, q2_t, delta, dq_t, grad_t, du_ref, core_ref, far_ref, own_ref, sems = refs[5:]
    length = qkv_ref.shape[0]
    each = length // 4
    ends = (info[0], info[1], info[2])
    dev, half = info[3], info[4]
    blocks = length // BLK
    q01_t[...] = qkv_ref[:, 384:512].T
    q2_t[...] = qkv_ref[:, 512:576].T
    dq_t[...] = jnp.zeros_like(dq_t)
    for part, grad in enumerate((g0, g1, g2, g3)):
        grad_t[part] = grad[...]
        for head in range(3):
            rows = slice(head * HEAD, (head + 1) * HEAD)
            both = out_ref[part, rows].astype(F32) * grad[rows].astype(F32)
            delta[head : head + 1, part * each : (part + 1) * each] = jnp.sum(both, axis=0, keepdims=True)

    def per_block(step, nothing):
        mine = pl.ds(pl.multiple_of(step * BLK, BLK), BLK)
        first = block_place(step, dev, half) * BLK
        seg_k = seg_of(first + lax.broadcasted_iota(jnp.int32, (BLK, 1), 0), ends)
        k01 = qkv_ref[mine, 0:128]
        k2v2 = qkv_ref[mine, 128:256]
        v01 = qkv_ref[mine, 256:384]
        k01_t = k01.T
        k2_t = k2v2.T[:HEAD]
        keys_t = (k01_t[:HEAD], k01_t[HEAD:], k2_t)
        low, high = doc_range(first, ends, length)

        def body(width, begin, at, carry):
            blank = jnp.zeros((HEAD, BLK), BF16)
            tiles = []
            for more in range(width):
                block = begin + width * at + more
                place = block_place(block, dev, half)
                cols = pl.ds(pl.multiple_of(place * BLK, BLK), BLK)
                part_cols = pl.ds(pl.multiple_of((place % 2) * BLK, BLK), BLK)
                places = block * BLK + lax.broadcasted_iota(jnp.int32, (1, BLK), 1)
                allowed = seg_k == seg_of(places, ends)
                queries = three_heads(q01_t[:, cols], q2_t[:, cols])
                grads = grad_t[place // 2, :, part_cols]
                dos = (
                    jnp.concatenate((grads[:HEAD], blank), axis=0),
                    jnp.concatenate((blank, grads[HEAD:128]), axis=0),
                    jnp.concatenate((blank, grads[128:192]), axis=0),
                )
                tiles.append((cols, allowed, queries, dos))

            def first_dots(at):
                cols, allowed, queries, dos = tiles[at // 3]
                head = at % 3
                return (
                    dot(k2v2 if head == 2 else k01, queries[head]),
                    dot(k2v2 if head == 2 else v01, dos[head]),
                )

            def weigh(at, found):
                cols, allowed, queries, dos = tiles[at // 3]
                head = at % 3
                scores, grad_probs = found
                probs = jnp.where(allowed, jnp.exp(scores - lse_ref[head : head + 1, cols]), 0.0)
                grad_scores = (probs * (grad_probs - delta[head : head + 1, cols])).astype(BF16)
                return probs.astype(BF16), grad_scores

            def last_dots(at, found, sums):
                cols, allowed, queries, dos = tiles[at // 3]
                head = at % 3
                probs, grad_scores = found
                more_k = dot(grad_scores, queries[head], ((1,), (1,)))
                more_v = dot(probs, dos[head], ((1,), (1,)))
                more_q = dot(keys_t[head], grad_scores)
                dk01, dk2v2, dv01 = sums
                if head == 2:
                    dk2v2 = dk2v2 + more_k + more_v
                else:
                    dk01 = dk01 + more_k
                    dv01 = dv01 + more_v
                return (dk01, dk2v2, dv01), more_q

            count = 3 * width
            sums = carry
            more_q = []
            begun = {0: first_dots(0), 1: first_dots(1)}
            weighed = {}
            for at in range(count):
                if at + 2 < count:
                    begun[at + 2] = first_dots(at + 2)
                weighed[at] = weigh(at, begun[at])
                if at > 0:
                    sums, found = last_dots(at - 1, weighed[at - 1], sums)
                    more_q.append(found)
            sums, found = last_dots(count - 1, weighed[count - 1], sums)
            more_q.append(found)
            for tile in range(width):
                cols = tiles[tile][0]
                dq_t[:, cols] = dq_t[:, cols] + jnp.concatenate(more_q[3 * tile : 3 * tile + 3], axis=0)
            return sums

        zero = jnp.zeros((BLK, 128), F32)
        pairs, odd = (high - low) // 2, (high - low) % 2
        sums = lax.fori_loop(0, pairs, partial(body, 2, low), (zero, zero, zero))
        dk01, dk2v2, dv01 = lax.fori_loop(0, odd, partial(body, 1, high - 1), sums)
        du_ref[mine, 0:128] = dk01.astype(BF16)
        du_ref[mine, 128:256] = dk2v2.astype(BF16)
        du_ref[mine, 256:384] = dv01.astype(BF16)
        return nothing

    lax.fori_loop(0, blocks, per_block, 0)
    sums_ref[...] = jnp.zeros_like(sums_ref)
    scale = HEAD**-0.5

    def finish_rows(at, total):
        rows = pl.ds(pl.multiple_of(at * BLK, BLK), BLK)
        du_ref[rows, 384:512] = (dq_t[0:128, rows] * scale).T.astype(BF16)
        du_ref[rows, 512:576] = (dq_t[128:192, rows] * scale).T.astype(BF16)
        return total + jnp.sum(du_ref[rows, :].astype(F32), axis=0, keepdims=True)

    sums_ref[0:1, :] = lax.fori_loop(0, blocks, finish_rows, jnp.zeros((1, 576), F32))
    copies = [pltpu.make_async_copy(du_ref, du_out, sems.at[0])]
    copies[0].start()
    plan = ((1, core_ref.at[0], core_out.at[0]), (3, core_ref.at[1], core_out.at[1]), (2, far_ref, far_out), (0, own_ref, own_out))
    if norm:
        for copy in token_copies:
            copy.wait()
        width = da_ref.shape[1]
        totals = (jnp.zeros((1, width), F32), jnp.zeros((1, width), F32))
    for at, (part, target, goal) in enumerate(plan):
        kind = target.dtype
        found = dot(du_ref[part * each : (part + 1) * each, :], w_ref[:, 0:576], ((1,), (1,)))
        if norm:
            da_ref[...] = found

            def rows_of(step, sums, part=part):
                rows = pl.ds(pl.multiple_of(step * 128, 128), 128)
                grad = da_ref[rows, :]
                normed = x_ref[part, rows, :].astype(F32)
                return (
                    sums[0] + jnp.sum(grad * normed, axis=0, keepdims=True),
                    sums[1] + jnp.sum(grad, axis=0, keepdims=True),
                )

            totals = lax.fori_loop(0, each // 128, rows_of, totals)
            found = da_ref[...]
        target[...] = found.astype(kind)
        copies.append(pltpu.make_async_copy(target, goal, sems.at[at + 1]))
        copies[-1].start()
    if norm:
        norm_sums[...] = jnp.zeros_like(norm_sums)
        norm_sums[0:1, :] = totals[0]
        norm_sums[1:2, :] = totals[1]
    for copy in copies:
        copy.wait()


def attention_backward(info, qkv, out, lse, w_qkv, grads, tokens=()):
    norm = len(tokens) > 0
    length, each, width = qkv.shape[0], qkv.shape[0] // 4, w_qkv.shape[0]
    return pl.pallas_call(
        partial(attention_backward_kernel, norm),
        name="attention_backward",
        grid_spec=pltpu.PrefetchScalarGridSpec(
            num_scalar_prefetch=1,
            grid=(1,),
            in_specs=[whole(qkv.shape), whole(out.shape), whole(lse.shape), whole(w_qkv.shape)]
            + [whole((192, each))] * 4
            + [HBM] * len(tokens),
            out_specs=[HBM, HBM, HBM, HBM, whole((8, 576))] + [whole((8, width))] * norm,
            scratch_shapes=[
                pltpu.VMEM((128, length), BF16),
                pltpu.VMEM((64, length), BF16),
                pltpu.VMEM((8, length), F32),
                pltpu.VMEM((192, length), F32),
                pltpu.VMEM((4, 192, each), BF16),
                pltpu.VMEM((length, 576), BF16),
                pltpu.VMEM((2, each, width), BF16),
                pltpu.VMEM((each, width), F32),
                pltpu.VMEM((each, width), F32),
                pltpu.SemaphoreType.DMA((5,)),
            ]
            + [pltpu.VMEM((4, each, width), BF16), pltpu.VMEM((each, width), F32), pltpu.SemaphoreType.DMA((1,))] * norm,
        ),
        out_shape=(
            jax.ShapeDtypeStruct(qkv.shape, BF16),
            jax.ShapeDtypeStruct((2, each, width), BF16),
            jax.ShapeDtypeStruct((each, width), F32),
            jax.ShapeDtypeStruct((each, width), F32),
            jax.ShapeDtypeStruct((8, 576), F32),
        )
        + (jax.ShapeDtypeStruct((8, width), F32),) * norm,
        compiler_params=pltpu.CompilerParams(vmem_limit_bytes=56 << 20),
        cost_estimate=pl.CostEstimate(
            flops=20 * 10**9, transcendentals=3 * length * 1024, bytes_accessed=16 << 20
        ),
    )(info, qkv, out, lse, w_qkv, *grads, *tokens)


def attention_weights_kernel(at_ref, du_ref, vec_ref, own_ref, core_ref, far_ref, out_ref, spread):
    blank = jnp.zeros((128 - vec_ref.shape[0], vec_ref.shape[1]), F32)
    out_ref[:, 768:896] = jnp.concatenate((vec_ref[...], blank), axis=0).T.astype(BF16)
    out_ref[:, 0:576] = dot(at_ref[...], du_ref[...]).astype(BF16)
    total = own_ref[...].astype(F32) + core_ref[...].astype(F32) + far_ref[...].astype(F32)
    quarter = own_ref.shape[0]
    for piece in range(4):
        rows = pl.ds(piece, quarter, stride=4)
        spread[0, rows, :] = total[:, piece * 192 : piece * 192 + 128]
        spread[1, rows, :] = jnp.concatenate(
            (total[:, piece * 192 + 128 : (piece + 1) * 192], jnp.zeros((quarter, 64), F32)), axis=1
        )
    out_ref[:, 576:704] = spread[0].astype(BF16)
    out_ref[:, 704:768] = spread[1, :, 0:64].astype(BF16)


def attention_weights(a_t, du, vectors, own, core, far):
    width = a_t.shape[0]
    return pl.pallas_call(
        attention_weights_kernel,
        name="attention_weights",
        grid=(1,),
        in_specs=[whole(v.shape) for v in (a_t, du, vectors, own, core, far)],
        out_specs=whole((width, width + 128)),
        out_shape=jax.ShapeDtypeStruct((width, width + 128), BF16),
        scratch_shapes=[pltpu.VMEM((2, width, 128), F32)],
        compiler_params=pltpu.CompilerParams(vmem_limit_bytes=48 << 20),
        cost_estimate=pl.CostEstimate(flops=18 * 10**8, transcendentals=0, bytes_accessed=8 << 20),
    )(a_t, du, vectors, own, core, far)


def out_kernel(info, p0, p1, p2, p3, w_ref, x_ref, vec_ref, ctx_ref, mid_ref, c_ref, ctx):
    dev = info[3]
    loc, toks = p0.shape
    for rel, part in enumerate((p0, p1, p2, p3)):
        ctx[dev ^ rel] = part[...]
    ctx_ref[...] = ctx[...].reshape(4 * loc, toks)

    def rows_of(at, nothing):
        rows = pl.ds(pl.multiple_of(at * 128, 128), 128)
        found = dot(ctx_ref[:, rows].T, w_ref[...])
        middle = x_ref[rows, :] + found + vec_ref[0:1, :]
        mid_ref[rows, :] = middle
        c_ref[rows, :] = norm_rows(middle, vec_ref[1:2, :], vec_ref[2:3, :]).astype(BF16)
        return nothing

    lax.fori_loop(0, toks // 128, rows_of, 0)


def out_forward(info, parts, w_out, current, vectors):
    loc, toks = parts[0].shape
    width = w_out.shape[1]
    return pl.pallas_call(
        out_kernel,
        name="out_forward",
        grid_spec=pltpu.PrefetchScalarGridSpec(
            num_scalar_prefetch=1,
            grid=(1,),
            in_specs=[whole((loc, toks))] * 4 + [whole(w_out.shape), whole(current.shape), whole(vectors.shape)],
            out_specs=[whole((width, toks)), whole((toks, width)), whole((toks, width))],
            scratch_shapes=[pltpu.VMEM((4, loc, toks), BF16)],
        ),
        out_shape=(
            jax.ShapeDtypeStruct((width, toks), BF16),
            jax.ShapeDtypeStruct((toks, width), F32),
            jax.ShapeDtypeStruct((toks, width), BF16),
        ),
        compiler_params=pltpu.CompilerParams(vmem_limit_bytes=48 << 20),
        cost_estimate=pl.CostEstimate(flops=10**9, transcendentals=0, bytes_accessed=7 << 20),
    )(info, *parts, w_out, current, vectors)


def norm_back(grad, values, gain):
    centred = values - jnp.mean(values, axis=-1, keepdims=True)
    inv_std = lax.rsqrt(jnp.mean(centred * centred, axis=-1, keepdims=True) + EPS)
    normed = centred * inv_std
    scaled = grad * gain
    grad_in = inv_std * (
        scaled
        - jnp.mean(scaled, axis=-1, keepdims=True)
        - normed * jnp.mean(scaled * normed, axis=-1, keepdims=True)
    )
    return grad_in, jnp.sum(grad * normed, axis=0, keepdims=True), jnp.sum(grad, axis=0, keepdims=True)


def norm_back_kernel(own, core, far, x_ref, gain_ref, mid_ref, grad_ref, low_ref, sums_ref):
    toks, width = x_ref.shape
    step = pl.program_id(0)

    @pl.when(step == 0)
    def _():
        sums_ref[...] = jnp.zeros_like(sums_ref)

    def rows_of(at, sums):
        rows = pl.ds(pl.multiple_of(at * 64, 64), 64)
        found = own[rows, :] + core[0, rows, :].astype(F32) + far[rows, :].astype(F32)
        grad_in, gain_sum, bias_sum = norm_back(found, x_ref[rows, :], gain_ref[...])
        grad = mid_ref[rows, :] + grad_in
        grad_ref[rows, :] = grad
        low_ref[rows, :] = grad.astype(BF16)
        return sums[0] + gain_sum, sums[1] + bias_sum

    zero = jnp.zeros((1, width), F32)
    sums = lax.fori_loop(0, toks // 64, rows_of, (zero, zero))
    sums_ref[0:1, :] += sums[0]
    sums_ref[1:2, :] += sums[1]


def norm_backward(own, core, far, values, gain, middle_grad):
    toks, width = values.shape
    rows = pl.BlockSpec((toks // 4, width), lambda i: (i, 0))
    return pl.pallas_call(
        norm_back_kernel,
        name="norm_backward",
        grid=(4,),
        in_specs=[rows, pl.BlockSpec((1, toks // 4, width), lambda i: (0, i, 0)), rows, rows, whole(gain.shape), rows],
        out_specs=[rows, rows, whole((8, width))],
        out_shape=(
            jax.ShapeDtypeStruct((toks, width), F32),
            jax.ShapeDtypeStruct((toks, width), BF16),
            jax.ShapeDtypeStruct((8, width), F32),
        ),
        compiler_params=pltpu.CompilerParams(vmem_limit_bytes=48 << 20),
        cost_estimate=pl.CostEstimate(flops=10**7, transcendentals=0, bytes_accessed=9 << 20),
    )(own, core, far, values, gain, middle_grad)


GELU_A = (2.0 / 3.141592653589793) ** 0.5
GELU_B = 0.044715


def gelu(t):
    square = t * t
    tanh = jnp.tanh(t * (GELU_A + GELU_A * GELU_B * square))
    half = 0.5 * t
    side = 0.5 + 0.5 * tanh
    slope = side + (half - half * tanh * tanh) * (GELU_A + 3.0 * GELU_A * GELU_B * square)
    return t * side, slope


def fetch(parts, held, sems):
    units = parts[0].shape[0]
    copies = [
        pltpu.make_async_copy(part, held.at[at // 2, pl.ds((at % 2) * units, units)], sems.at[at])
        for at, part in enumerate(parts)
    ]
    for copy in copies:
        copy.start()
    return copies


def feed_kernel(c_ref, mid_ref, vec_ref, *refs):
    parts, refs = refs[:8], refs[8:]
    slope_out, own_out, other_out, x_ref, a_ref, slope_ref, act_ref, held, sems, out_sems = refs
    toks, width = mid_ref.shape
    copies = fetch(parts, held, sems)
    x_ref[...] = mid_ref[...] + vec_ref[0:1, :]
    outs = []

    def before(at):
        copies[2 * at].wait()
        copies[2 * at + 1].wait()
        bias = held[at, :, 2 * width : 2 * width + 128].T[0:1].astype(F32)
        return dot(c_ref[...], held[at, :, 0:width], ((1,), (1,))) + bias

    def after(at, pre):
        act, slope = gelu(pre)
        act = act.astype(BF16)
        slope_ref[at] = slope.astype(BF16)
        act_ref[at] = act.T
        outs.append(pltpu.make_async_copy(slope_ref.at[at], slope_out.at[at], out_sems.at[2 * at]))
        goal = (own_out, other_out)[at // 2].at[at % 2]
        outs.append(pltpu.make_async_copy(act_ref.at[at], goal, out_sems.at[2 * at + 1]))
        outs[-2].start()
        outs[-1].start()
        x_ref[...] += dot(act, held[at, :, width : 2 * width])

    pre = before(0)
    for at in range(4):
        later = before(at + 1) if at < 3 else None
        after(at, pre)
        pre = later

    def rows_of(at, nothing):
        rows = pl.ds(pl.multiple_of(at * 64, 64), 64)
        a_ref[rows, :] = norm_rows(x_ref[rows, :], vec_ref[1:2, :], vec_ref[2:3, :]).astype(BF16)
        return nothing

    lax.fori_loop(0, toks // 64, rows_of, 0)
    for copy in outs:
        copy.wait()


def feed_forward(c, middle, vectors, parts):
    toks, width = middle.shape
    units = 2 * parts[0].shape[0]
    return pl.pallas_call(
        feed_kernel,
        name="feed_forward",
        grid=(1,),
        in_specs=[whole(c.shape), whole(middle.shape), whole(vectors.shape)] + [HBM] * 8,
        out_specs=[HBM, HBM, HBM, whole((toks, width)), whole((toks, width))],
        out_shape=[
            jax.ShapeDtypeStruct((4, toks, units), BF16),
            jax.ShapeDtypeStruct((2, units, toks), BF16),
            jax.ShapeDtypeStruct((2, units, toks), BF16),
            jax.ShapeDtypeStruct((toks, width), F32),
            jax.ShapeDtypeStruct((toks, width), BF16),
        ],
        scratch_shapes=[
            pltpu.VMEM((4, toks, units), BF16),
            pltpu.VMEM((4, units, toks), BF16),
            pltpu.VMEM((4, units, parts[0].shape[1]), BF16),
            pltpu.SemaphoreType.DMA((8,)),
            pltpu.SemaphoreType.DMA((8,)),
        ],
        compiler_params=pltpu.CompilerParams(vmem_limit_bytes=56 << 20),
        cost_estimate=pl.CostEstimate(flops=5 * 10**9, transcendentals=2 * 10**6, bytes_accessed=20 << 20),
    )(c, middle, vectors, *parts)


def finish_back(dev, grad_ref, mid_ref, gain_ref, w_ref, dm_ref, dc, dmid_ref, da_ref, sums_ref, targets):
    toks, width = mid_ref.shape
    loc = targets[0].shape[0]

    def rows_of(at, sums):
        rows = pl.ds(pl.multiple_of(at * 64, 64), 64)
        grad_in, gain_sum, bias_sum = norm_back(dc[rows, :], mid_ref[rows, :], gain_ref[...])
        grad_mid = grad_ref[rows, :].astype(F32) + grad_in
        dmid_ref[rows, :] = grad_mid
        branch = grad_mid.astype(BF16)
        da_ref[rows, :] = branch
        out_sum = jnp.sum(branch.astype(F32), axis=0, keepdims=True)
        down_sum = jnp.sum(dm_ref[rows, :].astype(F32), axis=0, keepdims=True)
        return sums[0] + gain_sum, sums[1] + bias_sum, sums[2] + out_sum, sums[3] + down_sum

    zero = jnp.zeros((1, width), F32)
    sums = lax.fori_loop(0, toks // 64, rows_of, (zero,) * 4)
    sums_ref[...] = jnp.zeros_like(sums_ref)
    for at in range(4):
        sums_ref[at : at + 1, :] = sums[at]
    for rel, target in enumerate(targets):
        rows = pl.ds(pl.multiple_of((dev ^ rel) * loc, 64), loc)
        target[...] = dot(w_ref[rows, :], da_ref[...], ((1,), (1,))).astype(BF16)


def back_outputs(toks, width, units):
    return [
        jax.ShapeDtypeStruct((2, toks, units), BF16),
        jax.ShapeDtypeStruct((2, toks, units), BF16),
        jax.ShapeDtypeStruct((toks, width), F32),
        jax.ShapeDtypeStruct((toks, width), BF16),
        jax.ShapeDtypeStruct((8, width), F32),
    ] + [jax.ShapeDtypeStruct((width // 4, toks), BF16)] * 4


def feed_back_kernel(info, grad_ref, dm_ref, slope_in, mid_in, gain_ref, w_in, *refs):
    parts, refs = refs[:8], refs[8:]
    own_out, other_out, dmid_ref, da_ref, sums_ref, *targets = refs[:9]
    slope_ref, dh_ref, held, dc, mid_ref, w_ref, sems, slope_sems, out_sems, in_sems = refs[9:]
    width = mid_ref.shape[1]
    copies = fetch(parts, held, sems)
    slopes = [pltpu.make_async_copy(slope_in.at[at], slope_ref.at[at], slope_sems.at[at]) for at in range(4)]
    late_in = [pltpu.make_async_copy(mid_in, mid_ref, in_sems.at[0]), pltpu.make_async_copy(w_in, w_ref, in_sems.at[1])]
    for copy in slopes + late_in:
        copy.start()
    outs = []
    goals = (own_out.at[0], own_out.at[1], other_out.at[0], other_out.at[1])

    def before(at):
        copies[2 * at].wait()
        copies[2 * at + 1].wait()
        return dot(dm_ref[...], held[at, :, width : 2 * width], ((1,), (1,)))

    def after(at, dact):
        slopes[at].wait()
        dpre = (dact * slope_ref[at].astype(F32)).astype(BF16)
        dh_ref[at] = dpre
        outs.append(pltpu.make_async_copy(dh_ref.at[at], goals[at], out_sems.at[at]))
        outs[-1].start()
        term = dot(dpre, held[at, :, 0:width])
        if at == 0:
            dc[...] = term
        else:
            dc[...] += term

    dact = before(0)
    for at in range(4):
        later = before(at + 1) if at < 3 else None
        after(at, dact)
        dact = later
    for copy in late_in:
        copy.wait()
    finish_back(info[3], grad_ref, mid_ref, gain_ref, w_ref, dm_ref, dc, dmid_ref, da_ref, sums_ref, targets)
    for copy in outs:
        copy.wait()


def feed_backward(info, grad, dm, slope, middle, gain, w_out, parts):
    toks, width = middle.shape
    units = 2 * parts[0].shape[0]
    shapes = back_outputs(toks, width, units)
    return pl.pallas_call(
        feed_back_kernel,
        name="feed_backward",
        grid_spec=pltpu.PrefetchScalarGridSpec(
            num_scalar_prefetch=1,
            grid=(1,),
            in_specs=[whole(grad.shape), whole(dm.shape), HBM, HBM, whole(gain.shape), HBM] + [HBM] * 8,
            out_specs=[HBM] * 2 + [whole(shape.shape) for shape in shapes[2:]],
            scratch_shapes=[
                pltpu.VMEM((4, toks, units), BF16),
                pltpu.VMEM((4, toks, units), BF16),
                pltpu.VMEM((4, units, parts[0].shape[1]), BF16),
                pltpu.VMEM((toks, width), F32),
                pltpu.VMEM((toks, width), F32),
                pltpu.VMEM((width, width), BF16),
                pltpu.SemaphoreType.DMA((8,)),
                pltpu.SemaphoreType.DMA((4,)),
                pltpu.SemaphoreType.DMA((4,)),
                pltpu.SemaphoreType.DMA((2,)),
            ],
        ),
        out_shape=shapes,
        compiler_params=pltpu.CompilerParams(vmem_limit_bytes=60 << 20),
        cost_estimate=pl.CostEstimate(flops=6 * 10**9, transcendentals=2 * 10**6, bytes_accessed=24 << 20),
    )(info, grad, dm, slope, middle, gain, w_out, *parts)


def feed_both_kernel(info, c_ref, dm_ref, mid_ref, vec_ref, w_in, *refs):
    parts, refs = refs[:8], refs[8:]
    own_out, other_out, dmid_ref, da_ref, sums_ref, *targets = refs[:9]
    act_own, act_other, x_ref = refs[9:12]
    act_ref, dh_ref, held, dc, w_ref, sems, out_sems, in_sem = refs[12:]
    toks, width = mid_ref.shape
    copies = fetch(parts, held, sems)
    late_in = pltpu.make_async_copy(w_in, w_ref, in_sem.at[0])
    late_in.start()
    x_ref[...] = mid_ref[...] + vec_ref[0:1, :]
    outs = []
    goals = (own_out.at[0], own_out.at[1], other_out.at[0], other_out.at[1])

    def before(at):
        copies[2 * at].wait()
        copies[2 * at + 1].wait()
        bias = held[at, :, 2 * width : 2 * width + 128].T[0:1].astype(F32)
        pre = dot(c_ref[...], held[at, :, 0:width], ((1,), (1,))) + bias
        return pre, dot(dm_ref[...], held[at, :, width : 2 * width], ((1,), (1,)))

    def after(at, found):
        pre, dact = found
        act, slope = gelu(pre)
        act = act.astype(BF16)
        act_ref[at] = act.T
        dpre = (dact * slope).astype(BF16)
        dh_ref[at] = dpre
        goal = (act_own, act_other)[at // 2].at[at % 2]
        outs.append(pltpu.make_async_copy(dh_ref.at[at], goals[at], out_sems.at[2 * at]))
        outs.append(pltpu.make_async_copy(act_ref.at[at], goal, out_sems.at[2 * at + 1]))
        outs[-2].start()
        outs[-1].start()
        x_ref[...] += dot(act, held[at, :, width : 2 * width])
        term = dot(dpre, held[at, :, 0:width])
        if at == 0:
            dc[...] = term
        else:
            dc[...] += term

    found = before(0)
    for at in range(4):
        later = before(at + 1) if at < 3 else None
        after(at, found)
        found = later
    late_in.wait()
    finish_back(info[3], dm_ref, mid_ref, vec_ref.at[1:2], w_ref, dm_ref, dc, dmid_ref, da_ref, sums_ref, targets)
    for copy in outs:
        copy.wait()


def feed_both(info, c, dm, middle, vectors, w_out, parts):
    toks, width = middle.shape
    units = 2 * parts[0].shape[0]
    shapes = back_outputs(toks, width, units) + [
        jax.ShapeDtypeStruct((2, units, toks), BF16),
        jax.ShapeDtypeStruct((2, units, toks), BF16),
        jax.ShapeDtypeStruct((toks, width), F32),
    ]
    return pl.pallas_call(
        feed_both_kernel,
        name="feed_both",
        grid_spec=pltpu.PrefetchScalarGridSpec(
            num_scalar_prefetch=1,
            grid=(1,),
            in_specs=[whole(v.shape) for v in (c, dm, middle, vectors)] + [HBM] * 9,
            out_specs=[HBM] * 2 + [whole(shape.shape) for shape in shapes[2:9]] + [HBM, HBM, whole((toks, width))],
            scratch_shapes=[
                pltpu.VMEM((4, units, toks), BF16),
                pltpu.VMEM((4, toks, units), BF16),
                pltpu.VMEM((4, units, parts[0].shape[1]), BF16),
                pltpu.VMEM((toks, width), F32),
                pltpu.VMEM((width, width), BF16),
                pltpu.SemaphoreType.DMA((8,)),
                pltpu.SemaphoreType.DMA((8,)),
                pltpu.SemaphoreType.DMA((1,)),
            ],
        ),
        out_shape=shapes,
        compiler_params=pltpu.CompilerParams(vmem_limit_bytes=60 << 20),
        cost_estimate=pl.CostEstimate(flops=10**10, transcendentals=2 * 10**6, bytes_accessed=24 << 20),
    )(info, c, dm, middle, vectors, w_out, *parts)


def feed_weights_kernel(dh, dh2, act, act2, c, c2, dm, dm2, out_ref):
    width = c.shape[1]
    one, two = dh[0].T, dh2[0].T
    out_ref[:, 0:width] = (dot(one, c[...]) + dot(two, c2[...])).astype(BF16)
    out_ref[:, width : 2 * width] = (dot(act[0], dm[...]) + dot(act2[0], dm2[...])).astype(BF16)
    bias = jnp.sum(one.astype(F32), axis=1, keepdims=True) + jnp.sum(two.astype(F32), axis=1, keepdims=True)
    out_ref[:, 2 * width :] = jnp.broadcast_to(bias, (bias.shape[0], 128)).astype(BF16)


def feed_weights(half, dh, dh2, act, act2, c, c2, dm, dm2):
    toks, units, width = dh.shape[1], dh.shape[2], c.shape[1]
    wide = 2 * width + 128
    step = 256
    act_spec = pl.BlockSpec((1, step, toks), lambda i: (half, i, 0))
    return pl.pallas_call(
        feed_weights_kernel,
        name="feed_weights",
        grid=(units // step,),
        in_specs=[
            pl.BlockSpec((1, toks, step), lambda i: (half, 0, i)),
            pl.BlockSpec((1, toks, step), lambda i: (half, 0, i)),
            act_spec,
            act_spec,
        ]
        + [pl.BlockSpec(v.shape, lambda i: (0, 0)) for v in (c, c2, dm, dm2)],
        out_specs=pl.BlockSpec((step, wide), lambda i: (i, 0)),
        out_shape=jax.ShapeDtypeStruct((units, wide), BF16),
        compiler_params=pltpu.CompilerParams(vmem_limit_bytes=48 << 20),
        cost_estimate=pl.CostEstimate(flops=24 * 10**8, transcendentals=0, bytes_accessed=9 << 20),
    )(dh, dh2, act, act2, c, c2, dm, dm2)


def finish_kernel(last, info, *refs):
    attn, hidden, refs = refs[:4], refs[4:8], refs[8:]
    if last:
        (other_vec, other_bias), refs = refs[:2], refs[6:]
        qkv_ref, out_ref, up_ref, down_ref = refs[:4]
        vectors_out, qv_out, bias_out = refs[4:10], refs[10], refs[11]
        qkv_at, out_at, hid_at = refs[12:]
    else:
        qkv_ref, out_ref, up_ref, down_ref, vec_ref, bias_ref, qkv_at, out_at, hid_at = refs
    dev = info[3]
    spot = info[5]
    rows = attn[0].shape[0]
    loc = 192
    for rel in range(4):
        qkv_at[dev ^ rel] = attn[rel][:, 0:576].astype(F32)
        out_at[dev ^ rel, 0] = attn[rel][:, 576:704].astype(F32)
        out_at[dev ^ rel, 1, :, 0:64] = attn[rel][:, 704:768].astype(F32)
        hid_at[spot ^ rel] = hidden[rel][...].astype(F32)
    width = 4 * loc
    quarter = rows // 4
    units = hidden[0].shape[0]
    for at in range(4):
        found = qkv_at[at]
        qkv_ref[0, :, at * loc : (at + 1) * loc] = found[:, 384:576]
        qkv_ref[0, :, width + at * loc : width + (at + 1) * loc] = found[:, 0:192]
        v_at = 2 * width + at * loc
        qkv_ref[0, :, v_at : v_at + 128] = found[:, 256:384]
        qkv_ref[0, :, v_at + 128 : v_at + 192] = found[:, 192:256]
        for piece in range(4):
            goal = slice(at * quarter, (at + 1) * quarter)
            lane = piece * loc
            out_ref[0, goal, lane : lane + 128] = out_at[at, 0, pl.ds(piece, quarter, stride=4), :]
            out_ref[0, goal, lane + 128 : lane + 192] = out_at[at, 1, pl.ds(piece, quarter, stride=4), :][:, 0:64]
        down_ref[0, at * units : (at + 1) * units, :] = hid_at[at, :, width : 2 * width]
    up = jnp.concatenate([hid_at[at, :, 0:width] for at in range(4)], axis=0)
    up_ref[0] = up.T
    bias = jnp.concatenate([hid_at[at, :, 2 * width :] for at in range(4)], axis=0).T[0:8]
    vectors = sum(part[:, 768:896].astype(F32) for part in attn).T[0:16]
    if not last:
        vec_ref[...] = vectors
        bias_ref[...] = bias
        return
    bias_out[0:1, :] = bias[0:1]
    bias_out[1:2, :] = other_bias[0:1, :]
    order = (((12, 0), (10, 0)), ((13, 0), (11, 0)), ((0, 0), (0, 1)), ((1, 0), (1, 1)), ((2, 0), (2, 1)), ((3, 0), (3, 1)))
    for target, picks in zip(vectors_out, order):
        for layer, (row, from_other) in enumerate(picks):
            source = other_vec[row : row + 1, :] if from_other else vectors[row : row + 1]
            target[layer : layer + 1, :] = source
    for half in range(2):
        lanes = slice(half * rows, (half + 1) * rows)
        qv_out[0:1, lanes] = vectors[8 + half : 9 + half]
        qv_out[1:2, lanes] = other_vec[8 + half : 9 + half, :]


def finish(info, layer, attn, hidden, before):
    rows, width = attn[0].shape[0], attn[0].shape[1] - 128
    units = hidden[0].shape[0]
    shapes = [
        (LAYERS, rows, 3 * width),
        (LAYERS, rows, width),
        (LAYERS, width, 4 * units),
        (LAYERS, 4 * units, width),
    ]
    specs = [pl.BlockSpec((1, *shape[1:]), lambda i, info: (layer, 0, 0)) for shape in shapes]
    last = before is not None
    more = [(LAYERS, rows)] * 6 + [(LAYERS, 2 * rows), (LAYERS, 4 * units)] if last else [(16, rows), (8, 4 * units)]
    given = [*before[4:6], *before[:4]] if last else []
    return pl.pallas_call(
        partial(finish_kernel, last),
        name="finish",
        grid_spec=pltpu.PrefetchScalarGridSpec(
            num_scalar_prefetch=1,
            grid=(1,),
            in_specs=[whole(attn[0].shape)] * 4
            + [whole(hidden[0].shape)] * 4
            + ([whole(v.shape) for v in given[:2]] + [HBM] * 4 if last else []),
            out_specs=specs + [whole(shape) for shape in more],
            scratch_shapes=[
                pltpu.VMEM((4, rows, 576), F32),
                pltpu.VMEM((4, 2, rows, 128), F32),
                pltpu.VMEM((4, units, 2 * width + 128), F32),
            ],
        ),
        out_shape=[jax.ShapeDtypeStruct(shape, F32) for shape in shapes + more],
        input_output_aliases={11 + at: at for at in range(4)} if last else {},
        compiler_params=pltpu.CompilerParams(vmem_limit_bytes=56 << 20),
        cost_estimate=pl.CostEstimate(flops=10**6, transcendentals=0, bytes_accessed=8 << 20),
    )(info, *attn, *hidden, *given)


PLANE = ("cx", "core", "tp")


def turned(value, first):
    pairs = []
    for x in range(2):
        for core in range(2):
            for y in range(2):
                flip_x = (core == 0) == first
                target = ((1 - x) if flip_x else x, core, y if flip_x else 1 - y)
                pairs.append((x * 4 + core * 2 + y, target[0] * 4 + target[1] * 2 + target[2]))
    return lax.ppermute(value, PLANE, pairs)


def after(value, *others):
    return lax.optimization_barrier((value, *others))[0]


def diagonal(value):
    return lax.ppermute(value, ("cx", "core"), ((0, 3), (1, 2), (2, 1), (3, 0)))


def around(own):
    far = swap(own, "cx")
    return own, swap(own, "core"), far, swap(far, "core")


def local(
    hidden_in,
    doc_lengths,
    ln1_gain,
    ln1_bias,
    qkv_weight,
    qv_bias,
    out_weight,
    out_bias,
    ln2_gain,
    ln2_bias,
    up_weight,
    up_bias,
    down_weight,
    down_bias,
    output_grad,
):
    shards = lax.axis_size("shard")
    ix, ic, iy = lax.axis_index("cx"), lax.axis_index("core"), lax.axis_index("tp")
    dev = ix * 2 + ic
    seqs, toks, width = hidden_in.shape
    rows = ln1_gain.shape[1]
    units = up_bias.shape[1] // 4
    loc = width // 4
    quarter = rows // 4

    def to_sequence(*arrays):
        given = jnp.stack([lax.dynamic_index_in_dim(array, 1 - iy, 0, keepdims=False) for array in arrays])
        given = swap(given, "tp")
        return [
            jnp.concatenate((lax.dynamic_index_in_dim(array, iy, 0, keepdims=False), other), axis=0)
            for array, other in zip(arrays, given)
        ]

    def own_first(own, other):
        return jnp.where(iy == 0, jnp.stack((own, other)), jnp.stack((other, own)))

    def from_sequence(tokens):
        return own_first(tokens[:toks], swap(tokens[toks:], "tp"))

    lengths = lax.dynamic_index_in_dim(doc_lengths, iy, 0, keepdims=False)
    end0 = lengths[0]
    end1 = end0 + lengths[1]
    end2 = end1 + lengths[2]
    info = jnp.stack((end0, end1, end2, dev, iy, ic * 2 + ix, dev, dev)).astype(jnp.int32)
    row_ids = jnp.arange(2 * toks, dtype=jnp.int32)
    places = dev * (2 * toks) + ((row_ids // toks) ^ iy) * toks + row_ids % toks
    keep = (places < end2).astype(F32)[:, None]

    def columns(array, start):
        return lax.dynamic_slice_in_dim(array, start, loc, 1)

    small = jnp.concatenate(
        [ln1_gain, ln1_bias, out_bias, ln2_gain, ln2_bias, down_bias, qv_bias.reshape(2 * LAYERS, rows)], axis=0
    )
    small = jnp.pad(small, ((0, 128 - small.shape[0]), (0, 0))).T

    def attention_piece(layer):
        weight = qkv_weight[layer]
        q, k, v = (columns(weight, which * width + loc * dev) for which in range(3))
        out = lax.dynamic_slice_in_dim(out_weight[layer], quarter * dev, quarter, 0).reshape(rows, loc)
        pieces = [k[:, :128], k[:, 128:], v[:, 128:], v[:, :128], q, out]
        if layer == 0:
            pieces.append(small)
        return jnp.concatenate(pieces, axis=1)

    def hidden_piece(layer):
        start = ic * 2 * units + ix * units
        up = lax.dynamic_slice_in_dim(up_weight[layer], start, units, 1).T
        down = lax.dynamic_slice_in_dim(down_weight[layer], start, units, 0)
        bias = lax.dynamic_slice_in_dim(up_bias[layer], start, units, 0)
        bias = jnp.broadcast_to(bias[:, None], (units, 128))
        return jnp.concatenate((up, down, bias), axis=1)

    def over_shards(piece):
        return lax.all_gather(piece, "shard", axis=0, tiled=True)

    def send_shards(value, count):
        if shards != 4:
            return ()
        index = lax.axis_index("shard")
        return tuple(
            lax.ppermute(
                lax.dynamic_slice_in_dim(value, (index + by) % shards * count, count, 0),
                "shard",
                [(i, (i + by) % shards) for i in range(shards)],
            )
            for by in range(1, shards)
        )

    def sum_shards(value, count, arriving):
        if shards != 4:
            return lax.psum_scatter(value, "shard", scatter_dimension=0, tiled=True)
        own = lax.dynamic_slice_in_dim(value, lax.axis_index("shard") * count, count, 0).astype(F32)
        return (own + sum(piece.astype(F32) for piece in arriving)).astype(value.dtype)

    def around_hidden(own, *others):
        core, far = swap(own, "core"), swap(own, "cx")
        return own, far, core, swap(after(far, *others), "core")

    hidden_own, raw_grad = to_sequence(hidden_in, output_grad)
    first_piece, attn_piece = hidden_piece(0), attention_piece(0)
    first_parts = around(after(hidden_own, first_piece, attn_piece))
    feed0 = over_shards(first_piece)
    attn0 = over_shards(after(attn_piece, feed0, *first_parts))
    feed_piece, attn_piece = hidden_piece(1), attention_piece(1)
    feed1 = over_shards(after(feed_piece, attn0))
    one0, two0 = turned(feed0, True), turned(feed0, False)

    def out_weights(own):
        full = jnp.zeros((shards, 4, quarter, width), BF16)
        for rel, part in enumerate(around(own)):
            full = lax.dynamic_update_slice(full, part, (0, dev ^ rel, 0, 0))
        return full.reshape(width, width)

    def out_own(gathered):
        return gathered[:, 3 * loc : 4 * loc].reshape(shards, 1, quarter, width)

    weights = []

    smalls = attn0[:, 4 * loc :].T.astype(F32)
    names = [[smalls[which * LAYERS + layer][None] for which in range(6)] for layer in range(LAYERS)]
    qv = smalls[6 * LAYERS : 8 * LAYERS].reshape(LAYERS, 2, shards, rows)
    qv = jnp.transpose(qv, (0, 2, 1, 3)).reshape(LAYERS, 2 * width)

    current = hidden_own.astype(F32)
    attn_parts = first_parts
    saved = []
    for layer in range(LAYERS):
        gain_one, bias_one, bias_out, gain_two, bias_two, bias_down = names[layer]
        w_qkv = attn0 if layer == 0 else attn1
        q_bias = lax.dynamic_slice_in_dim(qv[layer], loc * dev, loc, 0)
        v_bias = lax.dynamic_slice_in_dim(qv[layer], width + loc * dev, loc, 0)
        bias = jnp.concatenate((jnp.zeros((192,), F32), v_bias[128:], v_bias[:128], q_bias))[None]
        if layer == 0:
            one0, two0, attn_piece, *attn_parts = lax.optimization_barrier((one0, two0, attn_piece, *attn_parts))
            three0 = turned(one0, False)
            early_core = [swap(part, "core") for part in (feed0, one0, two0)]
        attn_t, qkv, attended, lse, *normed_all = attention_forward(info, attn_parts, w_qkv, bias, gain_one, bias_one, layer == 0)
        if layer == 0:
            attn1 = over_shards(after(attn_piece, attended))
            w_out = out_weights(out_own(attn0))
            attended, w_out, three0, *early_core = lax.optimization_barrier((attended, w_out, three0, *early_core))
            w_feed = (feed0, one0, two0, three0, *early_core, swap(three0, "core"))
        else:
            own, one, two, three = w_feed1
            early_core = (swap(own, "core"), swap(one, "core"))
            attended, w_out, own, one, two, three, *early_core = lax.optimization_barrier(
                (attended, w_out1, own, one, two, three, *early_core)
            )
        parts = (
            attended[0],
            swap(attended[1], "core"),
            swap(attended[2], "cx"),
            diagonal(attended[3]),
        )
        if layer == 1:
            late_core = [swap(after(part, *parts), "core") for part in (two, three)]
            low_grad = raw_grad * keep.astype(BF16)
            low_other = swap(low_grad, "core")
            w_feed = (own, one, two, three, *early_core, *late_core)
        vectors = jnp.concatenate((bias_out, gain_two, bias_two), axis=0)
        context, middle, mlp_in = out_forward(info, parts, w_out, current, vectors)
        if layer == 0:
            vectors = jnp.concatenate((bias_down, names[1][0], names[1][1]), axis=0)
            mlp_in, feed1 = lax.optimization_barrier((mlp_in, feed1))
            one1 = turned(feed1, True)
            slope, act, act_other, result, attn_own = feed_forward(mlp_in, middle, vectors, w_feed)
            act_other, mlp_other = swap(act_other, "core"), swap(mlp_in, "core")
            attn_own = after(attn_own, one1)
            attn_parts = around(attn_own)
            w_out1 = out_weights(out_own(after(attn1, attn_own)))
            w_out1, act_other, mlp_other, *attn_parts = lax.optimization_barrier(
                (w_out1, act_other, mlp_other, *attn_parts)
            )
            feed1, one1 = lax.optimization_barrier((feed1, one1, *attn_parts))[:2]
            w_feed1 = (feed1, one1, turned(feed1, False), turned(one1, False))
        else:
            slope = act = act_other = result = None
            mlp_other = swap(mlp_in, "core")
        if layer == 0:
            first_normed = normed_all
        weights.append((w_qkv, w_out, w_feed))
        saved.append((current, attn_t, qkv, attended, lse, context, middle, mlp_in, mlp_other, slope, act, act_other))
        current = result
    n = shards * units

    before = ()
    for layer in reversed(range(LAYERS)):
        x_in, attn_t, qkv, attended, lse, context, middle, mlp_in, mlp_other, slope, act, act_other = saved[layer]
        gain_one, _, _, gain_two, _, _ = names[layer]
        w_qkv, w_out, w_feed = weights[layer]
        if layer == 0:
            found = feed_backward(info, grad, low_grad, slope, middle, gain_two, w_out, w_feed)
        else:
            vectors = jnp.concatenate((names[1][5], gain_two), axis=0)
            *found, act, act_other, result = feed_both(info, mlp_in, low_grad, middle, vectors, w_out, w_feed)
            act_other = swap(act_other, "core")
        dh, dh_other, middle_grad, branch_grad, sums_two, d0, d1, d2, d3 = found
        attn_grads = (d0, swap(d1, "core"), swap(d2, "cx"), diagonal(d3))
        tokens = (mlp_in, mlp_other, low_grad, low_other)
        dh_other = swap(dh_other, "core")
        *attn_grads, dh_other = lax.optimization_barrier((*attn_grads, dh_other, *before))[:5]
        late = feed_weights(1, dh, dh_other, act, act_other, *tokens)
        w_out_grad = dot(context, branch_grad).astype(BF16).reshape(shards, 4, quarter, width)
        pieces = [lax.dynamic_index_in_dim(w_out_grad, dev ^ rel, 1, keepdims=False) for rel in range(4)]
        got = swap(jnp.stack((pieces[1], pieces[3])), "core")
        far = swap((pieces[2].astype(F32) + got[1].astype(F32)).astype(BF16), "cx")
        ready = [*attn_grads, late, far]
        if layer == 0:
            attn_sum1 = after(attn_sum1, *attn_grads)
            attn_sum1 = (attn_sum1.astype(F32) + swap(attn_sum1, "tp").astype(F32)).astype(BF16)
            ready.append(attn_sum1)
            early = feed_weights(0, dh, dh_other, act, act_other, *tokens)
            ready.append(early)
        *attn_grads, late, far = lax.optimization_barrier(tuple(ready))[:6]
        du, to_core, to_far, own, sums_u, *norm_sums = attention_backward(
            info, qkv, attended, lse, w_qkv, attn_grads, first_normed if layer == 0 else ()
        )
        late = turned(late, False)
        to_core = after(to_core, late)
        from_core = swap(to_core, "core")
        du_sum = sums_u[0]
        v_sum = jnp.concatenate((du_sum[256:384], du_sum[192:256]))
        q_row = lax.dynamic_update_slice_in_dim(jnp.zeros((width,), F32), du_sum[384:], loc * dev, 0)
        v_row = lax.dynamic_update_slice_in_dim(jnp.zeros((width,), F32), v_sum, loc * dev, 0)
        qv_rows = jnp.concatenate((q_row, v_row)).reshape(shards, 2, rows).transpose(1, 0, 2).reshape(2, width)
        vectors = jnp.concatenate((sums_two, qv_rows, jnp.zeros((6, width), F32)), axis=0)
        if layer == 0:
            vectors = jnp.concatenate((vectors[:10], sums_one[:2], norm_sums[0][:2], vectors[14:]), axis=0)
        flat = [piece.reshape(shards * quarter, width) for piece in (pieces[0], got[0], far)]
        if layer == 0:
            joined = attention_weights(attn_t, du, vectors, *flat)
            attn_sum = lax.psum_scatter(joined, "shard", scatter_dimension=0, tiled=True)
            to_far = after(to_far, joined)
        to_far = (to_far + from_core[1].astype(F32)).astype(BF16)
        if layer == 0:
            attn_sum1, feed_sum1 = lax.optimization_barrier((attn_sum1, feed_sum1, late))[:2]
            attn_parts1, hidden_parts1 = around(attn_sum1), around_hidden(feed_sum1)
            part = (early[n:].astype(F32) + after(late, joined)[n:].astype(F32)).astype(BF16)
            part = after(part, *attn_parts1, *hidden_parts1)
            early_late = late
            arrived = turned(part, True)
            to_far = after(to_far, arrived)
            done = finish(info, 1, attn_parts1, hidden_parts1, None)
        from_far = swap(to_far, "cx")
        if layer == 0:
            from_far = after(from_far, done[5])
        if layer > 0:
            du, dh_now, early_late = lax.optimization_barrier((du, dh, late, to_far))[:3]
            early = feed_weights(0, dh_now, dh_other, act, act_other, *tokens)
            part = (early[n:].astype(F32) + early_late[n:].astype(F32)).astype(BF16)
        if layer > 0:
            hidden_own_out = (after(result, to_far) * keep).astype(BF16)
            hidden_other_out = swap(hidden_own_out[toks:], "tp")
            from_far, part, hidden_other_out = lax.optimization_barrier((from_far, part, hidden_other_out))
            arrived = turned(part, True)
        grad, low_grad, sums_one = norm_backward(own, from_core, from_far, x_in, gain_one, middle_grad)
        if layer > 0:
            low_other = swap(low_grad, "core")
            joined = attention_weights(attn_t, after(du, low_grad), vectors, *flat)
            attn_sum1 = lax.psum_scatter(joined, "shard", scatter_dimension=0, tiled=True)
            grad, low_grad, arrived = lax.optimization_barrier((grad, low_grad, arrived, joined))[:3]
            part = early[:n].astype(F32) + early_late[:n].astype(F32) + arrived.astype(F32)
            part = part.astype(BF16)
            before = (part,)
            feed_sum1 = lax.psum_scatter(part, "shard", scatter_dimension=0, tiled=True)
        else:
            part = (early[:n].astype(F32) + late[:n].astype(F32) + arrived.astype(F32)).astype(BF16)
            arriving = send_shards(part, units)
            attn_sum = after(attn_sum, from_far)
            attn_sum = (attn_sum.astype(F32) + swap(attn_sum, "tp").astype(F32)).astype(BF16)
            attn_parts0 = around(attn_sum)
            arriving = lax.optimization_barrier((*arriving, low_grad))[: len(arriving)]
            feed_sum = sum_shards(part, units, arriving)
            hidden_out = own_first(hidden_own_out[:toks], after(hidden_other_out, part))

    hidden_grad = from_sequence(low_grad).astype(F32)

    done = finish(info, 0, attn_parts0, around_hidden(feed_sum), done)

    return (
        hidden_out,
        hidden_grad,
        done[4],
        done[5],
        done[0],
        done[10],
        done[1],
        done[8],
        done[6],
        done[7],
        done[2],
        done[11],
        done[3],
        done[9],
    )


def solution(mesh):
    names = tuple(mesh.axis_names)
    shape = dict(mesh.shape)
    split = Mesh(
        mesh.devices.reshape(shape[names[0]], 2, shape[names[1]] // 2, shape[names[2]]),
        ("shard", "cx", "core", "tp"),
    )
    tokens = P("shard", ("cx", "core", "tp"), None)
    vector = P(None, "shard")
    attn = P(None, "shard", None)
    placed = (
        tokens,
        P("shard", None),
        vector,
        vector,
        attn,
        vector,
        attn,
        vector,
        vector,
        vector,
        P(None, None, ("shard", "tp")),
        P(None, ("shard", "tp")),
        P(None, ("shard", "tp"), None),
        vector,
        tokens,
    )
    return jax.shard_map(
        local,
        mesh=split,
        in_specs=placed,
        out_specs=(
            tokens,
            tokens,
            vector,
            vector,
            attn,
            vector,
            attn,
            vector,
            vector,
            vector,
            P(None, None, ("shard", "tp")),
            P(None, ("shard", "tp")),
            P(None, ("shard", "tp"), None),
            vector,
        ),
        check_vma=False,
    )
```

```python
from functools import partial, reduce

import jax
import jax.numpy as jnp
from jax import lax
from jax.experimental import pallas as pl
from jax.experimental.pallas import tpu as pltpu
from jax.sharding import Mesh
from jax.sharding import PartitionSpec as P

HEADS = 12
HEAD = 64
LAYERS = 2
BLK = 256
NEG = -1e30
EPS = 1e-06
F32 = jnp.float32
BF16 = jnp.bfloat16


def dot(left, right, dims=((1,), (0,))):
    return lax.dot_general(left, right, (dims, ((), ())), preferred_element_type=F32)


def swap(value, axis):
    return lax.ppermute(value, axis, ((0, 1), (1, 0)))


def block_place(block, dev, half):
    return (((block // 2) ^ dev) * 2) + ((block % 2) ^ half)


def doc_range(first, ends, length):
    last = first + BLK - 1
    start, stop = jnp.int32(0), jnp.int32(length)
    for end in ends:
        start = jnp.maximum(start, jnp.where(first >= end, end, 0))
        stop = jnp.minimum(stop, jnp.where(last < end, end, length))
    return start // BLK, (stop + BLK - 1) // BLK


def seg_of(places, ends):
    seg = (places >= ends[0]).astype(jnp.int32)
    for end in ends[1:]:
        seg = seg + (places >= end).astype(jnp.int32)
    return seg


def three_heads(pair, single):
    blank = jnp.zeros_like(single)
    return (
        jnp.concatenate((pair[:HEAD], blank), axis=0),
        jnp.concatenate((blank, pair[HEAD:]), axis=0),
        jnp.concatenate((single, blank), axis=0),
    )


def norm_rows(rows, gain, bias):
    centred = rows - jnp.mean(rows, axis=-1, keepdims=True)
    inv_std = lax.rsqrt(jnp.mean(centred * centred, axis=-1, keepdims=True) + EPS)
    return centred * inv_std * gain + bias


def whole(shape):
    return pl.BlockSpec(shape, lambda *at: (0,) * len(shape))


HBM = pl.BlockSpec(memory_space=pl.ANY)


def attention_forward_kernel(norm, info, *refs):
    parts, (w_ref, bias_ref, gain_ref, shift_ref) = refs[:4], refs[4:8]
    at_out, qkv_out, out_ref, lse_ref = refs[8:12]
    if norm:
        n_out = refs[12]
    a_ref, at_ref, qkv_ref, v_t, sems, out_sems = refs[13:19] if norm else refs[12:18]
    length = qkv_ref.shape[0]
    ends = (info[0], info[1], info[2])
    dev, half = info[3], info[4]
    each = parts[0].shape[0]
    copies = [pltpu.make_async_copy(part, a_ref.at[at], sems.at[at]) for at, part in enumerate(parts)]
    for copy in copies:
        copy.start()
    for part in range(4):
        copies[part].wait()

        def project(at, nothing):
            rows = pl.ds(pl.multiple_of(at * BLK, BLK), BLK)
            goal = pl.ds(pl.multiple_of(part * each + at * BLK, BLK), BLK)
            values = a_ref[part, rows, :]
            if norm:
                normed = norm_rows(values.astype(F32), 1.0, 0.0)
                a_ref[part, rows, :] = normed.astype(BF16)
                values = (normed * gain_ref[...] + shift_ref[...]).astype(BF16)
            found = dot(values, w_ref[:, 0:576]) + bias_ref[...]
            at_ref[:, goal] = values.T
            qkv_ref[goal, 0:384] = found[:, 0:384].astype(BF16)
            qkv_ref[goal, 384:576] = (found[:, 384:576] * HEAD**-0.5).astype(BF16)
            pair = qkv_ref[goal, 256:384].T
            ones = jnp.ones((16, BLK), BF16)
            for head, found in enumerate((pair[:HEAD], pair[HEAD:], qkv_ref[goal, 128:256].T[HEAD:])):
                v_t[head, 0:HEAD, goal] = found
                v_t[head, HEAD : HEAD + 16, goal] = ones
            return nothing

        lax.fori_loop(0, each // BLK, project, 0)
    out_copies = [
        pltpu.make_async_copy(at_ref, at_out, out_sems.at[0]),
        pltpu.make_async_copy(qkv_ref, qkv_out, out_sems.at[1]),
    ]
    if norm:
        out_copies.append(pltpu.make_async_copy(a_ref, n_out, out_sems.at[2]))
    for copy in out_copies:
        copy.start()

    blocks = length // BLK
    lse_ref[...] = jnp.zeros_like(lse_ref)

    def per_block(step, nothing):
        mine = pl.ds(pl.multiple_of(step * BLK, BLK), BLK)
        first = block_place(step, dev, half) * BLK
        seg_q = seg_of(first + lax.broadcasted_iota(jnp.int32, (1, BLK), 1), ends)
        queries = three_heads(qkv_ref[mine, 384:512].T, qkv_ref[mine, 512:576].T)
        low, high = doc_range(first, ends, length)

        def body(count, begin, at, carry):
            tiles = []
            for more in range(count):
                block = begin + count * at + more
                place = block_place(block, dev, half)
                rows = pl.ds(pl.multiple_of(place * BLK, BLK), BLK)
                places = block * BLK + lax.broadcasted_iota(jnp.int32, (BLK, 1), 0)
                tiles.append((rows, seg_of(places, ends) == seg_q))

            def score(head):
                lanes = slice(128, 256) if head == 2 else slice(0, 128)
                return [jnp.where(allowed, dot(qkv_ref[rows, lanes], queries[head]), NEG) for rows, allowed in tiles]

            def weigh(head, scores):
                top, acc = carry[head]
                new_top = jnp.maximum(top, jnp.max(reduce(jnp.maximum, scores), axis=0, keepdims=True))
                shrink = jnp.exp(top - new_top)
                exps = [jnp.exp(one - new_top) for one in scores]
                return new_top, acc * shrink, [exp.astype(BF16) for exp in exps]

            def gather(head, weighed):
                top, acc, exps = weighed
                for (rows, _), exp in zip(tiles, exps):
                    acc = acc + dot(v_t[head, :, rows], exp)
                return top, acc

            s0 = score(0)
            s1 = score(1)
            w0 = weigh(0, s0)
            s2 = score(2)
            w1 = weigh(1, s1)
            r0 = gather(0, w0)
            w2 = weigh(2, s2)
            r1 = gather(1, w1)
            r2 = gather(2, w2)
            return r0, r1, r2

        start = tuple(
            (
                jnp.full((1, BLK), NEG, F32),
                jnp.zeros((HEAD + 16, BLK), F32),
            )
            for _ in range(3)
        )
        pairs, odd = (high - low) // 2, (high - low) % 2
        final = lax.fori_loop(0, pairs, partial(body, 2, low), start)
        final = lax.fori_loop(0, odd, partial(body, 1, high - 1), final)
        cols = pl.ds(pl.multiple_of((step % 2) * BLK, BLK), BLK)
        for head in range(3):
            top, acc = final[head]
            total = acc[HEAD : HEAD + 1]
            out_ref[step // 2, head * HEAD : (head + 1) * HEAD, cols] = (acc[:HEAD] / total).astype(BF16)
            lse_ref[head : head + 1, mine] = top + jnp.log(total)
        return nothing

    lax.fori_loop(0, blocks, per_block, 0)
    for copy in out_copies:
        copy.wait()


def attention_forward(info, parts, w_qkv, bias, gain, shift, norm):
    each, width = parts[0].shape
    length = 4 * each
    return pl.pallas_call(
        partial(attention_forward_kernel, norm),
        name="attention_forward",
        grid_spec=pltpu.PrefetchScalarGridSpec(
            num_scalar_prefetch=1,
            grid=(1,),
            in_specs=[HBM] * 4 + [whole(w_qkv.shape), whole(bias.shape), whole(gain.shape), whole(shift.shape)],
            out_specs=[HBM, HBM, whole((4, 192, each)), whole((8, length))] + [HBM] * norm,
            scratch_shapes=[
                pltpu.VMEM((4, each, width), BF16),
                pltpu.VMEM((width, length), BF16),
                pltpu.VMEM((length, 576), BF16),
                pltpu.VMEM((3, HEAD + 16, length), BF16),
                pltpu.SemaphoreType.DMA((4,)),
                pltpu.SemaphoreType.DMA((3,)),
            ],
        ),
        out_shape=(
            jax.ShapeDtypeStruct((width, length), BF16),
            jax.ShapeDtypeStruct((length, 576), BF16),
            jax.ShapeDtypeStruct((4, 192, each), BF16),
            jax.ShapeDtypeStruct((8, length), F32),
        )
        + (jax.ShapeDtypeStruct((4, each, width), BF16),) * norm,
        compiler_params=pltpu.CompilerParams(vmem_limit_bytes=48 << 20),
        cost_estimate=pl.CostEstimate(
            flops=14 * 10**9, transcendentals=3 * length * 1024, bytes_accessed=12 << 20
        ),
    )(info, *parts, w_qkv, bias, gain, shift)


def attention_backward_kernel(norm, info, qkv_ref, out_ref, lse_ref, w_ref, g0, g1, g2, g3, *refs):
    if norm:
        tokens, refs = refs[0], refs[1:]
        norm_sums, refs = refs[5], refs[:5] + refs[6:]
        x_ref, da_ref, x_sems = refs[-3:]
        token_copies = [pltpu.make_async_copy(tokens, x_ref, x_sems.at[0])]
        for copy in token_copies:
            copy.start()
        refs = refs[:-3]
    du_out, core_out, far_out, own_out, sums_ref = refs[:5]
    q01_t, q2_t, delta, dq_t, grad_t, du_ref, core_ref, far_ref, own_ref, sems = refs[5:]
    length = qkv_ref.shape[0]
    each = length // 4
    ends = (info[0], info[1], info[2])
    dev, half = info[3], info[4]
    blocks = length // BLK
    q01_t[...] = qkv_ref[:, 384:512].T
    q2_t[...] = qkv_ref[:, 512:576].T
    dq_t[...] = jnp.zeros_like(dq_t)
    for part, grad in enumerate((g0, g1, g2, g3)):
        grad_t[part] = grad[...]
        for head in range(3):
            rows = slice(head * HEAD, (head + 1) * HEAD)
            both = out_ref[part, rows].astype(F32) * grad[rows].astype(F32)
            delta[head : head + 1, part * each : (part + 1) * each] = jnp.sum(both, axis=0, keepdims=True)

    def per_block(step, nothing):
        mine = pl.ds(pl.multiple_of(step * BLK, BLK), BLK)
        first = block_place(step, dev, half) * BLK
        seg_k = seg_of(first + lax.broadcasted_iota(jnp.int32, (BLK, 1), 0), ends)
        k01 = qkv_ref[mine, 0:128]
        k2v2 = qkv_ref[mine, 128:256]
        v01 = qkv_ref[mine, 256:384]
        k01_t = k01.T
        k2_t = k2v2.T[:HEAD]
        keys_t = (k01_t[:HEAD], k01_t[HEAD:], k2_t)
        low, high = doc_range(first, ends, length)

        def body(width, begin, at, carry):
            blank = jnp.zeros((HEAD, BLK), BF16)
            tiles = []
            for more in range(width):
                block = begin + width * at + more
                place = block_place(block, dev, half)
                cols = pl.ds(pl.multiple_of(place * BLK, BLK), BLK)
                part_cols = pl.ds(pl.multiple_of((place % 2) * BLK, BLK), BLK)
                places = block * BLK + lax.broadcasted_iota(jnp.int32, (1, BLK), 1)
                allowed = seg_k == seg_of(places, ends)
                queries = three_heads(q01_t[:, cols], q2_t[:, cols])
                grads = grad_t[place // 2, :, part_cols]
                dos = (
                    jnp.concatenate((grads[:HEAD], blank), axis=0),
                    jnp.concatenate((blank, grads[HEAD:128]), axis=0),
                    jnp.concatenate((blank, grads[128:192]), axis=0),
                )
                tiles.append((cols, allowed, queries, dos))

            def first_dots(at):
                cols, allowed, queries, dos = tiles[at // 3]
                head = at % 3
                return (
                    dot(k2v2 if head == 2 else k01, queries[head]),
                    dot(k2v2 if head == 2 else v01, dos[head]),
                )

            def weigh(at, found):
                cols, allowed, queries, dos = tiles[at // 3]
                head = at % 3
                scores, grad_probs = found
                probs = jnp.where(allowed, jnp.exp(scores - lse_ref[head : head + 1, cols]), 0.0)
                grad_scores = (probs * (grad_probs - delta[head : head + 1, cols])).astype(BF16)
                return probs.astype(BF16), grad_scores

            def last_dots(at, found, sums):
                cols, allowed, queries, dos = tiles[at // 3]
                head = at % 3
                probs, grad_scores = found
                more_k = dot(grad_scores, queries[head], ((1,), (1,)))
                more_v = dot(probs, dos[head], ((1,), (1,)))
                more_q = dot(keys_t[head], grad_scores)
                dk01, dk2v2, dv01 = sums
                if head == 2:
                    dk2v2 = dk2v2 + more_k + more_v
                else:
                    dk01 = dk01 + more_k
                    dv01 = dv01 + more_v
                return (dk01, dk2v2, dv01), more_q

            count = 3 * width
            sums = carry
            more_q = []
            begun = {0: first_dots(0), 1: first_dots(1)}
            weighed = {}
            for at in range(count):
                if at + 2 < count:
                    begun[at + 2] = first_dots(at + 2)
                weighed[at] = weigh(at, begun[at])
                if at > 0:
                    sums, found = last_dots(at - 1, weighed[at - 1], sums)
                    more_q.append(found)
            sums, found = last_dots(count - 1, weighed[count - 1], sums)
            more_q.append(found)
            for tile in range(width):
                cols = tiles[tile][0]
                dq_t[:, cols] = dq_t[:, cols] + jnp.concatenate(more_q[3 * tile : 3 * tile + 3], axis=0)
            return sums

        zero = jnp.zeros((BLK, 128), F32)
        pairs, odd = (high - low) // 2, (high - low) % 2
        sums = lax.fori_loop(0, pairs, partial(body, 2, low), (zero, zero, zero))
        dk01, dk2v2, dv01 = lax.fori_loop(0, odd, partial(body, 1, high - 1), sums)
        du_ref[mine, 0:128] = dk01.astype(BF16)
        du_ref[mine, 128:256] = dk2v2.astype(BF16)
        du_ref[mine, 256:384] = dv01.astype(BF16)
        return nothing

    lax.fori_loop(0, blocks, per_block, 0)
    sums_ref[...] = jnp.zeros_like(sums_ref)
    scale = HEAD**-0.5

    def finish_rows(at, total):
        rows = pl.ds(pl.multiple_of(at * BLK, BLK), BLK)
        du_ref[rows, 384:512] = (dq_t[0:128, rows] * scale).T.astype(BF16)
        du_ref[rows, 512:576] = (dq_t[128:192, rows] * scale).T.astype(BF16)
        return total + jnp.sum(du_ref[rows, :].astype(F32), axis=0, keepdims=True)

    sums_ref[0:1, :] = lax.fori_loop(0, blocks, finish_rows, jnp.zeros((1, 576), F32))
    copies = [pltpu.make_async_copy(du_ref, du_out, sems.at[0])]
    copies[0].start()
    plan = ((1, core_ref.at[0], core_out.at[0]), (3, core_ref.at[1], core_out.at[1]), (2, far_ref, far_out), (0, own_ref, own_out))
    if norm:
        for copy in token_copies:
            copy.wait()
        width = da_ref.shape[1]
        totals = (jnp.zeros((1, width), F32), jnp.zeros((1, width), F32))
    for at, (part, target, goal) in enumerate(plan):
        kind = target.dtype
        found = dot(du_ref[part * each : (part + 1) * each, :], w_ref[:, 0:576], ((1,), (1,)))
        if norm:
            da_ref[...] = found

            def rows_of(step, sums, part=part):
                rows = pl.ds(pl.multiple_of(step * 128, 128), 128)
                grad = da_ref[rows, :]
                normed = x_ref[part, rows, :].astype(F32)
                return (
                    sums[0] + jnp.sum(grad * normed, axis=0, keepdims=True),
                    sums[1] + jnp.sum(grad, axis=0, keepdims=True),
                )

            totals = lax.fori_loop(0, each // 128, rows_of, totals)
            found = da_ref[...]
        target[...] = found.astype(kind)
        copies.append(pltpu.make_async_copy(target, goal, sems.at[at + 1]))
        copies[-1].start()
    if norm:
        norm_sums[...] = jnp.zeros_like(norm_sums)
        norm_sums[0:1, :] = totals[0]
        norm_sums[1:2, :] = totals[1]
    for copy in copies:
        copy.wait()


def attention_backward(info, qkv, out, lse, w_qkv, grads, tokens=()):
    norm = len(tokens) > 0
    length, each, width = qkv.shape[0], qkv.shape[0] // 4, w_qkv.shape[0]
    return pl.pallas_call(
        partial(attention_backward_kernel, norm),
        name="attention_backward",
        grid_spec=pltpu.PrefetchScalarGridSpec(
            num_scalar_prefetch=1,
            grid=(1,),
            in_specs=[whole(qkv.shape), whole(out.shape), whole(lse.shape), whole(w_qkv.shape)]
            + [whole((192, each))] * 4
            + [HBM] * len(tokens),
            out_specs=[HBM, HBM, HBM, HBM, whole((8, 576))] + [whole((8, width))] * norm,
            scratch_shapes=[
                pltpu.VMEM((128, length), BF16),
                pltpu.VMEM((64, length), BF16),
                pltpu.VMEM((8, length), F32),
                pltpu.VMEM((192, length), F32),
                pltpu.VMEM((4, 192, each), BF16),
                pltpu.VMEM((length, 576), BF16),
                pltpu.VMEM((2, each, width), BF16),
                pltpu.VMEM((each, width), F32),
                pltpu.VMEM((each, width), F32),
                pltpu.SemaphoreType.DMA((5,)),
            ]
            + [pltpu.VMEM((4, each, width), BF16), pltpu.VMEM((each, width), F32), pltpu.SemaphoreType.DMA((1,))] * norm,
        ),
        out_shape=(
            jax.ShapeDtypeStruct(qkv.shape, BF16),
            jax.ShapeDtypeStruct((2, each, width), BF16),
            jax.ShapeDtypeStruct((each, width), F32),
            jax.ShapeDtypeStruct((each, width), F32),
            jax.ShapeDtypeStruct((8, 576), F32),
        )
        + (jax.ShapeDtypeStruct((8, width), F32),) * norm,
        compiler_params=pltpu.CompilerParams(vmem_limit_bytes=56 << 20),
        cost_estimate=pl.CostEstimate(
            flops=20 * 10**9, transcendentals=3 * length * 1024, bytes_accessed=16 << 20
        ),
    )(info, qkv, out, lse, w_qkv, *grads, *tokens)


def attention_weights_kernel(at_ref, du_ref, vec_ref, own_ref, core_ref, far_ref, out_ref, spread):
    blank = jnp.zeros((128 - vec_ref.shape[0], vec_ref.shape[1]), F32)
    out_ref[:, 768:896] = jnp.concatenate((vec_ref[...], blank), axis=0).T.astype(BF16)
    out_ref[:, 0:576] = dot(at_ref[...], du_ref[...]).astype(BF16)
    total = own_ref[...].astype(F32) + core_ref[...].astype(F32) + far_ref[...].astype(F32)
    quarter = own_ref.shape[0]
    for piece in range(4):
        rows = pl.ds(piece, quarter, stride=4)
        spread[0, rows, :] = total[:, piece * 192 : piece * 192 + 128]
        spread[1, rows, :] = jnp.concatenate(
            (total[:, piece * 192 + 128 : (piece + 1) * 192], jnp.zeros((quarter, 64), F32)), axis=1
        )
    out_ref[:, 576:704] = spread[0].astype(BF16)
    out_ref[:, 704:768] = spread[1, :, 0:64].astype(BF16)


def attention_weights(a_t, du, vectors, own, core, far):
    width = a_t.shape[0]
    return pl.pallas_call(
        attention_weights_kernel,
        name="attention_weights",
        grid=(1,),
        in_specs=[whole(v.shape) for v in (a_t, du, vectors, own, core, far)],
        out_specs=whole((width, width + 128)),
        out_shape=jax.ShapeDtypeStruct((width, width + 128), BF16),
        scratch_shapes=[pltpu.VMEM((2, width, 128), F32)],
        compiler_params=pltpu.CompilerParams(vmem_limit_bytes=48 << 20),
        cost_estimate=pl.CostEstimate(flops=18 * 10**8, transcendentals=0, bytes_accessed=8 << 20),
    )(a_t, du, vectors, own, core, far)


def out_kernel(info, p0, p1, p2, p3, w_ref, x_ref, vec_ref, ctx_ref, mid_ref, c_ref, ctx):
    dev = info[3]
    loc, toks = p0.shape
    for rel, part in enumerate((p0, p1, p2, p3)):
        ctx[dev ^ rel] = part[...]
    ctx_ref[...] = ctx[...].reshape(4 * loc, toks)

    def rows_of(at, nothing):
        rows = pl.ds(pl.multiple_of(at * 128, 128), 128)
        found = dot(ctx_ref[:, rows].T, w_ref[...])
        middle = x_ref[rows, :] + found + vec_ref[0:1, :]
        mid_ref[rows, :] = middle
        c_ref[rows, :] = norm_rows(middle, vec_ref[1:2, :], vec_ref[2:3, :]).astype(BF16)
        return nothing

    lax.fori_loop(0, toks // 128, rows_of, 0)


def out_forward(info, parts, w_out, current, vectors):
    loc, toks = parts[0].shape
    width = w_out.shape[1]
    return pl.pallas_call(
        out_kernel,
        name="out_forward",
        grid_spec=pltpu.PrefetchScalarGridSpec(
            num_scalar_prefetch=1,
            grid=(1,),
            in_specs=[whole((loc, toks))] * 4 + [whole(w_out.shape), whole(current.shape), whole(vectors.shape)],
            out_specs=[whole((width, toks)), whole((toks, width)), whole((toks, width))],
            scratch_shapes=[pltpu.VMEM((4, loc, toks), BF16)],
        ),
        out_shape=(
            jax.ShapeDtypeStruct((width, toks), BF16),
            jax.ShapeDtypeStruct((toks, width), F32),
            jax.ShapeDtypeStruct((toks, width), BF16),
        ),
        compiler_params=pltpu.CompilerParams(vmem_limit_bytes=48 << 20),
        cost_estimate=pl.CostEstimate(flops=10**9, transcendentals=0, bytes_accessed=7 << 20),
    )(info, *parts, w_out, current, vectors)


def norm_back(grad, values, gain):
    centred = values - jnp.mean(values, axis=-1, keepdims=True)
    inv_std = lax.rsqrt(jnp.mean(centred * centred, axis=-1, keepdims=True) + EPS)
    normed = centred * inv_std
    scaled = grad * gain
    grad_in = inv_std * (
        scaled
        - jnp.mean(scaled, axis=-1, keepdims=True)
        - normed * jnp.mean(scaled * normed, axis=-1, keepdims=True)
    )
    return grad_in, jnp.sum(grad * normed, axis=0, keepdims=True), jnp.sum(grad, axis=0, keepdims=True)


def norm_back_kernel(own, core, far, x_ref, gain_ref, mid_ref, grad_ref, low_ref, sums_ref):
    toks, width = x_ref.shape
    step = pl.program_id(0)

    @pl.when(step == 0)
    def _():
        sums_ref[...] = jnp.zeros_like(sums_ref)

    def rows_of(at, sums):
        rows = pl.ds(pl.multiple_of(at * 128, 128), 128)
        found = own[rows, :] + core[0, rows, :].astype(F32) + far[rows, :].astype(F32)
        grad_in, gain_sum, bias_sum = norm_back(found, x_ref[rows, :], gain_ref[...])
        grad = mid_ref[rows, :] + grad_in
        grad_ref[rows, :] = grad
        low_ref[rows, :] = grad.astype(BF16)
        return sums[0] + gain_sum, sums[1] + bias_sum

    zero = jnp.zeros((1, width), F32)
    sums = lax.fori_loop(0, toks // 128, rows_of, (zero, zero))
    sums_ref[0:1, :] += sums[0]
    sums_ref[1:2, :] += sums[1]


def norm_backward(own, core, far, values, gain, middle_grad):
    toks, width = values.shape
    rows = pl.BlockSpec((toks // 4, width), lambda i: (i, 0))
    return pl.pallas_call(
        norm_back_kernel,
        name="norm_backward",
        grid=(4,),
        in_specs=[rows, pl.BlockSpec((1, toks // 4, width), lambda i: (0, i, 0)), rows, rows, whole(gain.shape), rows],
        out_specs=[rows, rows, whole((8, width))],
        out_shape=(
            jax.ShapeDtypeStruct((toks, width), F32),
            jax.ShapeDtypeStruct((toks, width), BF16),
            jax.ShapeDtypeStruct((8, width), F32),
        ),
        compiler_params=pltpu.CompilerParams(vmem_limit_bytes=48 << 20),
        cost_estimate=pl.CostEstimate(flops=10**7, transcendentals=0, bytes_accessed=9 << 20),
    )(own, core, far, values, gain, middle_grad)


GELU_A = (2.0 / 3.141592653589793) ** 0.5
GELU_B = 0.044715


def gelu(t):
    square = t * t
    tanh = jnp.tanh(t * (GELU_A + GELU_A * GELU_B * square))
    half = 0.5 * t
    side = 0.5 + 0.5 * tanh
    slope = side + (half - half * tanh * tanh) * (GELU_A + 3.0 * GELU_A * GELU_B * square)
    return t * side, slope


def fetch(parts, held, sems):
    units = parts[0].shape[0]
    copies = [
        pltpu.make_async_copy(part, held.at[at // 2, pl.ds((at % 2) * units, units)], sems.at[at])
        for at, part in enumerate(parts)
    ]
    for copy in copies:
        copy.start()
    return copies


def feed_kernel(c_ref, mid_ref, vec_ref, *refs):
    parts, refs = refs[:8], refs[8:]
    slope_out, own_out, other_out, x_ref, a_ref, slope_ref, act_ref, held, sems, out_sems = refs
    toks, width = mid_ref.shape
    copies = fetch(parts, held, sems)
    x_ref[...] = mid_ref[...] + vec_ref[0:1, :]
    outs = []

    def before(at):
        copies[2 * at].wait()
        copies[2 * at + 1].wait()
        bias = held[at, :, 2 * width : 2 * width + 128].T[0:1].astype(F32)
        return dot(c_ref[...], held[at, :, 0:width], ((1,), (1,))) + bias

    def after(at, pre):
        act, slope = gelu(pre)
        act = act.astype(BF16)
        slope_ref[at] = slope.astype(BF16)
        act_ref[at] = act.T
        outs.append(pltpu.make_async_copy(slope_ref.at[at], slope_out.at[at], out_sems.at[2 * at]))
        goal = (own_out, other_out)[at // 2].at[at % 2]
        outs.append(pltpu.make_async_copy(act_ref.at[at], goal, out_sems.at[2 * at + 1]))
        outs[-2].start()
        outs[-1].start()
        x_ref[...] += dot(act, held[at, :, width : 2 * width])

    pre = before(0)
    for at in range(4):
        later = before(at + 1) if at < 3 else None
        after(at, pre)
        pre = later

    def rows_of(at, nothing):
        rows = pl.ds(pl.multiple_of(at * 128, 128), 128)
        a_ref[rows, :] = norm_rows(x_ref[rows, :], vec_ref[1:2, :], vec_ref[2:3, :]).astype(BF16)
        return nothing

    lax.fori_loop(0, toks // 128, rows_of, 0)
    for copy in outs:
        copy.wait()


def feed_forward(c, middle, vectors, parts):
    toks, width = middle.shape
    units = 2 * parts[0].shape[0]
    return pl.pallas_call(
        feed_kernel,
        name="feed_forward",
        grid=(1,),
        in_specs=[whole(c.shape), whole(middle.shape), whole(vectors.shape)] + [HBM] * 8,
        out_specs=[HBM, HBM, HBM, whole((toks, width)), whole((toks, width))],
        out_shape=[
            jax.ShapeDtypeStruct((4, toks, units), BF16),
            jax.ShapeDtypeStruct((2, units, toks), BF16),
            jax.ShapeDtypeStruct((2, units, toks), BF16),
            jax.ShapeDtypeStruct((toks, width), F32),
            jax.ShapeDtypeStruct((toks, width), BF16),
        ],
        scratch_shapes=[
            pltpu.VMEM((4, toks, units), BF16),
            pltpu.VMEM((4, units, toks), BF16),
            pltpu.VMEM((4, units, parts[0].shape[1]), BF16),
            pltpu.SemaphoreType.DMA((8,)),
            pltpu.SemaphoreType.DMA((8,)),
        ],
        compiler_params=pltpu.CompilerParams(vmem_limit_bytes=56 << 20),
        cost_estimate=pl.CostEstimate(flops=5 * 10**9, transcendentals=2 * 10**6, bytes_accessed=20 << 20),
    )(c, middle, vectors, *parts)


def finish_back(dev, grad_ref, mid_ref, gain_ref, w_ref, dm_ref, dc, dmid_ref, da_ref, sums_ref, targets):
    toks, width = mid_ref.shape
    loc = targets[0].shape[0]

    def rows_of(at, sums):
        rows = pl.ds(pl.multiple_of(at * 128, 128), 128)
        grad_in, gain_sum, bias_sum = norm_back(dc[rows, :], mid_ref[rows, :], gain_ref[...])
        grad_mid = grad_ref[rows, :].astype(F32) + grad_in
        dmid_ref[rows, :] = grad_mid
        branch = grad_mid.astype(BF16)
        da_ref[rows, :] = branch
        out_sum = jnp.sum(branch.astype(F32), axis=0, keepdims=True)
        down_sum = jnp.sum(dm_ref[rows, :].astype(F32), axis=0, keepdims=True)
        return sums[0] + gain_sum, sums[1] + bias_sum, sums[2] + out_sum, sums[3] + down_sum

    zero = jnp.zeros((1, width), F32)
    sums = lax.fori_loop(0, toks // 128, rows_of, (zero,) * 4)
    sums_ref[...] = jnp.zeros_like(sums_ref)
    for at in range(4):
        sums_ref[at : at + 1, :] = sums[at]
    for rel, target in enumerate(targets):
        rows = pl.ds(pl.multiple_of((dev ^ rel) * loc, 64), loc)
        target[...] = dot(w_ref[rows, :], da_ref[...], ((1,), (1,))).astype(BF16)


def back_outputs(toks, width, units):
    return [
        jax.ShapeDtypeStruct((2, toks, units), BF16),
        jax.ShapeDtypeStruct((2, toks, units), BF16),
        jax.ShapeDtypeStruct((toks, width), F32),
        jax.ShapeDtypeStruct((toks, width), BF16),
        jax.ShapeDtypeStruct((8, width), F32),
    ] + [jax.ShapeDtypeStruct((width // 4, toks), BF16)] * 4


def feed_back_kernel(info, grad_ref, dm_ref, slope_in, mid_in, gain_ref, w_in, *refs):
    parts, refs = refs[:8], refs[8:]
    own_out, other_out, dmid_ref, da_ref, sums_ref, *targets = refs[:9]
    slope_ref, dh_ref, held, dc, mid_ref, w_ref, sems, slope_sems, out_sems, in_sems = refs[9:]
    width = mid_ref.shape[1]
    copies = fetch(parts, held, sems)
    slopes = [pltpu.make_async_copy(slope_in.at[at], slope_ref.at[at], slope_sems.at[at]) for at in range(4)]
    late_in = [pltpu.make_async_copy(mid_in, mid_ref, in_sems.at[0]), pltpu.make_async_copy(w_in, w_ref, in_sems.at[1])]
    for copy in slopes + late_in:
        copy.start()
    outs = []
    goals = (own_out.at[0], own_out.at[1], other_out.at[0], other_out.at[1])

    def before(at):
        copies[2 * at].wait()
        copies[2 * at + 1].wait()
        return dot(dm_ref[...], held[at, :, width : 2 * width], ((1,), (1,)))

    def after(at, dact):
        slopes[at].wait()
        dpre = (dact * slope_ref[at].astype(F32)).astype(BF16)
        dh_ref[at] = dpre
        outs.append(pltpu.make_async_copy(dh_ref.at[at], goals[at], out_sems.at[at]))
        outs[-1].start()
        term = dot(dpre, held[at, :, 0:width])
        if at == 0:
            dc[...] = term
        else:
            dc[...] += term

    dact = before(0)
    for at in range(4):
        later = before(at + 1) if at < 3 else None
        after(at, dact)
        dact = later
    for copy in late_in:
        copy.wait()
    finish_back(info[3], grad_ref, mid_ref, gain_ref, w_ref, dm_ref, dc, dmid_ref, da_ref, sums_ref, targets)
    for copy in outs:
        copy.wait()


def feed_backward(info, grad, dm, slope, middle, gain, w_out, parts):
    toks, width = middle.shape
    units = 2 * parts[0].shape[0]
    shapes = back_outputs(toks, width, units)
    return pl.pallas_call(
        feed_back_kernel,
        name="feed_backward",
        grid_spec=pltpu.PrefetchScalarGridSpec(
            num_scalar_prefetch=1,
            grid=(1,),
            in_specs=[whole(grad.shape), whole(dm.shape), HBM, HBM, whole(gain.shape), HBM] + [HBM] * 8,
            out_specs=[HBM] * 2 + [whole(shape.shape) for shape in shapes[2:]],
            scratch_shapes=[
                pltpu.VMEM((4, toks, units), BF16),
                pltpu.VMEM((4, toks, units), BF16),
                pltpu.VMEM((4, units, parts[0].shape[1]), BF16),
                pltpu.VMEM((toks, width), F32),
                pltpu.VMEM((toks, width), F32),
                pltpu.VMEM((width, width), BF16),
                pltpu.SemaphoreType.DMA((8,)),
                pltpu.SemaphoreType.DMA((4,)),
                pltpu.SemaphoreType.DMA((4,)),
                pltpu.SemaphoreType.DMA((2,)),
            ],
        ),
        out_shape=shapes,
        compiler_params=pltpu.CompilerParams(vmem_limit_bytes=60 << 20),
        cost_estimate=pl.CostEstimate(flops=6 * 10**9, transcendentals=2 * 10**6, bytes_accessed=24 << 20),
    )(info, grad, dm, slope, middle, gain, w_out, *parts)


def feed_both_kernel(info, c_ref, dm_ref, mid_ref, vec_ref, w_in, *refs):
    parts, refs = refs[:8], refs[8:]
    own_out, other_out, dmid_ref, da_ref, sums_ref, *targets = refs[:9]
    act_own, act_other, x_ref = refs[9:12]
    act_ref, dh_ref, held, dc, w_ref, sems, out_sems, in_sem = refs[12:]
    toks, width = mid_ref.shape
    copies = fetch(parts, held, sems)
    late_in = pltpu.make_async_copy(w_in, w_ref, in_sem.at[0])
    late_in.start()
    x_ref[...] = mid_ref[...] + vec_ref[0:1, :]
    outs = []
    goals = (own_out.at[0], own_out.at[1], other_out.at[0], other_out.at[1])

    def before(at):
        copies[2 * at].wait()
        copies[2 * at + 1].wait()
        bias = held[at, :, 2 * width : 2 * width + 128].T[0:1].astype(F32)
        pre = dot(c_ref[...], held[at, :, 0:width], ((1,), (1,))) + bias
        return pre, dot(dm_ref[...], held[at, :, width : 2 * width], ((1,), (1,)))

    def after(at, found):
        pre, dact = found
        act, slope = gelu(pre)
        act = act.astype(BF16)
        act_ref[at] = act.T
        dpre = (dact * slope).astype(BF16)
        dh_ref[at] = dpre
        goal = (act_own, act_other)[at // 2].at[at % 2]
        outs.append(pltpu.make_async_copy(dh_ref.at[at], goals[at], out_sems.at[2 * at]))
        outs.append(pltpu.make_async_copy(act_ref.at[at], goal, out_sems.at[2 * at + 1]))
        outs[-2].start()
        outs[-1].start()
        x_ref[...] += dot(act, held[at, :, width : 2 * width])
        term = dot(dpre, held[at, :, 0:width])
        if at == 0:
            dc[...] = term
        else:
            dc[...] += term

    found = before(0)
    for at in range(4):
        later = before(at + 1) if at < 3 else None
        after(at, found)
        found = later
    late_in.wait()
    finish_back(info[3], dm_ref, mid_ref, vec_ref.at[1:2], w_ref, dm_ref, dc, dmid_ref, da_ref, sums_ref, targets)
    for copy in outs:
        copy.wait()


def feed_both(info, c, dm, middle, vectors, w_out, parts):
    toks, width = middle.shape
    units = 2 * parts[0].shape[0]
    shapes = back_outputs(toks, width, units) + [
        jax.ShapeDtypeStruct((2, units, toks), BF16),
        jax.ShapeDtypeStruct((2, units, toks), BF16),
        jax.ShapeDtypeStruct((toks, width), F32),
    ]
    return pl.pallas_call(
        feed_both_kernel,
        name="feed_both",
        grid_spec=pltpu.PrefetchScalarGridSpec(
            num_scalar_prefetch=1,
            grid=(1,),
            in_specs=[whole(v.shape) for v in (c, dm, middle, vectors)] + [HBM] * 9,
            out_specs=[HBM] * 2 + [whole(shape.shape) for shape in shapes[2:9]] + [HBM, HBM, whole((toks, width))],
            scratch_shapes=[
                pltpu.VMEM((4, units, toks), BF16),
                pltpu.VMEM((4, toks, units), BF16),
                pltpu.VMEM((4, units, parts[0].shape[1]), BF16),
                pltpu.VMEM((toks, width), F32),
                pltpu.VMEM((width, width), BF16),
                pltpu.SemaphoreType.DMA((8,)),
                pltpu.SemaphoreType.DMA((8,)),
                pltpu.SemaphoreType.DMA((1,)),
            ],
        ),
        out_shape=shapes,
        compiler_params=pltpu.CompilerParams(vmem_limit_bytes=60 << 20),
        cost_estimate=pl.CostEstimate(flops=10**10, transcendentals=2 * 10**6, bytes_accessed=24 << 20),
    )(info, c, dm, middle, vectors, w_out, *parts)


def feed_weights_kernel(dh, dh2, act, act2, c, c2, dm, dm2, out_ref):
    width = c.shape[1]
    one, two = dh[0].T, dh2[0].T
    out_ref[:, 0:width] = (dot(one, c[...]) + dot(two, c2[...])).astype(BF16)
    out_ref[:, width : 2 * width] = (dot(act[0], dm[...]) + dot(act2[0], dm2[...])).astype(BF16)
    bias = jnp.sum(one.astype(F32), axis=1, keepdims=True) + jnp.sum(two.astype(F32), axis=1, keepdims=True)
    out_ref[:, 2 * width :] = jnp.broadcast_to(bias, (bias.shape[0], 128)).astype(BF16)


def feed_weights(half, dh, dh2, act, act2, c, c2, dm, dm2):
    toks, units, width = dh.shape[1], dh.shape[2], c.shape[1]
    wide = 2 * width + 128
    step = 256
    act_spec = pl.BlockSpec((1, step, toks), lambda i: (half, i, 0))
    return pl.pallas_call(
        feed_weights_kernel,
        name="feed_weights",
        grid=(units // step,),
        in_specs=[
            pl.BlockSpec((1, toks, step), lambda i: (half, 0, i)),
            pl.BlockSpec((1, toks, step), lambda i: (half, 0, i)),
            act_spec,
            act_spec,
        ]
        + [pl.BlockSpec(v.shape, lambda i: (0, 0)) for v in (c, c2, dm, dm2)],
        out_specs=pl.BlockSpec((step, wide), lambda i: (i, 0)),
        out_shape=jax.ShapeDtypeStruct((units, wide), BF16),
        compiler_params=pltpu.CompilerParams(vmem_limit_bytes=48 << 20),
        cost_estimate=pl.CostEstimate(flops=24 * 10**8, transcendentals=0, bytes_accessed=9 << 20),
    )(dh, dh2, act, act2, c, c2, dm, dm2)


def finish_kernel(last, info, *refs):
    attn, hidden, refs = refs[:4], refs[4:8], refs[8:]
    if last:
        (other_vec, other_bias), refs = refs[:2], refs[6:]
        qkv_ref, out_ref, up_ref, down_ref = refs[:4]
        vectors_out, qv_out, bias_out = refs[4:10], refs[10], refs[11]
        qkv_at, out_at, hid_at = refs[12:]
    else:
        qkv_ref, out_ref, up_ref, down_ref, vec_ref, bias_ref, qkv_at, out_at, hid_at = refs
    dev = info[3]
    spot = info[5]
    rows = attn[0].shape[0]
    loc = 192
    for rel in range(4):
        qkv_at[dev ^ rel] = attn[rel][:, 0:576].astype(F32)
        out_at[dev ^ rel, 0] = attn[rel][:, 576:704].astype(F32)
        out_at[dev ^ rel, 1, :, 0:64] = attn[rel][:, 704:768].astype(F32)
        hid_at[spot ^ rel] = hidden[rel][...].astype(F32)
    width = 4 * loc
    quarter = rows // 4
    units = hidden[0].shape[0]
    for at in range(4):
        found = qkv_at[at]
        qkv_ref[0, :, at * loc : (at + 1) * loc] = found[:, 384:576]
        qkv_ref[0, :, width + at * loc : width + (at + 1) * loc] = found[:, 0:192]
        v_at = 2 * width + at * loc
        qkv_ref[0, :, v_at : v_at + 128] = found[:, 256:384]
        qkv_ref[0, :, v_at + 128 : v_at + 192] = found[:, 192:256]
        for piece in range(4):
            goal = slice(at * quarter, (at + 1) * quarter)
            lane = piece * loc
            out_ref[0, goal, lane : lane + 128] = out_at[at, 0, pl.ds(piece, quarter, stride=4), :]
            out_ref[0, goal, lane + 128 : lane + 192] = out_at[at, 1, pl.ds(piece, quarter, stride=4), :][:, 0:64]
        down_ref[0, at * units : (at + 1) * units, :] = hid_at[at, :, width : 2 * width]
    up = jnp.concatenate([hid_at[at, :, 0:width] for at in range(4)], axis=0)
    up_ref[0] = up.T
    bias = jnp.concatenate([hid_at[at, :, 2 * width :] for at in range(4)], axis=0).T[0:8]
    vectors = sum(part[:, 768:896].astype(F32) for part in attn).T[0:16]
    if not last:
        vec_ref[...] = vectors
        bias_ref[...] = bias
        return
    bias_out[0:1, :] = bias[0:1]
    bias_out[1:2, :] = other_bias[0:1, :]
    order = (((12, 0), (10, 0)), ((13, 0), (11, 0)), ((0, 0), (0, 1)), ((1, 0), (1, 1)), ((2, 0), (2, 1)), ((3, 0), (3, 1)))
    for target, picks in zip(vectors_out, order):
        for layer, (row, from_other) in enumerate(picks):
            source = other_vec[row : row + 1, :] if from_other else vectors[row : row + 1]
            target[layer : layer + 1, :] = source
    for half in range(2):
        lanes = slice(half * rows, (half + 1) * rows)
        qv_out[0:1, lanes] = vectors[8 + half : 9 + half]
        qv_out[1:2, lanes] = other_vec[8 + half : 9 + half, :]


def finish(info, layer, attn, hidden, before):
    rows, width = attn[0].shape[0], attn[0].shape[1] - 128
    units = hidden[0].shape[0]
    shapes = [
        (LAYERS, rows, 3 * width),
        (LAYERS, rows, width),
        (LAYERS, width, 4 * units),
        (LAYERS, 4 * units, width),
    ]
    specs = [pl.BlockSpec((1, *shape[1:]), lambda i, info: (layer, 0, 0)) for shape in shapes]
    last = before is not None
    more = [(LAYERS, rows)] * 6 + [(LAYERS, 2 * rows), (LAYERS, 4 * units)] if last else [(16, rows), (8, 4 * units)]
    given = [*before[4:6], *before[:4]] if last else []
    return pl.pallas_call(
        partial(finish_kernel, last),
        name="finish",
        grid_spec=pltpu.PrefetchScalarGridSpec(
            num_scalar_prefetch=1,
            grid=(1,),
            in_specs=[whole(attn[0].shape)] * 4
            + [whole(hidden[0].shape)] * 4
            + ([whole(v.shape) for v in given[:2]] + [HBM] * 4 if last else []),
            out_specs=specs + [whole(shape) for shape in more],
            scratch_shapes=[
                pltpu.VMEM((4, rows, 576), F32),
                pltpu.VMEM((4, 2, rows, 128), F32),
                pltpu.VMEM((4, units, 2 * width + 128), F32),
            ],
        ),
        out_shape=[jax.ShapeDtypeStruct(shape, F32) for shape in shapes + more],
        input_output_aliases={11 + at: at for at in range(4)} if last else {},
        compiler_params=pltpu.CompilerParams(vmem_limit_bytes=56 << 20),
        cost_estimate=pl.CostEstimate(flops=10**6, transcendentals=0, bytes_accessed=8 << 20),
    )(info, *attn, *hidden, *given)


PLANE = ("cx", "core", "tp")


def turned(value, first):
    pairs = []
    for x in range(2):
        for core in range(2):
            for y in range(2):
                flip_x = (core == 0) == first
                target = ((1 - x) if flip_x else x, core, y if flip_x else 1 - y)
                pairs.append((x * 4 + core * 2 + y, target[0] * 4 + target[1] * 2 + target[2]))
    return lax.ppermute(value, PLANE, pairs)


def after(value, *others):
    return lax.optimization_barrier((value, *others))[0]


def diagonal(value):
    return lax.ppermute(value, ("cx", "core"), ((0, 3), (1, 2), (2, 1), (3, 0)))


def around(own):
    far = swap(own, "cx")
    return own, swap(own, "core"), far, swap(far, "core")


def local(
    hidden_in,
    doc_lengths,
    ln1_gain,
    ln1_bias,
    qkv_weight,
    qv_bias,
    out_weight,
    out_bias,
    ln2_gain,
    ln2_bias,
    up_weight,
    up_bias,
    down_weight,
    down_bias,
    output_grad,
):
    shards = lax.axis_size("shard")
    ix, ic, iy = lax.axis_index("cx"), lax.axis_index("core"), lax.axis_index("tp")
    dev = ix * 2 + ic
    seqs, toks, width = hidden_in.shape
    rows = ln1_gain.shape[1]
    units = up_bias.shape[1] // 4
    loc = width // 4
    quarter = rows // 4

    def to_sequence(*arrays):
        given = jnp.stack([lax.dynamic_index_in_dim(array, 1 - iy, 0, keepdims=False) for array in arrays])
        given = swap(given, "tp")
        return [
            jnp.concatenate((lax.dynamic_index_in_dim(array, iy, 0, keepdims=False), other), axis=0)
            for array, other in zip(arrays, given)
        ]

    def own_first(own, other):
        return jnp.where(iy == 0, jnp.stack((own, other)), jnp.stack((other, own)))

    def from_sequence(tokens):
        return own_first(tokens[:toks], swap(tokens[toks:], "tp"))

    lengths = lax.dynamic_index_in_dim(doc_lengths, iy, 0, keepdims=False)
    end0 = lengths[0]
    end1 = end0 + lengths[1]
    end2 = end1 + lengths[2]
    info = jnp.stack((end0, end1, end2, dev, iy, ic * 2 + ix, dev, dev)).astype(jnp.int32)
    row_ids = jnp.arange(2 * toks, dtype=jnp.int32)
    places = dev * (2 * toks) + ((row_ids // toks) ^ iy) * toks + row_ids % toks
    keep = (places < end2).astype(F32)[:, None]

    def columns(array, start):
        return lax.dynamic_slice_in_dim(array, start, loc, 1)

    small = jnp.concatenate(
        [ln1_gain, ln1_bias, out_bias, ln2_gain, ln2_bias, down_bias, qv_bias.reshape(2 * LAYERS, rows)], axis=0
    )
    small = jnp.pad(small, ((0, 128 - small.shape[0]), (0, 0))).T

    def attention_piece(layer):
        weight = qkv_weight[layer]
        q, k, v = (columns(weight, which * width + loc * dev) for which in range(3))
        out = lax.dynamic_slice_in_dim(out_weight[layer], quarter * dev, quarter, 0).reshape(rows, loc)
        pieces = [k[:, :128], k[:, 128:], v[:, 128:], v[:, :128], q, out]
        if layer == 0:
            pieces.append(small)
        return jnp.concatenate(pieces, axis=1)

    def hidden_piece(layer):
        start = ic * 2 * units + ix * units
        up = lax.dynamic_slice_in_dim(up_weight[layer], start, units, 1).T
        down = lax.dynamic_slice_in_dim(down_weight[layer], start, units, 0)
        bias = lax.dynamic_slice_in_dim(up_bias[layer], start, units, 0)
        bias = jnp.broadcast_to(bias[:, None], (units, 128))
        return jnp.concatenate((up, down, bias), axis=1)

    def over_shards(piece):
        return lax.all_gather(piece, "shard", axis=0, tiled=True)

    def send_shards(value, count):
        if shards != 4:
            return ()
        index = lax.axis_index("shard")
        return tuple(
            lax.ppermute(
                lax.dynamic_slice_in_dim(value, (index + by) % shards * count, count, 0),
                "shard",
                [(i, (i + by) % shards) for i in range(shards)],
            )
            for by in range(1, shards)
        )

    def sum_shards(value, count, arriving):
        if shards != 4:
            return lax.psum_scatter(value, "shard", scatter_dimension=0, tiled=True)
        own = lax.dynamic_slice_in_dim(value, lax.axis_index("shard") * count, count, 0).astype(F32)
        return (own + sum(piece.astype(F32) for piece in arriving)).astype(value.dtype)

    def around_hidden(own, *others):
        core, far = swap(own, "core"), swap(own, "cx")
        return own, far, core, swap(after(far, *others), "core")

    hidden_own, raw_grad = to_sequence(hidden_in, output_grad)
    first_piece, attn_piece = hidden_piece(0), attention_piece(0)
    first_parts = around(after(hidden_own, first_piece, attn_piece))
    feed0 = over_shards(first_piece)
    attn0 = over_shards(after(attn_piece, feed0, *first_parts))
    feed_piece, attn_piece = hidden_piece(1), attention_piece(1)
    feed1 = over_shards(after(feed_piece, attn0))
    one0, two0 = turned(feed0, True), turned(feed0, False)

    def out_weights(own):
        full = jnp.zeros((shards, 4, quarter, width), BF16)
        for rel, part in enumerate(around(own)):
            full = lax.dynamic_update_slice(full, part, (0, dev ^ rel, 0, 0))
        return full.reshape(width, width)

    def out_own(gathered):
        return gathered[:, 3 * loc : 4 * loc].reshape(shards, 1, quarter, width)

    weights = []

    smalls = attn0[:, 4 * loc :].T.astype(F32)
    names = [[smalls[which * LAYERS + layer][None] for which in range(6)] for layer in range(LAYERS)]
    qv = smalls[6 * LAYERS : 8 * LAYERS].reshape(LAYERS, 2, shards, rows)
    qv = jnp.transpose(qv, (0, 2, 1, 3)).reshape(LAYERS, 2 * width)

    current = hidden_own.astype(F32)
    attn_parts = first_parts
    saved = []
    for layer in range(LAYERS):
        gain_one, bias_one, bias_out, gain_two, bias_two, bias_down = names[layer]
        w_qkv = attn0 if layer == 0 else attn1
        q_bias = lax.dynamic_slice_in_dim(qv[layer], loc * dev, loc, 0)
        v_bias = lax.dynamic_slice_in_dim(qv[layer], width + loc * dev, loc, 0)
        bias = jnp.concatenate((jnp.zeros((192,), F32), v_bias[128:], v_bias[:128], q_bias))[None]
        if layer == 0:
            one0, two0, attn_piece, *attn_parts = lax.optimization_barrier((one0, two0, attn_piece, *attn_parts))
            three0 = turned(one0, False)
            early_core = [swap(part, "core") for part in (feed0, one0, two0)]
        attn_t, qkv, attended, lse, *normed_all = attention_forward(info, attn_parts, w_qkv, bias, gain_one, bias_one, layer == 0)
        if layer == 0:
            attn1 = over_shards(after(attn_piece, attended))
            w_out = out_weights(out_own(attn0))
            attended, w_out, three0, *early_core = lax.optimization_barrier((attended, w_out, three0, *early_core))
            w_feed = (feed0, one0, two0, three0, *early_core, swap(three0, "core"))
        else:
            own, one, two, three = w_feed1
            early_core = (swap(own, "core"), swap(one, "core"))
            attended, w_out, own, one, two, three, *early_core = lax.optimization_barrier(
                (attended, w_out1, own, one, two, three, *early_core)
            )
        parts = (
            attended[0],
            swap(attended[1], "core"),
            swap(attended[2], "cx"),
            diagonal(attended[3]),
        )
        if layer == 1:
            late_core = [swap(after(part, *parts), "core") for part in (two, three)]
            low_grad = raw_grad * keep.astype(BF16)
            low_other = swap(low_grad, "core")
            w_feed = (own, one, two, three, *early_core, *late_core)
        vectors = jnp.concatenate((bias_out, gain_two, bias_two), axis=0)
        context, middle, mlp_in = out_forward(info, parts, w_out, current, vectors)
        if layer == 0:
            vectors = jnp.concatenate((bias_down, names[1][0], names[1][1]), axis=0)
            mlp_in, feed1 = lax.optimization_barrier((mlp_in, feed1))
            one1 = turned(feed1, True)
            slope, act, act_other, result, attn_own = feed_forward(mlp_in, middle, vectors, w_feed)
            act_other, mlp_other = swap(act_other, "core"), swap(mlp_in, "core")
            attn_own = after(attn_own, one1)
            attn_parts = around(attn_own)
            w_out1 = out_weights(out_own(after(attn1, attn_own)))
            w_out1, act_other, mlp_other, *attn_parts = lax.optimization_barrier(
                (w_out1, act_other, mlp_other, *attn_parts)
            )
            feed1, one1 = lax.optimization_barrier((feed1, one1, *attn_parts))[:2]
            w_feed1 = (feed1, one1, turned(feed1, False), turned(one1, False))
        else:
            slope = act = act_other = result = None
            mlp_other = swap(mlp_in, "core")
        if layer == 0:
            first_normed = normed_all
        weights.append((w_qkv, w_out, w_feed))
        saved.append((current, attn_t, qkv, attended, lse, context, middle, mlp_in, mlp_other, slope, act, act_other))
        current = result
    n = shards * units

    before = ()
    for layer in reversed(range(LAYERS)):
        x_in, attn_t, qkv, attended, lse, context, middle, mlp_in, mlp_other, slope, act, act_other = saved[layer]
        gain_one, _, _, gain_two, _, _ = names[layer]
        w_qkv, w_out, w_feed = weights[layer]
        if layer == 0:
            found = feed_backward(info, grad, low_grad, slope, middle, gain_two, w_out, w_feed)
        else:
            vectors = jnp.concatenate((names[1][5], gain_two), axis=0)
            *found, act, act_other, result = feed_both(info, mlp_in, low_grad, middle, vectors, w_out, w_feed)
            act_other = swap(act_other, "core")
        dh, dh_other, middle_grad, branch_grad, sums_two, d0, d1, d2, d3 = found
        attn_grads = (d0, swap(d1, "core"), swap(d2, "cx"), diagonal(d3))
        tokens = (mlp_in, mlp_other, low_grad, low_other)
        dh_other = swap(dh_other, "core")
        *attn_grads, dh_other = lax.optimization_barrier((*attn_grads, dh_other, *before))[:5]
        late = feed_weights(1, dh, dh_other, act, act_other, *tokens)
        w_out_grad = dot(context, branch_grad).astype(BF16).reshape(shards, 4, quarter, width)
        pieces = [lax.dynamic_index_in_dim(w_out_grad, dev ^ rel, 1, keepdims=False) for rel in range(4)]
        got = swap(jnp.stack((pieces[1], pieces[3])), "core")
        far = swap((pieces[2].astype(F32) + got[1].astype(F32)).astype(BF16), "cx")
        ready = [*attn_grads, late, far]
        if layer == 0:
            attn_sum1 = after(attn_sum1, *attn_grads)
            attn_sum1 = (attn_sum1.astype(F32) + swap(attn_sum1, "tp").astype(F32)).astype(BF16)
            ready.append(attn_sum1)
            early = feed_weights(0, dh, dh_other, act, act_other, *tokens)
            ready.append(early)
        *attn_grads, late, far = lax.optimization_barrier(tuple(ready))[:6]
        du, to_core, to_far, own, sums_u, *norm_sums = attention_backward(
            info, qkv, attended, lse, w_qkv, attn_grads, first_normed if layer == 0 else ()
        )
        late = turned(late, False)
        to_core = after(to_core, late)
        from_core = swap(to_core, "core")
        du_sum = sums_u[0]
        v_sum = jnp.concatenate((du_sum[256:384], du_sum[192:256]))
        q_row = lax.dynamic_update_slice_in_dim(jnp.zeros((width,), F32), du_sum[384:], loc * dev, 0)
        v_row = lax.dynamic_update_slice_in_dim(jnp.zeros((width,), F32), v_sum, loc * dev, 0)
        qv_rows = jnp.concatenate((q_row, v_row)).reshape(shards, 2, rows).transpose(1, 0, 2).reshape(2, width)
        vectors = jnp.concatenate((sums_two, qv_rows, jnp.zeros((6, width), F32)), axis=0)
        if layer == 0:
            vectors = jnp.concatenate((vectors[:10], sums_one[:2], norm_sums[0][:2], vectors[14:]), axis=0)
        flat = [piece.reshape(shards * quarter, width) for piece in (pieces[0], got[0], far)]
        if layer == 0:
            joined = attention_weights(attn_t, du, vectors, *flat)
            attn_sum = lax.psum_scatter(joined, "shard", scatter_dimension=0, tiled=True)
            to_far = after(to_far, joined)
        to_far = (to_far + from_core[1].astype(F32)).astype(BF16)
        if layer == 0:
            attn_sum1, feed_sum1 = lax.optimization_barrier((attn_sum1, feed_sum1, late))[:2]
            attn_parts1, hidden_parts1 = around(attn_sum1), around_hidden(feed_sum1)
            part = (early[n:].astype(F32) + after(late, joined)[n:].astype(F32)).astype(BF16)
            part = after(part, *attn_parts1, *hidden_parts1)
            early_late = late
            arrived = turned(part, True)
            to_far = after(to_far, arrived)
            done = finish(info, 1, attn_parts1, hidden_parts1, None)
        from_far = swap(to_far, "cx")
        if layer == 0:
            from_far = after(from_far, done[5])
        if layer > 0:
            du, dh_now, early_late = lax.optimization_barrier((du, dh, late, to_far))[:3]
            early = feed_weights(0, dh_now, dh_other, act, act_other, *tokens)
            part = (early[n:].astype(F32) + early_late[n:].astype(F32)).astype(BF16)
        if layer > 0:
            hidden_own_out = (after(result, to_far) * keep).astype(BF16)
            hidden_other_out = swap(hidden_own_out[toks:], "tp")
            from_far, part, hidden_other_out = lax.optimization_barrier((from_far, part, hidden_other_out))
            arrived = turned(part, True)
        grad, low_grad, sums_one = norm_backward(own, from_core, from_far, x_in, gain_one, middle_grad)
        if layer > 0:
            low_other = swap(low_grad, "core")
            joined = attention_weights(attn_t, after(du, low_grad), vectors, *flat)
            attn_sum1 = lax.psum_scatter(joined, "shard", scatter_dimension=0, tiled=True)
            grad, low_grad, arrived = lax.optimization_barrier((grad, low_grad, arrived, joined))[:3]
            part = early[:n].astype(F32) + early_late[:n].astype(F32) + arrived.astype(F32)
            part = part.astype(BF16)
            before = (part,)
            feed_sum1 = lax.psum_scatter(part, "shard", scatter_dimension=0, tiled=True)
        else:
            part = (early[:n].astype(F32) + late[:n].astype(F32) + arrived.astype(F32)).astype(BF16)
            arriving = send_shards(part, units)
            attn_sum = after(attn_sum, from_far)
            attn_sum = (attn_sum.astype(F32) + swap(attn_sum, "tp").astype(F32)).astype(BF16)
            attn_parts0 = around(attn_sum)
            arriving = lax.optimization_barrier((*arriving, low_grad))[: len(arriving)]
            feed_sum = sum_shards(part, units, arriving)
            hidden_out = own_first(hidden_own_out[:toks], after(hidden_other_out, part))

    hidden_grad = from_sequence(low_grad).astype(F32)

    done = finish(info, 0, attn_parts0, around_hidden(feed_sum), done)

    return (
        hidden_out,
        hidden_grad,
        done[4],
        done[5],
        done[0],
        done[10],
        done[1],
        done[8],
        done[6],
        done[7],
        done[2],
        done[11],
        done[3],
        done[9],
    )


def solution(mesh):
    names = tuple(mesh.axis_names)
    shape = dict(mesh.shape)
    split = Mesh(
        mesh.devices.reshape(shape[names[0]], 2, shape[names[1]] // 2, shape[names[2]]),
        ("shard", "cx", "core", "tp"),
    )
    tokens = P("shard", ("cx", "core", "tp"), None)
    vector = P(None, "shard")
    attn = P(None, "shard", None)
    placed = (
        tokens,
        P("shard", None),
        vector,
        vector,
        attn,
        vector,
        attn,
        vector,
        vector,
        vector,
        P(None, None, ("shard", "tp")),
        P(None, ("shard", "tp")),
        P(None, ("shard", "tp"), None),
        vector,
        tokens,
    )
    return jax.shard_map(
        local,
        mesh=split,
        in_specs=placed,
        out_specs=(
            tokens,
            tokens,
            vector,
            vector,
            attn,
            vector,
            attn,
            vector,
            vector,
            vector,
            P(None, None, ("shard", "tp")),
            P(None, ("shard", "tp")),
            P(None, ("shard", "tp"), None),
            vector,
        ),
        check_vma=False,
    )
```
